32 devices in a mesh: groups: 2 (over y), pts: 16 (over z, x, core).
Axes of the slice: x: 2, y: 2, z: 4, core: 2. Of those that a mesh axis runs over, the one named last changes fastest.
Arguments:
- latents: bfloat16 [2048, 768], P(('groups', 'pts')), parts along dimension 0, may hold values from -160 to 160
- points: bfloat16 [12288, 768], P(('groups', 'pts')), parts along dimension 0, may hold values from -6 to 6
- counts: int32 [32], P(('groups', 'pts')), parts along dimension 0, may hold values from 48 to 384, as said below
- w_query: bfloat16 [768, 768], replicated, may hold values from -0.21875 to 0.21875
- w_key: bfloat16 [768, 768], replicated, may hold values from -0.21875 to 0.21875
- w_value: bfloat16 [768, 768], replicated, may hold values from -0.21875 to 0.21875
- w_out: bfloat16 [768, 768], replicated, may hold values from -0.21875 to 0.21875
- d_out: bfloat16 [2048, 768], P(('groups', 'pts')), parts along dimension 0, may hold values from -6 to 6
Outputs:
- result: bfloat16 [2048, 768], P(('groups', 'pts')), parts along dimension 0
- d_latents: bfloat16 [2048, 768], P(('groups', 'pts')), parts along dimension 0
- d_points: bfloat16 [12288, 768], P(('groups', 'pts')), parts along dimension 0
The draws below stay inside these ranges and needn't reach their ends.
There are 2 independent parts, one for each index of `groups`. The reference program is written for one: setup_inputs(seed, part) draws one part's arguments, and reference() takes and returns one part's arrays. A program takes and returns all parts, laid end to end along the dimension named above; an argument that names none is the same for every part. Nothing has to cross between parts.
Inputs may be any that keep to these rules, and one draw needn't show every extreme that they name: counts[s] live points fill the first slots of block s; in every part one block is full with 384 and another holds only 48.
All inputs are finite; a program needn't handle non-finite values.
Results may differ from the reference program's by a relative error of at most 0.018.
The reference program's roundings to bfloat16 on the way (of `query`, `attended`, `grad_attended` and `grad_scores`) count: a program that leaves them out, or rounds other values in their place, can miss the bound.
Values may be sent and summed in bfloat16 or wider, within the bound.
No kernel may reach another device: no remote copies, remote signals or barrier semaphores. Data moves between devices by JAX's collectives and lax.ppermute only.
A program may use at most 128 MiB of HBM per device.

```python
import jax
import jax.numpy as jnp
from jax import lax

D = 768
HEADS = 12
NQ = 1024
P_DEV = 384
SHARDS = 16
POINTS = 6144


def draw_latents(key, part):
    first_key = jax.random.fold_in(key, 11)
    normal_key = jax.random.fold_in(first_key, 0)
    base = jnp.clip(jax.random.normal(normal_key, (NQ, D), jnp.float32), -4.0, 4.0)
    return base.astype(jnp.bfloat16)


def draw_counts(key, part):
    first_key = jax.random.fold_in(key, 23)
    count_key, full_key = jax.random.split(first_key)
    drawn = jax.random.randint(count_key, (SHARDS,), P_DEV // 8, P_DEV + 1)
    full_shard = jax.random.randint(full_key, (), 0, SHARDS)
    sparse_shard = (full_shard + 1) % SHARDS
    shard_ids = jnp.arange(SHARDS)
    filled = jnp.where(shard_ids == sparse_shard, P_DEV // 8, drawn)
    return jnp.where(shard_ids == full_shard, P_DEV, filled).astype(jnp.int32)


def level_of(stream_key, dims, pieces, low, largest):
    loudness, own = 1.0, jax.random.fold_in(stream_key, 6)
    for dim, parts in pieces:
        heights = jnp.exp(jax.random.uniform(jax.random.fold_in(own, dim), (parts,), jnp.float32, low / len(pieces), largest / len(pieces)))
        loudness = loudness * jnp.repeat(heights, dims[dim] // parts).reshape([-1 if axis == dim else 1 for axis in range(len(dims))])
    return loudness


def gaussian(stream_key, extent, spread, bound, cuts=(), kind=jnp.bfloat16):
    level = level_of(stream_key, extent, cuts, -0.22, 0.18) if cuts else 1.0
    array = jax.random.normal(stream_key, extent, jnp.float32) * spread * level
    return jnp.minimum(jnp.maximum(array, -bound), bound).astype(kind)


def setup_inputs(seed: int = 0, part: int = 0) -> dict:
    seeds = jax.random.split(jax.random.key(seed), 9)
    part_splits = jax.random.split(jax.random.fold_in(seeds[8], part), 9)
    latents = draw_latents(jax.random.fold_in(jax.random.fold_in(seeds[8], part), 71), part)
    points = gaussian(part_splits[1], (POINTS, D), 1.0, 6.0, ((0, 16),))
    counts = draw_counts(jax.random.fold_in(jax.random.fold_in(seeds[8], part), 71), part)
    w_query = gaussian(seeds[3], (D, D), D ** -0.5, 0.21875)
    w_key = gaussian(seeds[4], (D, D), D ** -0.5, 0.21875)
    w_value = gaussian(seeds[5], (D, D), D ** -0.5, 0.21875)
    w_out = gaussian(seeds[6], (D, D), D ** -0.5, 0.21875)
    d_out = gaussian(part_splits[7], (NQ, D), 1.0, 6.0, ((0, 16),))
    return dict(latents=latents, points=points, counts=counts, w_query=w_query, w_key=w_key, w_value=w_value, w_out=w_out, d_out=d_out)


def masked_scores(query_head, key_head, live_mask):
    raw = jnp.dot(query_head, key_head.T, preferred_element_type=jnp.float32) * 0.125
    return jnp.where(live_mask[None, :], raw, -jnp.inf)


def reference(latents, points, counts, w_query, w_key, w_value, w_out, d_out):
    head_dim = D // HEADS
    query = jnp.dot(latents, w_query, preferred_element_type=jnp.float32).astype(jnp.bfloat16)
    keys = jnp.dot(points, w_key, preferred_element_type=jnp.float32).astype(jnp.bfloat16)
    values = jnp.dot(points, w_value, preferred_element_type=jnp.float32).astype(jnp.bfloat16)
    position = jnp.arange(SHARDS * P_DEV, dtype=jnp.int32)
    live_mask = (position % P_DEV) < counts[position // P_DEV]

    def split_heads(matrix):
        return matrix.reshape(matrix.shape[0], HEADS, head_dim).transpose(1, 0, 2)

    def join_heads(stack):
        return stack.transpose(1, 0, 2).reshape(stack.shape[1], D)

    query_heads = split_heads(query)
    key_heads = split_heads(keys)
    value_heads = split_heads(values)

    def forward_head(operands):
        query_head, key_head, value_head = operands
        scores = masked_scores(query_head, key_head, live_mask)
        row_max = jnp.max(scores, axis=1)
        weights = jnp.exp(scores - row_max[:, None])
        total = jnp.sum(weights, axis=1)
        numerator = jnp.dot(weights.astype(jnp.bfloat16), value_head, preferred_element_type=jnp.float32)
        return row_max, total, numerator

    row_max, total, numerator = lax.map(forward_head, (query_heads, key_heads, value_heads))
    attended_heads = (numerator / total[:, :, None]).astype(jnp.bfloat16)
    attended = join_heads(attended_heads)
    result = (latents.astype(jnp.float32) + jnp.dot(attended, w_out, preferred_element_type=jnp.float32)).astype(jnp.bfloat16)

    grad_attended = jnp.dot(d_out, w_out.T, preferred_element_type=jnp.float32).astype(jnp.bfloat16)
    grad_heads = split_heads(grad_attended)
    delta = jnp.sum(grad_heads.astype(jnp.float32) * attended_heads.astype(jnp.float32), axis=2)
    lse = row_max + jnp.log(total)

    def backward_head(operands):
        query_head, key_head, value_head, grad_head, lse_head, delta_head = operands
        probability = jnp.exp(masked_scores(query_head, key_head, live_mask) - lse_head[:, None])
        grad_value = jnp.dot(probability.astype(jnp.bfloat16).T, grad_head, preferred_element_type=jnp.float32)
        grad_weights = jnp.dot(grad_head, value_head.T, preferred_element_type=jnp.float32)
        grad_scores = (probability * (grad_weights - delta_head[:, None])).astype(jnp.bfloat16)
        grad_query = jnp.dot(grad_scores, key_head, preferred_element_type=jnp.float32) * 0.125
        grad_key = jnp.dot(grad_scores.T, query_head, preferred_element_type=jnp.float32) * 0.125
        return grad_query, grad_key, grad_value

    grad_query, grad_key, grad_value = lax.map(backward_head, (query_heads, key_heads, value_heads, grad_heads, lse, delta))
    grad_query = join_heads(grad_query)
    d_latents = (d_out.astype(jnp.float32) + jnp.dot(grad_query.astype(jnp.bfloat16), w_query.T, preferred_element_type=jnp.float32)).astype(jnp.bfloat16)
    d_points = (jnp.dot(join_heads(grad_key).astype(jnp.bfloat16), w_key.T, preferred_element_type=jnp.float32)
                + jnp.dot(join_heads(grad_value).astype(jnp.bfloat16), w_value.T, preferred_element_type=jnp.float32)).astype(jnp.bfloat16)
    return result, d_latents, d_points
```

```python
import functools

import jax
import jax.numpy as jnp
from jax import lax
from jax.experimental import pallas as pl
from jax.experimental.pallas import tpu as pltpu
from jax.sharding import PartitionSpec as P

HEADS = 12
BF16 = jnp.bfloat16
F32 = jnp.float32
NT = (((1,), (1,)), ((), ()))


def dot(a, b):
    return jnp.dot(a, b, preferred_element_type=F32)


def dot_nt(a, b):
    return lax.dot_general(a, b, NT, preferred_element_type=F32)


def low_lanes(shape):
    return lax.broadcasted_iota(jnp.int32, shape, 1) < shape[1] // 2


def keep_half(pair, half):
    low = low_lanes(pair.shape)
    return jnp.where(low if half == 0 else ~low, pair, jnp.zeros_like(pair))


def head_scores(key_pair, half, query_pair, dead):
    raw = dot_nt(keep_half(key_pair, half), query_pair)
    return jnp.where(dead, -jnp.inf, raw)


def forward_kernel(count_ref, q_ref, g_ref, key_ref, value_t_ref, numer_ref, max_ref, stat_ref):
    rows, width = q_ref.shape
    slots = key_ref.shape[0]
    head_dim = width // HEADS
    span = 2 * head_dim
    dead = lax.broadcasted_iota(jnp.int32, (slots, rows), 0) >= count_ref[0]
    for pair in range(HEADS // 2):
        cols = slice(pair * span, (pair + 1) * span)
        query_pair = q_ref[:, cols]
        key_pair = key_ref[:, cols]
        grad_t = g_ref[:, cols].astype(F32).T
        for half in range(2):
            head = 2 * pair + half
            at = slice(head * head_dim, (head + 1) * head_dim)
            scores = head_scores(key_pair, half, query_pair, dead)
            top = jnp.max(scores, axis=0, keepdims=True)
            weights = jnp.exp(scores - top)
            total = jnp.sum(weights, axis=0, keepdims=True)
            numer = dot(value_t_ref[at, :], weights.astype(BF16))
            numer_ref[at, :] = numer
            mine = grad_t[half * head_dim : (half + 1) * head_dim, :]
            inner = jnp.sum(mine * numer, axis=0, keepdims=True)
            max_ref[head : head + 1, :] = top
            stat_ref[head : head + 1, :] = top + jnp.log(total)
            stat_ref[HEADS + head : HEADS + head + 1, :] = inner / total


def scale_kernel(numer_ref, max_ref, stat_ref, out_ref):
    width, rows = numer_ref.shape
    head_dim = width // HEADS
    for pair in range(HEADS // 2):
        parts = []
        for half in range(2):
            head = 2 * pair + half
            scale = jnp.exp(max_ref[head : head + 1, :] - stat_ref[head : head + 1, :])
            parts.append(numer_ref[head * head_dim : (head + 1) * head_dim, :] * scale)
        out_ref[:, 2 * pair * head_dim : 2 * (pair + 1) * head_dim] = (
            jnp.concatenate(parts, axis=0).T.astype(out_ref.dtype)
        )


def backward_kernel(
    first,
    last,
    count_ref,
    q_ref,
    g_ref,
    stat_ref,
    key_ref,
    key_t_ref,
    value_ref,
    *refs,
):
    if first:
        gq_ref, gk_ref, gv_ref = refs
    else:
        gk_in_ref, gv_in_ref, gq_ref, gk_ref, gv_ref = refs
    rows, width = q_ref.shape
    slots = key_ref.shape[0]
    head_dim = width // HEADS
    span = 2 * head_dim
    dead = lax.broadcasted_iota(jnp.int32, (slots, rows), 0) >= count_ref[0]
    low = low_lanes((slots, span))
    for pair in range(HEADS // 2):
        cols = slice(pair * span, (pair + 1) * span)
        query_pair = q_ref[:, cols]
        grad_pair = g_ref[:, cols]
        key_pair = key_ref[:, cols]
        value_pair = value_ref[:, cols]
        gk, gv, gq = [], [], []
        for half in range(2):
            head = 2 * pair + half
            scores = head_scores(key_pair, half, query_pair, dead)
            prob = jnp.exp(scores - stat_ref[head : head + 1, :])
            gv.append(dot(prob.astype(BF16), grad_pair))
            gw = dot_nt(keep_half(value_pair, half), grad_pair)
            ds = (prob * (gw - stat_ref[HEADS + head : HEADS + head + 1, :])).astype(BF16)
            gk.append(dot(ds, query_pair))
            gq.append(dot(key_t_ref[head * head_dim : (head + 1) * head_dim, :], ds))
        gq_ref[:, cols] = jnp.concatenate(gq, axis=0).T.astype(gq_ref.dtype)
        gk_sum = jnp.where(low, gk[0], gk[1])
        gv_sum = jnp.where(low, gv[0], gv[1])
        if not first:
            gk_sum += gk_in_ref[:, cols]
            gv_sum += gv_in_ref[:, cols]
        if last:
            gk_sum *= 0.125
        gk_ref[:, cols] = gk_sum.astype(gk_ref.dtype)
        gv_ref[:, cols] = gv_sum.astype(gv_ref.dtype)


def call(kernel, ins, out_shapes, flops=0, exps=0):
    vmem = pl.BlockSpec(memory_space=pltpu.VMEM)
    smem = pl.BlockSpec(memory_space=pltpu.SMEM)
    specs = [smem if a.dtype == jnp.int32 else vmem for a in ins]
    moved = sum(a.size * a.dtype.itemsize for a in list(ins) + list(out_shapes))
    return pl.pallas_call(
        kernel,
        in_specs=specs,
        out_specs=[vmem] * len(out_shapes),
        out_shape=out_shapes,
        compiler_params=pltpu.CompilerParams(vmem_limit_bytes=40 << 20),
        cost_estimate=pl.CostEstimate(flops=flops, transcendentals=exps, bytes_accessed=moved),
    )(*ins)


def body(size, latents, points, counts, w_query, w_key, w_value, w_out, d_out):
    own, width = latents.shape
    slots = points.shape[0]
    shape = jax.ShapeDtypeStruct
    direct = [0, size // 4, size // 2, size // 4 + size // 2]
    middle = []
    bit = size // 8
    while bit >= 4:
        middle.append(bit)
        bit //= 2

    def swap(array, mask):
        return lax.ppermute(array, "pts", [(i, i ^ mask) for i in range(size)])

    query_own = dot(latents, w_query).astype(BF16)
    grad_own = dot(d_out, w_out.T).astype(BF16)

    def gather(block):
        near = jnp.concatenate([block] + [swap(block, m) for m in direct[1:]], axis=0)
        for mask in middle:
            near = jnp.concatenate([near, swap(near, mask)], axis=0)
        across = swap(near, 2)
        return [near, across, swap(near, 1), swap(across, 1)]

    query = gather(query_own)
    grad = gather(grad_own)
    keys = dot(points, w_key).astype(BF16) * jnp.asarray(0.125, BF16)
    values = dot(points, w_value).astype(BF16)
    keys_t = keys.T
    values_t = values.T
    rows = query[0].shape[0]
    work = 2 * rows * slots * width

    def forward(i):
        return call(
            forward_kernel,
            [counts, query[i], grad[i], keys, values_t],
            [shape((width, rows), F32), shape((HEADS, rows), F32), shape((2 * HEADS, rows), F32)],
            flops=8 * work,
            exps=rows * slots * HEADS,
        )

    numer, tops, stats = [None] * 4, [None] * 4, [None] * 4
    for i in (0, 2, 1, 3):
        numer[i], tops[i], stats[i] = forward(i)

    def merge(*parts):
        lse = [p[:HEADS] for p in parts]
        top = functools.reduce(jnp.maximum, lse)
        scale = [jnp.exp(x - top) for x in lse]
        total = sum(scale)
        delta = sum(s * p[HEADS:] for s, p in zip(scale, parts)) / total
        return jnp.concatenate([top + jnp.log(total), delta], axis=0)

    came = swap(jnp.stack([stats[2], stats[3]]), 1)
    mine = merge(stats[0], came[0])
    other = merge(stats[1], came[1])
    mine = merge(mine, swap(other, 2))
    for mask in reversed(middle):
        half = mine.shape[1] // 2
        mine = merge(mine[:, :half], swap(mine[:, half:], mask))
    quarter = mine.shape[1] // 4

    def turned(array, p):
        blocks = [array[:, t * quarter : (t + 1) * quarter] for t in range(4)]
        return jnp.concatenate([blocks[t ^ p] for t in range(4)], axis=1)

    mine = merge(mine, *[turned(swap(mine, direct[p]), p) for p in range(1, 4)])
    for mask in middle:
        mine = jnp.concatenate([mine, swap(mine, mask)], axis=1)
    both = jnp.stack([mine, swap(mine, 2)])
    far = swap(both, 1)
    final = [both[0], both[1], far[0], far[1]]

    def scaled(i, dtype):
        return call(scale_kernel, [numer[i], tops[i], final[i]], [shape((rows, width), dtype)])[0]

    def total_of(near, across):
        summed = near + swap(across.astype(BF16), 2).astype(F32)
        for mask in reversed(middle):
            half = summed.shape[0] // 2
            summed = summed[:half] + swap(summed[half:].astype(BF16), mask).astype(F32)
        out = summed[:own]
        for p in range(1, 4):
            sent = summed[p * own : (p + 1) * own].astype(BF16)
            out = out + swap(sent, direct[p]).astype(F32)
        return out

    def add(array, came):
        return array + came.astype(F32)

    sent = swap(jnp.concatenate([scaled(2, BF16), scaled(3, BF16)], axis=0), 1)
    attended = total_of(
        add(scaled(0, F32), sent[:rows]), add(scaled(1, F32), sent[rows:])
    ).astype(BF16)
    result = (latents.astype(F32) + dot(attended, w_out)).astype(BF16)

    def backward(i, sums, dtype, last=False):
        kind = BF16 if last else F32
        outs = [shape((rows, width), dtype), shape((slots, width), kind), shape((slots, width), kind)]
        gq, gk, gv = call(
            functools.partial(backward_kernel, not sums, last),
            [counts, query[i], grad[i], final[i], keys, keys_t, values] + sums,
            outs,
            flops=14 * work,
            exps=rows * slots * HEADS,
        )
        return gq, [gk, gv]

    gq_2, sums = backward(2, [], BF16)
    sent_2 = swap(gq_2, 1)
    gq_3, sums = backward(3, sums, BF16)
    sent_3 = swap(gq_3, 1)
    gq_1, sums = backward(1, sums, F32)
    across = add(gq_1, sent_3)
    gq_0, sums = backward(0, sums, F32, last=True)
    grad_query = total_of(add(gq_0, sent_2), across)
    d_latents = (d_out.astype(F32) + dot(grad_query.astype(BF16), w_query.T)).astype(BF16)
    d_points = (dot(sums[0], w_key.T) + dot(sums[1], w_value.T)).astype(BF16)
    return (result, d_latents, d_points)


def solution(mesh):
    part = P(("groups", "pts"), None)
    in_specs = (part, part, P(("groups", "pts")), P(), P(), P(), P(), part)
    return jax.shard_map(
        functools.partial(body, mesh.shape["pts"]),
        mesh=mesh,
        in_specs=in_specs,
        out_specs=(part, part, part),
        check_vma=False,
    )
```

```python
import functools

import jax
import jax.numpy as jnp
from jax import lax
from jax.experimental import pallas as pl
from jax.experimental.pallas import tpu as pltpu
from jax.sharding import PartitionSpec as P

HEADS = 12
BF16 = jnp.bfloat16
F32 = jnp.float32
NT = (((1,), (1,)), ((), ()))


def dot(a, b):
    return jnp.dot(a, b, preferred_element_type=F32)


def dot_nt(a, b):
    return lax.dot_general(a, b, NT, preferred_element_type=F32)


def low_lanes(shape):
    return lax.broadcasted_iota(jnp.int32, shape, 1) < shape[1] // 2


def keep_half(pair, half):
    low = low_lanes(pair.shape)
    return jnp.where(low if half == 0 else ~low, pair, jnp.zeros_like(pair))


def head_scores(key_pair, half, query_pair, dead):
    raw = dot_nt(keep_half(key_pair, half), query_pair)
    return jnp.where(dead, -jnp.inf, raw)


def forward_kernel(
    count_ref, q_ref, g_ref, key_ref, value_t_ref, numer_ref, max_ref, stat_ref, score_ref, weight_ref
):
    rows, width = q_ref.shape
    slots = key_ref.shape[0]
    head_dim = width // HEADS
    span = 2 * head_dim
    depth = score_ref.shape[0]
    dead = lax.broadcasted_iota(jnp.int32, (slots, rows), 0) >= count_ref[0]
    tops, totals = [None] * HEADS, [None] * HEADS

    def score(head):
        pair, half = divmod(head, 2)
        cols = slice(pair * span, (pair + 1) * span)
        score_ref[head % depth] = dot_nt(keep_half(key_ref[:, cols], half), q_ref[:, cols])

    def weigh(head):
        scores = jnp.where(dead, -jnp.inf, score_ref[head % depth])
        tops[head] = jnp.max(scores, axis=0, keepdims=True)
        weights = jnp.exp(scores - tops[head])
        totals[head] = jnp.sum(weights, axis=0, keepdims=True)
        weight_ref[head % depth] = weights.astype(BF16)

    def attend(head):
        pair, half = divmod(head, 2)
        at = slice(head * head_dim, (head + 1) * head_dim)
        numer = dot(value_t_ref[at, :], weight_ref[head % depth])
        numer_ref[at, :] = numer
        grad_t = g_ref[:, pair * span : (pair + 1) * span].astype(F32).T
        mine = grad_t[half * head_dim : (half + 1) * head_dim, :]
        inner = jnp.sum(mine * numer, axis=0, keepdims=True)
        max_ref[head : head + 1, :] = tops[head]
        stat_ref[head : head + 1, :] = tops[head] + jnp.log(totals[head])
        stat_ref[HEADS + head : HEADS + head + 1, :] = inner / totals[head]

    for step in range(HEADS + 2):
        if step < HEADS:
            score(step)
        if 0 <= step - 1 < HEADS:
            weigh(step - 1)
        if 0 <= step - 2:
            attend(step - 2)


def scale_kernel(numer_ref, max_ref, stat_ref, out_ref):
    width, rows = numer_ref.shape
    head_dim = width // HEADS
    for pair in range(HEADS // 2):
        parts = []
        for half in range(2):
            head = 2 * pair + half
            scale = jnp.exp(max_ref[head : head + 1, :] - stat_ref[head : head + 1, :])
            parts.append(numer_ref[head * head_dim : (head + 1) * head_dim, :] * scale)
        out_ref[:, 2 * pair * head_dim : 2 * (pair + 1) * head_dim] = (
            jnp.concatenate(parts, axis=0).T.astype(out_ref.dtype)
        )


def backward_kernel(first, last, count_ref, q_ref, g_ref, stat_ref, key_ref, key_t_ref, value_ref, *refs):
    if not first:
        gk_in_ref, gv_in_ref, *refs = refs
    gq_ref, gk_ref, gv_ref, score_ref, gw_ref, prob_ref, ds_ref = refs
    rows, width = q_ref.shape
    slots = key_ref.shape[0]
    head_dim = width // HEADS
    span = 2 * head_dim
    depth = score_ref.shape[0]
    dead = lax.broadcasted_iota(jnp.int32, (slots, rows), 0) >= count_ref[0]
    low = low_lanes((slots, span))
    gq, gk, gv = [None] * HEADS, [None] * HEADS, [None] * HEADS

    def score(head):
        pair, half = divmod(head, 2)
        cols = slice(pair * span, (pair + 1) * span)
        score_ref[head % depth] = dot_nt(keep_half(key_ref[:, cols], half), q_ref[:, cols])
        gw_ref[head % depth] = dot_nt(keep_half(value_ref[:, cols], half), g_ref[:, cols])

    def weigh(head):
        scores = jnp.where(dead, -jnp.inf, score_ref[head % depth])
        prob = jnp.exp(scores - stat_ref[head : head + 1, :])
        delta = stat_ref[HEADS + head : HEADS + head + 1, :]
        prob_ref[head % depth] = prob.astype(BF16)
        ds_ref[head % depth] = (prob * (gw_ref[head % depth] - delta)).astype(BF16)

    def collect(head):
        pair, half = divmod(head, 2)
        cols = slice(pair * span, (pair + 1) * span)
        gv[head] = dot(prob_ref[head % depth], g_ref[:, cols])
        gk[head] = dot(ds_ref[head % depth], q_ref[:, cols])
        gq[head] = dot(key_t_ref[head * head_dim : (head + 1) * head_dim, :], ds_ref[head % depth])
        if half == 0:
            return
        gq_ref[:, cols] = jnp.concatenate(gq[head - 1 : head + 1], axis=0).T.astype(gq_ref.dtype)
        gk_sum = jnp.where(low, gk[head - 1], gk[head])
        gv_sum = jnp.where(low, gv[head - 1], gv[head])
        if not first:
            gk_sum += gk_in_ref[:, cols]
            gv_sum += gv_in_ref[:, cols]
        if last:
            gk_sum *= 0.125
        gk_ref[:, cols] = gk_sum.astype(gk_ref.dtype)
        gv_ref[:, cols] = gv_sum.astype(gv_ref.dtype)

    for step in range(HEADS + 2):
        if 0 <= step - 2:
            collect(step - 2)
        if 0 <= step - 1 < HEADS:
            weigh(step - 1)
        if step < HEADS:
            score(step)


def after(array, *others):
    return lax.optimization_barrier((array, *others))[0]


def call(kernel, ins, out_shapes, scratch=(), flops=0, exps=0):
    vmem = pl.BlockSpec(memory_space=pltpu.VMEM)
    smem = pl.BlockSpec(memory_space=pltpu.SMEM)
    specs = [smem if a.dtype == jnp.int32 else vmem for a in ins]
    moved = sum(a.size * a.dtype.itemsize for a in list(ins) + list(out_shapes))
    return pl.pallas_call(
        kernel,
        in_specs=specs,
        out_specs=[vmem] * len(out_shapes),
        out_shape=out_shapes,
        scratch_shapes=scratch,
        compiler_params=pltpu.CompilerParams(vmem_limit_bytes=40 << 20),
        cost_estimate=pl.CostEstimate(flops=flops, transcendentals=exps, bytes_accessed=moved),
    )(*ins)


def body(size, latents, points, counts, w_query, w_key, w_value, w_out, d_out):
    own, width = latents.shape
    slots = points.shape[0]
    shape = jax.ShapeDtypeStruct
    direct = [0, size // 4, size // 2, size // 4 + size // 2]
    middle = []
    bit = size // 8
    while bit >= 4:
        middle.append(bit)
        bit //= 2

    def swap(array, mask):
        return lax.ppermute(array, "pts", [(i, i ^ mask) for i in range(size)])

    query_own = dot(latents, w_query).astype(BF16)
    grad_own = dot(d_out, w_out.T).astype(BF16)

    def near_of(block, came):
        near = jnp.concatenate([block] + came, axis=0)
        for mask in middle:
            near = jnp.concatenate([near, swap(near, mask)], axis=0)
        return near

    came_q = [swap(query_own, m) for m in direct[1:]]
    grad_own = after(grad_own, came_q[0])
    came_g = [swap(grad_own, m) for m in direct[1:]]
    keys = dot(points, w_key).astype(BF16) * jnp.asarray(0.125, BF16)
    values = dot(points, w_value).astype(BF16)
    keys_t = keys.T
    values_t = values.T
    came_q[2] = after(came_q[2], keys, values_t)
    near_q = near_of(query_own, came_q)
    near_g = near_of(grad_own, came_g)
    query = [near_q, swap(near_q, 2), swap(near_q, 1)]
    grad = [near_g, swap(near_g, 2), swap(near_g, 1)]
    rows = query[0].shape[0]
    work = 2 * rows * slots * width

    def forward(i):
        return call(
            forward_kernel,
            [counts, query[i], grad[i], keys, values_t],
            [shape((width, rows), F32), shape((HEADS, rows), F32), shape((2 * HEADS, rows), F32)],
            [pltpu.VMEM((3, slots, rows), F32), pltpu.VMEM((3, slots, rows), BF16)],
            flops=8 * work,
            exps=rows * slots * HEADS,
        )

    numer, tops, stats = [None] * 4, [None] * 4, [None] * 4
    for i in (0, 2):
        numer[i], tops[i], stats[i] = forward(i)
    query[1] = after(query[1], stats[0])
    grad[1] = after(grad[1], stats[2])
    query.append(swap(query[1], 1))
    grad.append(swap(grad[1], 1))
    for i in (1, 3):
        numer[i], tops[i], stats[i] = forward(i)

    def merge(*parts):
        lse = [p[:HEADS] for p in parts]
        top = functools.reduce(jnp.maximum, lse)
        scale = [jnp.exp(x - top) for x in lse]
        total = sum(scale)
        delta = sum(s * p[HEADS:] for s, p in zip(scale, parts)) / total
        return jnp.concatenate([top + jnp.log(total), delta], axis=0)

    came = swap(jnp.stack([stats[2], stats[3]]), 1)
    mine = merge(stats[0], came[0])
    other = merge(stats[1], came[1])
    mine = merge(mine, swap(other, 2))
    for mask in reversed(middle):
        half = mine.shape[1] // 2
        mine = merge(mine[:, :half], swap(mine[:, half:], mask))
    quarter = mine.shape[1] // 4

    def turned(array, p):
        blocks = [array[:, t * quarter : (t + 1) * quarter] for t in range(4)]
        return jnp.concatenate([blocks[t ^ p] for t in range(4)], axis=1)

    mine = merge(mine, *[turned(swap(mine, direct[p]), p) for p in range(1, 4)])
    for mask in middle:
        mine = jnp.concatenate([mine, swap(mine, mask)], axis=1)
    both = jnp.stack([mine, swap(mine, 2)])
    far = swap(both, 1)
    final = [both[0], both[1], far[0], far[1]]

    def scaled(i, dtype):
        return call(scale_kernel, [numer[i], tops[i], final[i]], [shape((rows, width), dtype)])[0]

    def add(array, came):
        return array + came.astype(F32)

    def inner_sums(near, across):
        summed = add(near, across)
        for mask in reversed(middle):
            half = summed.shape[0] // 2
            summed = add(summed[:half], swap(summed[half:].astype(BF16), mask))
        out = [summed[p * own : (p + 1) * own] for p in range(4)]
        return [out[0]] + [x.astype(BF16) for x in out[1:]]

    def outer_sum(blocks):
        out = blocks[0]
        for p in range(1, 4):
            out = add(out, swap(blocks[p], direct[p]))
        return out

    def backward(i, sums, dtype, behind=(), last=False):
        kind = BF16 if last else F32
        outs = [shape((rows, width), dtype), shape((slots, width), kind), shape((slots, width), kind)]
        stat = after(final[i], *behind)
        gq, gk, gv = call(
            functools.partial(backward_kernel, not sums, last),
            [counts, query[i], grad[i], stat, keys, keys_t, values] + sums,
            outs,
            [pltpu.VMEM((2, slots, rows), F32)] * 2 + [pltpu.VMEM((2, slots, rows), BF16)] * 2,
            flops=14 * work,
            exps=rows * slots * HEADS,
        )
        return gq, [gk, gv]

    near_0, near_1 = scaled(0, F32), scaled(1, F32)
    sent_a = swap(jnp.concatenate([scaled(2, BF16), scaled(3, BF16)], axis=0), 1)
    gq_3, sums = backward(3, [], BF16, [near_0, near_1])
    sent_3 = swap(gq_3, 1)
    across_a = add(near_1, sent_a[rows:]).astype(BF16)
    came_a = swap(across_a, 2)
    gq_1, sums = backward(1, sums, F32, [across_a])
    across = add(gq_1, sent_3).astype(BF16)
    came = swap(across, 2)
    blocks_a = inner_sums(add(near_0, sent_a[:rows]), came_a)
    gq_2, sums = backward(2, sums, BF16, [across, blocks_a[3]])
    sent_2 = swap(gq_2, 1)
    gq_0, sums = backward(0, sums, F32, last=True)
    attended = outer_sum(blocks_a).astype(BF16)
    result = (latents.astype(F32) + dot(attended, w_out)).astype(BF16)
    grad_query = outer_sum(inner_sums(add(gq_0, sent_2), came))
    d_latents = (d_out.astype(F32) + dot(grad_query.astype(BF16), w_query.T)).astype(BF16)
    d_points = (dot(sums[0], w_key.T) + dot(sums[1], w_value.T)).astype(BF16)
    return (result, d_latents, d_points)


def solution(mesh):
    part = P(("groups", "pts"), None)
    in_specs = (part, part, P(("groups", "pts")), P(), P(), P(), P(), part)
    return jax.shard_map(
        functools.partial(body, mesh.shape["pts"]),
        mesh=mesh,
        in_specs=in_specs,
        out_specs=(part, part, part),
        check_vma=False,
    )
```

```python
import functools

import jax
import jax.numpy as jnp
from jax import lax
from jax.experimental import pallas as pl
from jax.experimental.pallas import tpu as pltpu
from jax.sharding import PartitionSpec as P

HEADS = 12
TEAM = 4
MINE = HEADS // TEAM
BF16 = jnp.bfloat16
F32 = jnp.float32
LANES = 128
NT = (((1,), (1,)), ((), ()))


def dot(a, b):
    return jnp.dot(a, b, preferred_element_type=F32)


def dot_nt(a, b):
    return lax.dot_general(a, b, NT, preferred_element_type=F32)


def after(array, *others):
    return lax.optimization_barrier((array, *others))[0]


def low_lanes(shape):
    return lax.broadcasted_iota(jnp.int32, shape, 1) < shape[1] // 2


def lanes_of(part):
    start = part // 2 * LANES
    return slice(start, start + LANES)


def keep_part(array, part):
    low = low_lanes(array.shape)
    return jnp.where(low if part % 2 == 0 else ~low, array, jnp.zeros_like(array))


def block_of(refs, block, slots):
    start = block % 2 * slots
    return refs[block // 2].at[start : start + slots]


def columns_of(refs, block, slots):
    start = block % 2 * slots
    return refs[block // 2].at[:, start : start + slots]


def forward_kernel(
    count_ref, qg_ref, kv_0, kv_1, kv_t_0, kv_t_1, numer_ref, max_ref, stat_ref, score_ref, weight_ref
):
    kv_refs, kv_t_refs = (kv_0, kv_1), (kv_t_0, kv_t_1)
    rows = qg_ref.shape[0]
    dim = kv_t_0.shape[0] // (2 * MINE)
    slots = kv_0.shape[0] // 2
    depth = score_ref.shape[0]
    slot = lax.broadcasted_iota(jnp.int32, (slots, rows), 0)
    units = [(head, block) for head in range(MINE) for block in range(TEAM)]
    tops, totals, numers = {}, {}, {}

    def score(step):
        head, block = units[step]
        keys = keep_part(block_of(kv_refs, block, slots)[:, lanes_of(head)], head)
        score_ref[step % depth] = dot_nt(keys, qg_ref[:, lanes_of(head)])

    def weigh(step):
        scores = jnp.where(slot >= count_ref[units[step][1]], -jnp.inf, score_ref[step % depth])
        tops[step] = jnp.max(scores, axis=0, keepdims=True)
        weights = jnp.exp(scores - tops[step])
        totals[step] = jnp.sum(weights, axis=0, keepdims=True)
        weight_ref[step % depth] = weights.astype(BF16)

    def attend(step):
        head, block = units[step]
        part = MINE + head
        at = slice(part * dim, (part + 1) * dim)
        numers[step] = dot(columns_of(kv_t_refs, block, slots)[at, :], weight_ref[step % depth])
        if block < TEAM - 1:
            return
        steps = range(step - TEAM + 1, step + 1)
        top = functools.reduce(jnp.maximum, [tops[s] for s in steps])
        scale = {s: jnp.exp(tops[s] - top) for s in steps}
        total = sum(scale[s] * totals[s] for s in steps)
        numer = sum(scale[s] * numers[s] for s in steps)
        numer_ref[head * dim : (head + 1) * dim, :] = numer
        half = part % 2 * dim
        grad_t = qg_ref[:, lanes_of(part)].astype(F32).T[half : half + dim, :]
        inner = jnp.sum(grad_t * numer, axis=0, keepdims=True)
        max_ref[head : head + 1, :] = top
        stat_ref[head : head + 1, :] = top + jnp.log(total)
        stat_ref[MINE + head : MINE + head + 1, :] = inner / total

    for step in range(len(units) + 2):
        if step < len(units):
            score(step)
        if 0 <= step - 1 < len(units):
            weigh(step - 1)
        if 0 <= step - 2:
            attend(step - 2)


def backward_kernel(first, last, count_ref, qg_ref, stat_ref, kv_0, kv_1, kv_t_0, kv_t_1, *refs):
    kv_refs, kv_t_refs = (kv_0, kv_1), (kv_t_0, kv_t_1)
    if not first:
        sum_in_refs, refs = refs[:2], refs[2:]
    gq_ref, *sum_refs, score_ref, gw_ref, prob_ref, ds_ref = refs
    rows = qg_ref.shape[0]
    dim = kv_t_0.shape[0] // (2 * MINE)
    slots = kv_0.shape[0] // 2
    depth = score_ref.shape[0]
    slot = lax.broadcasted_iota(jnp.int32, (slots, rows), 0)
    low = low_lanes((slots, LANES))
    units = [(head, block) for block in range(TEAM) for head in range(MINE)]
    gq, held = {}, {}

    def product(block, part):
        rows_of = block_of(kv_refs, block, slots)
        return dot_nt(keep_part(rows_of[:, lanes_of(part)], part), qg_ref[:, lanes_of(part)])

    def score(step):
        head, block = units[step]
        score_ref[step % depth] = product(block, head)
        gw_ref[step % depth] = product(block, MINE + head)

    def weigh(step):
        head, block = units[step]
        scores = jnp.where(slot >= count_ref[block], -jnp.inf, score_ref[step % depth])
        prob = jnp.exp(scores - stat_ref[head : head + 1, :])
        delta = stat_ref[MINE + head : MINE + head + 1, :]
        prob_ref[step % depth] = prob.astype(BF16)
        ds_ref[step % depth] = (prob * (gw_ref[step % depth] - delta)).astype(BF16)

    def store(block, part, value):
        held[block, part] = value
        first_part = part // 2 * 2
        if (block, first_part) not in held or (block, first_part + 1) not in held:
            return
        pair = [held.pop((block, p)) for p in (first_part, first_part + 1)]
        if last:
            pair = [x * 0.125 if p < MINE else x for p, x in zip((first_part, first_part + 1), pair)]
        total = jnp.where(low, pair[0], pair[1])
        if not first:
            before = block_of(sum_in_refs, block, slots)[:, lanes_of(part)]
            if last:
                scales = [0.125 if p < MINE else 1.0 for p in (first_part, first_part + 1)]
                before = before * (scales[0] if scales[0] == scales[1] else jnp.where(low, *scales))
            total += before
        block_of(sum_refs, block, slots)[:, lanes_of(part)] = total.astype(sum_refs[0].dtype)

    def collect(step):
        head, block = units[step]
        store(block, head, dot(ds_ref[step % depth], qg_ref[:, lanes_of(head)]))
        store(block, MINE + head, dot(prob_ref[step % depth], qg_ref[:, lanes_of(MINE + head)]))
        keys_t = columns_of(kv_t_refs, block, slots)[head * dim : (head + 1) * dim, :]
        term = dot(keys_t, ds_ref[step % depth])
        gq[head] = gq[head] + term if head in gq else term
        if block == TEAM - 1:
            gq_ref[head * dim : (head + 1) * dim, :] = gq[head].astype(gq_ref.dtype)

    for step in range(len(units) + 2):
        if 0 <= step - 2:
            collect(step - 2)
        if 0 <= step - 1 < len(units):
            weigh(step - 1)
        if step < len(units):
            score(step)


def call(kernel, ins, out_shapes, scratch, flops, exps):
    vmem = pl.BlockSpec(memory_space=pltpu.VMEM)
    smem = pl.BlockSpec(memory_space=pltpu.SMEM)
    moved = sum(a.size * a.dtype.itemsize for a in list(ins) + list(out_shapes))
    return pl.pallas_call(
        kernel,
        in_specs=[smem if a.dtype == jnp.int32 else vmem for a in ins],
        out_specs=[vmem] * len(out_shapes),
        out_shape=out_shapes,
        scratch_shapes=scratch,
        compiler_params=pltpu.CompilerParams(vmem_limit_bytes=40 << 20),
        cost_estimate=pl.CostEstimate(flops=flops, transcendentals=exps, bytes_accessed=moved),
    )(*ins)


def body(size, latents, points, counts, w_query, w_key, w_value, w_out, d_out):
    own, width = latents.shape
    slots = points.shape[0]
    mine = width // TEAM
    shape = jax.ShapeDtypeStruct
    direct = [0, size // 4, size // 2, size // 4 + size // 2]
    middle = []
    bit = size // 8
    while bit >= TEAM:
        middle.append(bit)
        bit //= 2
    place = lax.axis_index("pts")
    even_core, even_x = place % 2 == 0, place // 2 % 2 == 0

    def swap(array, mask):
        return lax.ppermute(array, "pts", [(i, i ^ mask) for i in range(size)])

    def sort(test, a, b):
        return jnp.where(test, a, b), jnp.where(test, b, a)

    def spread(one, two, behind=None):
        quarter = [
            jnp.concatenate([a[:, i * mine : (i + 1) * mine] for a in (one, two)], axis=1)
            for i in range(TEAM)
        ]
        keep, send = sort(
            even_core,
            jnp.concatenate([quarter[0], quarter[2]], axis=1),
            jnp.concatenate([quarter[1], quarter[3]], axis=1),
        )
        if behind is not None:
            send = after(send, behind)
        both = jnp.concatenate([keep, swap(send, 1)], axis=0)
        keep, send = sort(even_x, both[:, : 2 * mine], both[:, 2 * mine :])
        return keep, send

    query_own = dot(latents, w_query).astype(BF16)
    grad_own = dot(d_out, w_out.T).astype(BF16)
    keep_qg, send_qg = spread(query_own, grad_own)
    came_qg = swap(send_qg, 2)
    points = after(points, keep_qg)
    keys = dot(points, w_key).astype(BF16) * jnp.asarray(0.125, BF16)
    values = dot(points, w_value).astype(BF16)
    keep_kv, send_kv = spread(keys, values, came_qg)
    came_kv = swap(send_kv, 2)
    qg = jnp.concatenate([keep_qg, came_qg], axis=0)
    for mask in middle:
        qg = jnp.concatenate([qg, swap(qg, mask)], axis=0)
    qg = [qg] + [swap(qg, m) for m in direct[1:]]
    pair = jnp.concatenate([counts, swap(counts, 1)])
    pair = after(pair, keep_kv)
    count_all = jnp.concatenate([pair, swap(pair, 2)])
    kv = [keep_kv, came_kv, keep_kv.T, came_kv.T]
    rows = qg[0].shape[0]
    team_slots = TEAM * slots
    work = 2 * rows * team_slots * mine

    numer, tops, stats = [None] * 4, [None] * 4, [None] * 4
    for p in range(4):
        if p:
            qg[p] = after(qg[p], stats[p - 1])
        numer[p], tops[p], stats[p] = call(
            forward_kernel,
            [count_all, qg[p]] + kv,
            [shape((mine, rows), F32), shape((MINE, rows), F32), shape((2 * MINE, rows), F32)],
            [pltpu.VMEM((3, slots, rows), F32), pltpu.VMEM((3, slots, rows), BF16)],
            flops=8 * work,
            exps=rows * team_slots * MINE,
        )

    def merge(*parts):
        lse = [p[..., :MINE, :] for p in parts]
        top = functools.reduce(jnp.maximum, lse)
        scale = [jnp.exp(x - top) for x in lse]
        total = sum(scale)
        delta = sum(s * p[..., MINE:, :] for s, p in zip(scale, parts)) / total
        return jnp.concatenate([top + jnp.log(total), delta], axis=-2)

    stat = jnp.stack(stats)
    came = [stat] + [swap(stat, m) for m in direct[1:]]
    final = jnp.stack([merge(*[came[p][q ^ p] for p in range(4)]) for q in range(4)])
    for mask in reversed(middle):
        half = final.shape[-1] // 2
        final = merge(final[..., :half], swap(final[..., half:], mask))
    for mask in middle:
        final = jnp.concatenate([final, swap(final, mask)], axis=-1)

    def add(array, came):
        return array.astype(F32) + came.astype(F32)

    def scaled(p):
        scale = jnp.exp(tops[p] - final[p, :MINE])
        return (numer[p].reshape(MINE, -1, rows) * scale[:, None, :]).reshape(mine, rows)

    scaled_a = [scaled(p) for p in range(4)]
    came_a = scaled_a[:1] + [swap(scaled_a[p].astype(BF16), direct[p]) for p in range(1, 4)]

    def backward(p, sums, behind=(), last=False):
        kind = BF16 if last else F32
        gq, *sums = call(
            functools.partial(backward_kernel, not sums, last),
            [count_all, qg[p], after(final[p], *behind)] + kv + sums,
            [shape((mine, rows), F32 if p == 0 else BF16)] + [shape((team_slots // 2, 2 * mine), kind)] * 2,
            [pltpu.VMEM((2, slots, rows), F32)] * 2 + [pltpu.VMEM((2, slots, rows), BF16)] * 2,
            flops=14 * work,
            exps=rows * team_slots * MINE,
        )
        return gq, sums

    came_q = [None] * 4
    gq, sums = backward(3, [], scaled_a[1:])
    came_q[3] = swap(gq, direct[3])
    gq, sums = backward(2, sums, [came_a[3]])
    came_q[2] = swap(gq, direct[2])
    gq, sums = backward(1, sums, [came_a[2], came_q[3]])
    came_q[1] = swap(gq, direct[1])
    came_q[0], gkv = backward(0, sums, [came_a[1], came_q[2]], last=True)

    came = swap(gkv[1], 2)
    low, high = sort(even_x, gkv[0], came)
    sides = jnp.concatenate([low, high], axis=1)
    came = swap(sides[slots:], 1)
    even, odd = sort(even_core, sides[:slots], came)

    def columns(which):
        at = [i * 2 * mine + which * mine for i in range(2)]
        return jnp.concatenate([a[:, i : i + mine] for i in at for a in (even, odd)], axis=1)

    d_points = (dot(columns(0), w_key.T) + dot(columns(1), w_value.T)).astype(BF16)

    both = jnp.stack([functools.reduce(add, came_a), functools.reduce(add, came_q)])
    for mask in reversed(middle):
        half = both.shape[-1] // 2
        both = add(both[..., :half], swap(both[..., half:].astype(BF16), mask))
    both = both.astype(BF16)
    came = swap(both[..., 2 * own :], 2)
    low, high = sort(even_x, both[..., : 2 * own], came)
    sides = jnp.stack([low, high], axis=1)
    came = swap(sides[..., own:], 1)
    even, odd = sort(even_core, sides[..., :own], came)
    joined = jnp.stack([even, odd], axis=2).reshape(2, width, own)
    result = (latents.astype(F32) + dot(joined[0].T, w_out)).astype(BF16)
    d_latents = (d_out.astype(F32) + dot(joined[1].T, w_query.T)).astype(BF16)
    return (result, d_latents, d_points)


def solution(mesh):
    part = P(("groups", "pts"), None)
    in_specs = (part, part, P(("groups", "pts")), P(), P(), P(), P(), part)
    return jax.shard_map(
        functools.partial(body, mesh.shape["pts"]),
        mesh=mesh,
        in_specs=in_specs,
        out_specs=(part, part, part),
        check_vma=False,
    )
```

```python
import functools

import jax
import jax.numpy as jnp
from jax import lax
from jax.experimental import pallas as pl
from jax.experimental.pallas import tpu as pltpu
from jax.sharding import PartitionSpec as P

HEADS = 12
TEAM = 4
MINE = HEADS // TEAM
BF16 = jnp.bfloat16
F32 = jnp.float32
LANES = 128
NT = (((1,), (1,)), ((), ()))


def dot(a, b):
    return jnp.dot(a, b, preferred_element_type=F32)


def dot_nt(a, b):
    return lax.dot_general(a, b, NT, preferred_element_type=F32)


def after(array, *others):
    return lax.optimization_barrier((array, *others))[0]


def low_lanes(shape):
    return lax.broadcasted_iota(jnp.int32, shape, 1) < shape[1] // 2


def lanes_of(part):
    start = part // 2 * LANES
    return slice(start, start + LANES)


def keep_part(array, part):
    low = low_lanes(array.shape)
    return jnp.where(low if part % 2 == 0 else ~low, array, jnp.zeros_like(array))


def block_of(refs, block, slots):
    start = block % 2 * slots
    return refs[block // 2].at[start : start + slots]


def columns_of(refs, block, slots):
    start = block % 2 * slots
    return refs[block // 2].at[:, start : start + slots]


def forward_kernel(
    count_ref, qg_ref, kv_0, kv_1, kv_t_0, kv_t_1, numer_ref, max_ref, stat_ref, score_ref, weight_ref
):
    kv_refs, kv_t_refs = (kv_0, kv_1), (kv_t_0, kv_t_1)
    rows = qg_ref.shape[0]
    dim = kv_t_0.shape[0] // (2 * MINE)
    slots = kv_0.shape[0] // 2
    depth = score_ref.shape[0]
    slot = lax.broadcasted_iota(jnp.int32, (slots, rows), 0)
    units = [(head, block) for head in range(MINE) for block in range(TEAM)]
    tops, totals, numers = {}, {}, {}

    def score(step):
        head, block = units[step]
        keys = keep_part(block_of(kv_refs, block, slots)[:, lanes_of(head)], head)
        score_ref[step % depth] = dot_nt(keys, qg_ref[:, lanes_of(head)])

    def weigh(step):
        scores = jnp.where(slot >= count_ref[units[step][1]], -jnp.inf, score_ref[step % depth])
        tops[step] = jnp.max(scores, axis=0, keepdims=True)
        weights = jnp.exp(scores - tops[step])
        totals[step] = jnp.sum(weights, axis=0, keepdims=True)
        weight_ref[step % depth] = weights.astype(BF16)

    def attend(step):
        head, block = units[step]
        part = MINE + head
        at = slice(part * dim, (part + 1) * dim)
        numers[step] = dot(columns_of(kv_t_refs, block, slots)[at, :], weight_ref[step % depth])
        if block < TEAM - 1:
            return
        steps = range(step - TEAM + 1, step + 1)
        top = functools.reduce(jnp.maximum, [tops[s] for s in steps])
        scale = {s: jnp.exp(tops[s] - top) for s in steps}
        total = sum(scale[s] * totals[s] for s in steps)
        numer = sum(scale[s] * numers[s] for s in steps)
        numer_ref[head * dim : (head + 1) * dim, :] = numer
        half = part % 2 * dim
        grad_t = qg_ref[:, lanes_of(part)].astype(F32).T[half : half + dim, :]
        inner = jnp.sum(grad_t * numer, axis=0, keepdims=True)
        max_ref[head : head + 1, :] = top
        stat_ref[head : head + 1, :] = top + jnp.log(total)
        stat_ref[MINE + head : MINE + head + 1, :] = inner / total

    for step in range(len(units) + 2):
        if step < len(units):
            score(step)
        if 0 <= step - 1 < len(units):
            weigh(step - 1)
        if 0 <= step - 2:
            attend(step - 2)


def backward_kernel(chunks, first, last, count_ref, *refs):
    qg_refs, stat_refs, refs = refs[:chunks], refs[chunks : 2 * chunks], refs[2 * chunks :]
    kv_ref, kv_t_ref, *refs = refs
    if not first:
        sum_in_ref, *refs = refs
    gq_in_refs = ()
    if len(refs) > chunks + 6:
        gq_in_refs, refs = refs[:chunks], refs[chunks:]
    gq_refs, (sum_ref, total_ref, score_ref, gw_ref, prob_ref, ds_ref) = refs[:chunks], refs[chunks:]
    rows = qg_refs[0].shape[0]
    dim = kv_t_ref.shape[0] // (2 * MINE)
    slots = kv_ref.shape[0] // 2
    depth = score_ref.shape[0]
    slot = lax.broadcasted_iota(jnp.int32, (slots, rows), 0)
    low = low_lanes((slots, LANES))
    units = [(c, head, block) for c in range(chunks) for block in range(2) for head in range(MINE)]
    gq, held = {}, {}

    def product(chunk, block, part):
        keys = kv_ref[block * slots : (block + 1) * slots, lanes_of(part)]
        return dot_nt(keep_part(keys, part), qg_refs[chunk][:, lanes_of(part)])

    def score(step):
        chunk, head, block = units[step]
        score_ref[step % depth] = product(chunk, block, head)
        gw_ref[step % depth] = product(chunk, block, MINE + head)

    def weigh(step):
        chunk, head, block = units[step]
        scores = jnp.where(slot >= count_ref[block], -jnp.inf, score_ref[step % depth])
        prob = jnp.exp(scores - stat_refs[chunk][head : head + 1, :])
        delta = stat_refs[chunk][MINE + head : MINE + head + 1, :]
        prob_ref[step % depth] = prob.astype(BF16)
        ds_ref[step % depth] = (prob * (gw_ref[step % depth] - delta)).astype(BF16)

    def store(chunk, block, part, value):
        held[part] = value
        pair = part // 2 * 2, part // 2 * 2 + 1
        if not all(p in held for p in pair):
            return
        at = slice(block * slots, (block + 1) * slots), lanes_of(part)
        total = jnp.where(low, held.pop(pair[0]), held.pop(pair[1]))
        if chunk > 0:
            total += total_ref[at]
        elif not first:
            total += sum_in_ref[at]
        if chunk < chunks - 1:
            total_ref[at] = total
            return
        if last:
            scales = [0.125 if p < MINE else 1.0 for p in pair]
            total *= scales[0] if scales[0] == scales[1] else jnp.where(low, *scales)
        sum_ref[at] = total.astype(sum_ref.dtype)

    def collect(step):
        chunk, head, block = units[step]
        qg_ref = qg_refs[chunk]
        store(chunk, block, head, dot(ds_ref[step % depth], qg_ref[:, lanes_of(head)]))
        store(chunk, block, MINE + head, dot(prob_ref[step % depth], qg_ref[:, lanes_of(MINE + head)]))
        at = slice(head * dim, (head + 1) * dim)
        term = dot(kv_t_ref[at, block * slots : (block + 1) * slots], ds_ref[step % depth])
        if block == 0:
            gq[head] = term + gq_in_refs[chunk][at, :] if gq_in_refs else term
        else:
            gq_refs[chunk][at, :] = (gq[head] + term).astype(gq_refs[chunk].dtype)

    for step in range(len(units) + 2):
        if 0 <= step - 2:
            collect(step - 2)
        if 0 <= step - 1 < len(units):
            weigh(step - 1)
        if step < len(units):
            score(step)


def queries_kernel(place_ref, near_ref, far_ref, core_ref, latents_ref, d_out_ref, w_out_ref, w_query_ref,
                   result_ref, d_latents_ref, joined_ref):
    own = latents_ref.shape[0]
    mine = near_ref.shape[1]
    even_core = place_ref[0] % 2
    even_x = place_ref[0] // 2 % 2
    for kind in range(2):
        for across in range(2):
            for core in range(2):
                quarter = 2 * (even_x ^ across) + (even_core ^ core)
                piece = core_ref[across, kind] if core else (near_ref, far_ref)[across][kind, :, :own]
                joined_ref[pl.ds(pl.multiple_of(quarter * mine, mine), mine), :] = piece.astype(F32)
        joined = joined_ref[...].T.astype(BF16)
        if kind == 0:
            result_ref[...] = (latents_ref[...].astype(F32) + dot(joined, w_out_ref[...])).astype(BF16)
        else:
            d_latents_ref[...] = (
                d_out_ref[...].astype(F32) + dot_nt(joined, w_query_ref[...])
            ).astype(BF16)


def points_kernel(place_ref, near_ref, far_ref, core_ref, weight_ref, out_ref):
    slots = out_ref.shape[0]
    even_core = place_ref[0] % 2
    even_x = place_ref[0] // 2 % 2
    total = None
    for across in range(2):
        for core in range(2):
            quarter = 2 * (even_x ^ across) + (even_core ^ core)
            piece = core_ref[across] if core else (near_ref, far_ref)[across][:slots, :]
            term = dot(piece, weight_ref[quarter])
            total = term if total is None else total + term
    out_ref[...] = total.astype(BF16)


def call(kernel, ins, out_shapes, scratch=(), flops=0, exps=0):
    vmem = pl.BlockSpec(memory_space=pltpu.VMEM)
    smem = pl.BlockSpec(memory_space=pltpu.SMEM)
    moved = sum(a.size * a.dtype.itemsize for a in list(ins) + list(out_shapes))
    return pl.pallas_call(
        kernel,
        in_specs=[smem if a.dtype == jnp.int32 else vmem for a in ins],
        out_specs=[vmem] * len(out_shapes),
        out_shape=out_shapes,
        scratch_shapes=scratch,
        compiler_params=pltpu.CompilerParams(vmem_limit_bytes=40 << 20),
        cost_estimate=pl.CostEstimate(flops=flops, transcendentals=exps, bytes_accessed=moved),
    )(*ins)


def body(size, latents, points, counts, w_query, w_key, w_value, w_out, d_out):
    own, width = latents.shape
    slots = points.shape[0]
    mine = width // TEAM
    shape = jax.ShapeDtypeStruct
    near_bit, far_bit = size // 4, size // 2
    middle = []
    bit = size // 8
    while bit >= TEAM:
        middle.append(bit)
        bit //= 2
    place = lax.axis_index("pts").astype(jnp.int32).reshape(1)
    even_core, even_x = place[0] % 2 == 0, place[0] // 2 % 2 == 0

    def swap(array, mask):
        return lax.ppermute(array, "pts", [(i, i ^ mask) for i in range(size)])

    def sort(test, a, b):
        return jnp.where(test, a, b), jnp.where(test, b, a)

    def halves(one, two):
        quarter = [
            jnp.concatenate([a[:, i * mine : (i + 1) * mine] for a in (one, two)], axis=1)
            for i in range(TEAM)
        ]
        return sort(
            even_core,
            jnp.concatenate([quarter[0], quarter[2]], axis=1),
            jnp.concatenate([quarter[1], quarter[3]], axis=1),
        )

    def spread(keep, send):
        both = jnp.concatenate([keep, swap(send, 1)], axis=0)
        return sort(even_x, both[:, : 2 * mine], both[:, 2 * mine :])

    keys = dot(points, w_key).astype(BF16) * jnp.asarray(0.125, BF16)
    values = dot(points, w_value).astype(BF16)
    keep_kv, send_kv = halves(keys, values)
    extra = 16
    high = jnp.broadcast_to((counts // 16).astype(BF16), (extra, width))
    rest = jnp.broadcast_to((counts % 16).astype(BF16), (extra, width))
    latents_in = after(latents, send_kv)
    query_own = jnp.concatenate([dot(latents_in, w_query).astype(BF16), high], axis=0)
    grad_own = jnp.concatenate([dot(d_out, w_out.T).astype(BF16), rest], axis=0)
    keep_qg, send_qg = spread(*halves(query_own, grad_own))
    came_qg = swap(send_qg, 2)
    keep_kv, send_kv = spread(keep_kv, send_kv)
    came_kv = swap(send_kv, 2)
    each = own + extra
    blocks = [a[i * each : (i + 1) * each] for a in (keep_qg, came_qg) for i in range(2)]
    qg = jnp.concatenate([a[:own] for a in blocks], axis=0)
    count = jnp.stack([16 * a[own, 0].astype(jnp.int32) + a[own, mine].astype(jnp.int32) for a in blocks])
    for mask in middle:
        qg = jnp.concatenate([qg, swap(qg, mask)], axis=0)
    qg = [qg, swap(qg, near_bit), swap(qg, far_bit)]
    qg.append(swap(qg[2], near_bit))
    kv = [keep_kv, came_kv, keep_kv.T, came_kv.T]
    weights = jnp.concatenate(
        [w.T.reshape(TEAM, mine, width) for w in (w_key, w_value)], axis=1
    )
    weights = after(weights, came_qg)
    rows = qg[0].shape[0]
    team_slots = TEAM * slots
    work = 2 * rows * team_slots * mine

    numer, tops, stats = [None] * 4, [None] * 4, [None] * 4
    for p in range(4):
        if p:
            qg[p] = after(qg[p], stats[p - 1])
        numer[p], tops[p], stats[p] = call(
            forward_kernel,
            [count, qg[p]] + kv,
            [shape((mine, rows), F32), shape((MINE, rows), F32), shape((2 * MINE, rows), F32)],
            [pltpu.VMEM((3, slots, rows), F32), pltpu.VMEM((3, slots, rows), BF16)],
            flops=8 * work,
            exps=rows * team_slots * MINE,
        )

    def merge(*parts):
        lse = [p[..., :MINE, :] for p in parts]
        top = functools.reduce(jnp.maximum, lse)
        scale = [jnp.exp(x - top) for x in lse]
        total = sum(scale)
        delta = sum(s * p[..., MINE:, :] for s, p in zip(scale, parts)) / total
        return jnp.concatenate([top + jnp.log(total), delta], axis=-2)

    stat = jnp.stack(stats)
    came = [stat] + [swap(stat, m) for m in (near_bit, far_bit, near_bit + far_bit)]
    final = [merge(*[came[p][q ^ p] for p in range(4)]) for q in range(4)]
    if middle:
        final = jnp.stack(final)
        for mask in reversed(middle):
            half = final.shape[-1] // 2
            final = merge(final[..., :half], swap(final[..., half:], mask))
        for mask in middle:
            final = jnp.concatenate([final, swap(final, mask)], axis=-1)
        final = [final[q] for q in range(4)]

    def add(array, came):
        return array.astype(F32) + came.astype(F32)

    def scaled(p):
        scale = jnp.exp(tops[p] - final[p][:MINE])
        return (numer[p].reshape(MINE, -1, rows) * scale[:, None, :]).reshape(mine, rows)

    def backward(chunks, side, sums=(), partial=(), behind=(), first=True, last=False, kinds=()):
        stat = [final[p] for p in chunks]
        stat[0] = after(stat[0], *behind)
        kept = (team_slots // 2, 2 * mine)
        return call(
            functools.partial(backward_kernel, len(chunks), first, last),
            [count[2 * side : 2 * side + 2]]
            + [qg[p] for p in chunks]
            + stat
            + [kv[side], kv[2 + side]]
            + list(sums)
            + list(partial),
            [shape((mine, rows), k) for k in kinds] + [shape(kept, BF16 if last else F32)],
            [pltpu.VMEM(kept if len(chunks) > 1 else (8, LANES), F32)]
            + [pltpu.VMEM((2, slots, rows), F32)] * 2
            + [pltpu.VMEM((2, slots, rows), BF16)] * 2,
            flops=7 * work * len(chunks),
            exps=rows * team_slots // 2 * MINE * len(chunks),
        )

    scaled_3 = scaled(3).astype(BF16)
    scaled_2 = scaled(2)
    came_a3 = swap(scaled_3, near_bit)
    order = (3, 2, 1, 0)
    *partial, gkv_far = backward(order, 1, behind=[scaled_2, scaled_3], last=True, kinds=[F32] * 4)
    came_far = swap(gkv_far, 2)
    came_a2 = swap(add(scaled_2, came_a3).astype(BF16), far_bit)
    came_a1 = swap(scaled(1).astype(BF16), near_bit)
    gq_3, total = backward((3,), 0, partial=partial[:1], behind=[gkv_far], kinds=[BF16])
    came_3 = swap(gq_3, near_bit)
    gq_2, total = backward((2,), 0, [total], partial[1:2], [came_a2], False, kinds=[F32])
    sent_2 = add(gq_2, came_3).astype(BF16)
    came_2 = swap(sent_2, far_bit)
    gq_1, total = backward((1,), 0, [total], partial[2:3], [came_a1, sent_2], False, kinds=[BF16])
    came_1 = swap(gq_1, near_bit)
    gq_0, gkv_near = backward((0,), 0, [total], partial[3:], (), False, True, kinds=[F32])
    attended = add(add(scaled(0), came_a1), came_a2)
    grad_query = add(add(gq_0, came_1), came_2)

    both = jnp.stack([attended, grad_query])
    for mask in reversed(middle):
        half = both.shape[-1] // 2
        both = add(both[..., :half], swap(both[..., half:].astype(BF16), mask))
    both = both.astype(BF16)
    far = swap(both[..., 2 * own :], 2)
    near = both[..., : 2 * own]
    core = swap(jnp.stack([near[..., own:], far[..., own:]]), 1)
    result, d_latents = call(
        queries_kernel,
        [place, near, far, core, latents, d_out, w_out, w_query],
        [shape((own, width), BF16)] * 2,
        [pltpu.VMEM((width, own), F32)],
        flops=4 * own * width * width,
    )

    core = swap(jnp.stack([gkv_near[slots:], came_far[slots:]]), 1)
    (d_points,) = call(
        points_kernel,
        [place, gkv_near, came_far, core, weights],
        [shape((slots, width), BF16)],
        flops=4 * slots * width * width,
    )
    return (result, d_latents, d_points)


def solution(mesh):
    part = P(("groups", "pts"), None)
    in_specs = (part, part, P(("groups", "pts")), P(), P(), P(), P(), part)
    return jax.shard_map(
        functools.partial(body, mesh.shape["pts"]),
        mesh=mesh,
        in_specs=in_specs,
        out_specs=(part, part, part),
        check_vma=False,
    )
```

```python
import functools

import jax
import jax.numpy as jnp
from jax import lax
from jax.experimental import pallas as pl
from jax.experimental.pallas import tpu as pltpu
from jax.sharding import PartitionSpec as P

HEADS = 12
TEAM = 4
MINE = HEADS // TEAM
BF16 = jnp.bfloat16
F32 = jnp.float32
LANES = 128
NT = (((1,), (1,)), ((), ()))


def dot(a, b):
    return jnp.dot(a, b, preferred_element_type=F32)


def dot_nt(a, b):
    return lax.dot_general(a, b, NT, preferred_element_type=F32)


def after(array, *others):
    return lax.optimization_barrier((array, *others))[0]


def low_lanes(shape):
    return lax.broadcasted_iota(jnp.int32, shape, 1) < shape[1] // 2


def lanes_of(part):
    start = part // 2 * LANES
    return slice(start, start + LANES)


def keep_part(array, part):
    low = low_lanes(array.shape)
    return jnp.where(low if part % 2 == 0 else ~low, array, jnp.zeros_like(array))


def team_place(place_ref, quarter):
    relative = (place_ref[0] % TEAM) ^ quarter
    return relative % 2, relative // 2


def store_quarters(place_ref, keep_ref, send_ref, one, two, at):
    mine = one.shape[1] // TEAM
    for quarter in range(TEAM):
        cols = slice(quarter * mine, (quarter + 1) * mine)
        piece = jnp.concatenate([one[:, cols], two[:, cols]], axis=1)
        core, across = team_place(place_ref, quarter)
        for ref, which in ((keep_ref, 0), (send_ref, 1)):

            @pl.when(core == which)
            def _():
                ref[across, at, :] = piece


def slots_kernel(place_ref, points_ref, w_key_ref, w_value_ref, keep_ref, send_ref):
    keys = dot(points_ref[...], w_key_ref[...]).astype(BF16) * jnp.asarray(0.125, BF16)
    values = dot(points_ref[...], w_value_ref[...]).astype(BF16)
    store_quarters(place_ref, keep_ref, send_ref, keys, values, slice(0, keys.shape[0]))


def rows_kernel(
    place_ref, count_ref, latents_ref, d_out_ref, w_query_ref, w_out_ref, keep_ref, send_ref
):
    own = latents_ref.shape[0]
    query = dot(latents_ref[...], w_query_ref[...]).astype(BF16)
    grad = dot_nt(d_out_ref[...], w_out_ref[...]).astype(BF16)
    store_quarters(place_ref, keep_ref, send_ref, query, grad, slice(0, own))
    extra = keep_ref.shape[1] - own, keep_ref.shape[2]
    first = lax.broadcasted_iota(jnp.int32, extra, 1) < extra[1] // 2
    count = jnp.where(first, count_ref[0] // 16, count_ref[0] % 16).astype(F32).astype(BF16)
    for ref in (keep_ref, send_ref):
        for across in range(2):
            ref[across, own:, :] = count


def dead_slots(slot, count_ref, block):
    count = jnp.concatenate([count_ref[block : block + 1, :]] * (slot.shape[1] // LANES), axis=1)
    return slot >= count


def forward_kernel(
    count_ref, qg_ref, keep_ref, core_ref, far_ref, near_t_ref, far_t_ref,
    numer_ref, max_ref, stat_ref, score_ref, weight_ref
):
    rows = qg_ref.shape[0]
    slots = keep_ref.shape[1]
    dim = keep_ref.shape[2] // (2 * MINE)
    depth = score_ref.shape[0]
    kv_refs = [keep_ref.at[0], core_ref.at[0], far_ref.at[0], far_ref.at[1]]
    kv_t_refs = [near_t_ref.at[0], near_t_ref.at[1], far_t_ref.at[0], far_t_ref.at[1]]
    slot = lax.broadcasted_iota(jnp.int32, (slots, rows), 0).astype(F32)
    units = [(head, block) for head in range(MINE) for block in range(TEAM)]
    tops, totals, numers = {}, {}, {}

    def score(step):
        head, block = units[step]
        keys = keep_part(kv_refs[block][:, lanes_of(head)], head)
        score_ref[step % depth] = dot_nt(keys, qg_ref[:, lanes_of(head)])

    def weigh(step):
        dead = dead_slots(slot, count_ref, units[step][1])
        scores = jnp.where(dead, -jnp.inf, score_ref[step % depth])
        tops[step] = jnp.max(scores, axis=0, keepdims=True)
        weights = jnp.exp(scores - tops[step])
        totals[step] = jnp.sum(weights, axis=0, keepdims=True)
        weight_ref[step % depth] = weights.astype(BF16)

    def attend(step):
        head, block = units[step]
        part = MINE + head
        at = slice(part * dim, (part + 1) * dim)
        numers[step] = dot(kv_t_refs[block][at, :], weight_ref[step % depth])
        if block < TEAM - 1:
            return
        steps = range(step - TEAM + 1, step + 1)
        top = functools.reduce(jnp.maximum, [tops[s] for s in steps])
        scale = {s: jnp.exp(tops[s] - top) for s in steps}
        total = sum(scale[s] * totals[s] for s in steps)
        numer = sum(scale[s] * numers[s] for s in steps)
        numer_ref[head * dim : (head + 1) * dim, :] = numer
        half = part % 2 * dim
        grad_t = qg_ref[:, lanes_of(part)].astype(F32).T[half : half + dim, :]
        inner = jnp.sum(grad_t * numer, axis=0, keepdims=True)
        max_ref[head : head + 1, :] = top
        stat_ref[head : head + 1, :] = top + jnp.log(total)
        stat_ref[MINE + head : MINE + head + 1, :] = inner / total

    for step in range(len(units) + 2):
        if step < len(units):
            score(step)
        if 0 <= step - 1 < len(units):
            weigh(step - 1)
        if 0 <= step - 2:
            attend(step - 2)


def backward_kernel(chunks, start, side, first, last, count_ref, *refs):
    qg_refs, stat_refs, refs = refs[:chunks], refs[chunks : 2 * chunks], refs[2 * chunks :]
    even_ref, odd_ref, kv_t_ref, *refs = refs
    kv_refs = even_ref.at[0], odd_ref.at[side]
    if not first:
        sum_in_ref, *refs = refs
    gq_in_ref = None
    if side == 0:
        gq_in_ref, *refs = refs
    gq_ref, sum_ref, total_ref, score_ref, gw_ref, prob_ref, ds_ref = refs
    rows = qg_refs[0].shape[0]
    slots, dim = even_ref.shape[1], even_ref.shape[2] // (2 * MINE)
    depth = score_ref.shape[0]
    slot = lax.broadcasted_iota(jnp.int32, (slots, rows), 0).astype(F32)
    low = low_lanes((slots, LANES))
    units = [(c, head, block) for c in range(chunks) for block in range(2) for head in range(MINE)]
    gq, held = {}, {}

    def product(chunk, block, part):
        return dot_nt(keep_part(kv_refs[block][:, lanes_of(part)], part), qg_refs[chunk][:, lanes_of(part)])

    def score(step):
        chunk, head, block = units[step]
        score_ref[step % depth] = product(chunk, block, head)
        gw_ref[step % depth] = product(chunk, block, MINE + head)

    def weigh(step):
        chunk, head, block = units[step]
        dead = dead_slots(slot, count_ref, 2 * side + block)
        scores = jnp.where(dead, -jnp.inf, score_ref[step % depth])
        prob = jnp.exp(scores - stat_refs[chunk][head : head + 1, :])
        delta = stat_refs[chunk][MINE + head : MINE + head + 1, :]
        prob_ref[step % depth] = prob.astype(BF16)
        ds_ref[step % depth] = (prob * (gw_ref[step % depth] - delta)).astype(BF16)

    def store(chunk, block, part, value):
        held[part] = value
        pair = part // 2 * 2, part // 2 * 2 + 1
        if not all(p in held for p in pair):
            return
        at = block, slice(0, slots), lanes_of(part)
        total = jnp.where(low, held.pop(pair[0]), held.pop(pair[1]))
        if chunk > 0:
            total += total_ref[at]
        elif not first:
            total += sum_in_ref[at]
        if chunk < chunks - 1:
            total_ref[at] = total
            return
        if last:
            scales = [0.125 if p < MINE else 1.0 for p in pair]
            total *= scales[0] if scales[0] == scales[1] else jnp.where(low, *scales)
        sum_ref[at] = total.astype(sum_ref.dtype)

    def collect(step):
        chunk, head, block = units[step]
        qg_ref = qg_refs[chunk]
        store(chunk, block, head, dot(ds_ref[step % depth], qg_ref[:, lanes_of(head)]))
        store(chunk, block, MINE + head, dot(prob_ref[step % depth], qg_ref[:, lanes_of(MINE + head)]))
        at = slice(head * dim, (head + 1) * dim)
        term = dot(kv_t_ref[block, at, :], ds_ref[step % depth])
        if block == 0:
            gq[head] = term if gq_in_ref is None else term + gq_in_ref[start + chunk, at, :]
        else:
            gq_ref[chunk, at, :] = (gq[head] + term).astype(gq_ref.dtype)

    for step in range(len(units) + 2):
        if 0 <= step - 2:
            collect(step - 2)
        if 0 <= step - 1 < len(units):
            weigh(step - 1)
        if step < len(units):
            score(step)


def queries_kernel(
    place_ref, near_ref, far_ref, core_ref, latents_ref, d_out_ref, w_out_ref, w_query_ref,
    result_ref, d_latents_ref, joined_ref
):
    own = latents_ref.shape[0]
    mine = near_ref.shape[1]
    for kind in range(2):
        for relative in range(TEAM):
            core, across = relative % 2, relative // 2
            quarter = (place_ref[0] % TEAM) ^ relative
            piece = core_ref[across, kind] if core else (near_ref, far_ref)[across][kind, :, :own]
            joined_ref[pl.ds(pl.multiple_of(quarter * mine, mine), mine), :] = piece.astype(F32)
        joined = joined_ref[...].T.astype(BF16)
        if kind == 0:
            result_ref[...] = (latents_ref[...].astype(F32) + dot(joined, w_out_ref[...])).astype(BF16)
        else:
            d_latents_ref[...] = (
                d_out_ref[...].astype(F32) + dot_nt(joined, w_query_ref[...])
            ).astype(BF16)


def points_kernel(
    place_ref, near_ref, far_ref, core_ref, w_key_ref, w_value_ref, out_ref, key_ref, value_ref
):
    mine = key_ref.shape[1] // TEAM
    for relative in range(TEAM):
        core, across = relative % 2, relative // 2
        piece = core_ref[across] if core else (near_ref, far_ref)[across][0]
        for quarter in range(TEAM):

            @pl.when((place_ref[0] % TEAM) ^ relative == quarter)
            def _():
                key_ref[:, quarter * mine : (quarter + 1) * mine] = piece[:, :mine]
                value_ref[:, quarter * mine : (quarter + 1) * mine] = piece[:, mine:]

    total = dot_nt(key_ref[...], w_key_ref[...]) + dot_nt(value_ref[...], w_value_ref[...])
    out_ref[...] = total.astype(BF16)


def call(kernel, ins, out_shapes, scratch=(), flops=0, exps=0):
    vmem = pl.BlockSpec(memory_space=pltpu.VMEM)
    smem = pl.BlockSpec(memory_space=pltpu.SMEM)
    moved = sum(a.size * a.dtype.itemsize for a in list(ins) + list(out_shapes))
    return pl.pallas_call(
        kernel,
        in_specs=[smem if a.dtype == jnp.int32 else vmem for a in ins],
        out_specs=[vmem] * len(out_shapes),
        out_shape=out_shapes,
        scratch_shapes=scratch,
        compiler_params=pltpu.CompilerParams(vmem_limit_bytes=40 << 20),
        cost_estimate=pl.CostEstimate(flops=flops // 8, transcendentals=exps // 8, bytes_accessed=moved // 8),
    )(*ins)


def body(size, latents, points, counts, w_query, w_key, w_value, w_out, d_out):
    own, width = latents.shape
    slots = points.shape[0]
    mine = width // TEAM
    shape = jax.ShapeDtypeStruct
    near_bit, far_bit = size // 4, size // 2
    middle = []
    bit = size // 8
    while bit >= TEAM:
        middle.append(bit)
        bit //= 2
    place = lax.axis_index("pts").astype(jnp.int32).reshape(1)

    def swap(array, mask):
        return lax.ppermute(array, "pts", [(i, i ^ mask) for i in range(size)])

    each = own + 16
    keep_qg, send_qg = call(
        rows_kernel,
        [place, counts, latents, d_out, w_query, w_out],
        [shape((2, each, 2 * mine), BF16)] * 2,
        flops=4 * own * width * width,
    )
    keep, send = call(
        slots_kernel,
        [place, after(points, send_qg), w_key, w_value],
        [shape((2, slots, 2 * mine), BF16)] * 2,
        flops=4 * slots * width * width,
    )
    core_qg = swap(send_qg, 1)
    far_qg = swap(jnp.stack([keep_qg[1], core_qg[1]]), 2)
    core = swap(send, 1)
    far = swap(jnp.stack([keep[1], core[1]]), 2)
    blocks = [keep_qg[0], core_qg[0], far_qg[0], far_qg[1]]
    qg = jnp.concatenate([a[:own] for a in blocks], axis=0)
    tail = jnp.concatenate([a[own : own + 1] for a in blocks], axis=0).astype(F32)
    count = 16 * tail[:, :LANES] + tail[:, mine : mine + LANES]
    for mask in middle:
        qg = jnp.concatenate([qg, swap(qg, mask)], axis=0)
    qg = [qg, swap(qg, near_bit), swap(qg, far_bit)]
    qg.append(swap(qg[2], near_bit))
    near_t = jnp.stack([keep[0].T, core[0].T])
    far_t = jnp.swapaxes(far, 1, 2)
    rows = qg[0].shape[0]
    team_slots = TEAM * slots
    work = 2 * rows * team_slots * mine

    numer, tops, stats = [None] * 4, [None] * 4, [None] * 4
    for p in range(4):
        if p:
            qg[p] = after(qg[p], stats[p - 1])
        numer[p], tops[p], stats[p] = call(
            forward_kernel,
            [count, qg[p], keep, core, far, near_t, far_t],
            [shape((mine, rows), F32), shape((MINE, rows), F32), shape((2 * MINE, rows), F32)],
            [pltpu.VMEM((3, slots, rows), F32), pltpu.VMEM((3, slots, rows), BF16)],
            flops=8 * work,
            exps=rows * team_slots * MINE,
        )

    def merge(*parts):
        lse = [p[..., :MINE, :] for p in parts]
        top = functools.reduce(jnp.maximum, lse)
        scale = [jnp.exp(x - top) for x in lse]
        total = sum(scale)
        delta = sum(s * p[..., MINE:, :] for s, p in zip(scale, parts)) / total
        return jnp.concatenate([top + jnp.log(total), delta], axis=-2)

    stat = jnp.stack(stats)
    came = [stat] + [swap(stat, m) for m in (near_bit, far_bit, near_bit + far_bit)]
    final = [merge(*[came[p][q ^ p] for p in range(4)]) for q in range(4)]
    if middle:
        final = jnp.stack(final)
        for mask in reversed(middle):
            half = final.shape[-1] // 2
            final = merge(final[..., :half], swap(final[..., half:], mask))
        for mask in middle:
            final = jnp.concatenate([final, swap(final, mask)], axis=-1)
        final = [final[q] for q in range(4)]

    def add(array, came):
        return array.astype(F32) + came.astype(F32)

    def scaled(p):
        scale = jnp.exp(tops[p] - final[p][:MINE])
        return (numer[p].reshape(MINE, -1, rows) * scale[:, None, :]).reshape(mine, rows)

    order = (3, 2, 1, 0)

    def backward(chunks, side, kind, sums=(), partial=(), last=False):
        kept = (2, slots, 2 * mine)
        return call(
            functools.partial(
                backward_kernel, len(chunks), order.index(chunks[0]), side, not sums, last
            ),
            [count]
            + [qg[p] for p in chunks]
            + [final[p] for p in chunks]
            + ([far, far, far_t] if side else [keep, core, near_t])
            + list(sums)
            + list(partial),
            [shape((len(chunks), mine, rows), kind), shape(kept, BF16 if last else F32)],
            [pltpu.VMEM(kept if len(chunks) > 1 else (1, 8, LANES), F32)]
            + [pltpu.VMEM((2, slots, rows), F32)] * 2
            + [pltpu.VMEM((2, slots, rows), BF16)] * 2,
            flops=7 * work * len(chunks),
            exps=rows * team_slots // 2 * MINE * len(chunks),
        )

    came_a = swap(jnp.stack([scaled(3), scaled(2)]).astype(BF16), far_bit)
    partial, gkv_far = backward(order, 1, F32, last=True)
    came_a, partial = lax.optimization_barrier((came_a, partial))
    came_far = swap(gkv_far, 2)
    near_a = swap(add(scaled(1), came_a[0]).astype(BF16), near_bit)
    gq, total = backward((3, 2), 0, BF16, partial=[partial])
    came_q = swap(gq, far_bit)
    gq, total = backward((1,), 0, F32, [total], [partial])
    near_q = swap(add(gq[0], came_q[0]).astype(BF16), near_bit)
    gq, gkv_near = backward((0,), 0, F32, [total], [partial], True)
    attended = add(add(scaled(0), near_a), came_a[1])
    grad_query = add(add(gq[0], near_q), came_q[1])

    both = jnp.stack([attended, grad_query])
    for mask in reversed(middle):
        half = both.shape[-1] // 2
        both = add(both[..., :half], swap(both[..., half:].astype(BF16), mask))
    both, came_far = lax.optimization_barrier((both.astype(BF16), came_far))
    far_both = swap(both[..., 2 * own :], 2)
    near_both = both[..., : 2 * own]

    core_gkv = swap(jnp.stack([gkv_near[1], came_far[1]]), 1)
    (d_points,) = call(
        points_kernel,
        [place, gkv_near, came_far, core_gkv, w_key, w_value],
        [shape((slots, width), BF16)],
        [pltpu.VMEM((slots, width), BF16)] * 2,
        flops=4 * slots * width * width,
    )
    far_both, d_points = lax.optimization_barrier((far_both, d_points))
    core_both = swap(jnp.stack([near_both[..., own:], far_both[..., own:]]), 1)
    result, d_latents = call(
        queries_kernel,
        [place, near_both, far_both, core_both, latents, d_out, w_out, w_query],
        [shape((own, width), BF16)] * 2,
        [pltpu.VMEM((width, own), F32)],
        flops=4 * own * width * width,
    )
    return (result, d_latents, d_points)


def solution(mesh):
    part = P(("groups", "pts"), None)
    in_specs = (part, part, P(("groups", "pts")), P(), P(), P(), P(), part)
    return jax.shard_map(
        functools.partial(body, mesh.shape["pts"]),
        mesh=mesh,
        in_specs=in_specs,
        out_specs=(part, part, part),
        check_vma=False,
    )
```

```python
import functools

import jax
import jax.numpy as jnp
from jax import lax
from jax.experimental import pallas as pl
from jax.experimental.pallas import tpu as pltpu
from jax.sharding import PartitionSpec as P

HEADS = 12
TEAM = 4
MINE = HEADS // TEAM
BF16 = jnp.bfloat16
F32 = jnp.float32
LANES = 128
NT = (((1,), (1,)), ((), ()))


def dot(a, b):
    return jnp.dot(a, b, preferred_element_type=F32)


def dot_nt(a, b):
    return lax.dot_general(a, b, NT, preferred_element_type=F32)


def low_lanes(shape):
    return lax.broadcasted_iota(jnp.int32, shape, 1) < shape[1] // 2


def lanes_of(part):
    start = part // 2 * LANES
    return slice(start, start + LANES)


def keep_part(array, part):
    low = low_lanes(array.shape)
    return jnp.where(low if part % 2 == 0 else ~low, array, jnp.zeros_like(array))


def team_place(place_ref, quarter):
    relative = (place_ref[0] % TEAM) ^ quarter
    return relative % 2, relative // 2


def store_quarters(place_ref, keep_ref, send_ref, one, two, at):
    mine = one.shape[1] // TEAM
    for quarter in range(TEAM):
        cols = slice(quarter * mine, (quarter + 1) * mine)
        piece = jnp.concatenate([one[:, cols], two[:, cols]], axis=1)
        core, across = team_place(place_ref, quarter)
        for ref, which in ((keep_ref, 0), (send_ref, 1)):

            @pl.when(core == which)
            def _():
                ref[across, at, :] = piece


def slots_kernel(place_ref, points_ref, w_key_ref, w_value_ref, keep_ref, send_ref):
    keys = dot(points_ref[...], w_key_ref[...]).astype(BF16) * jnp.asarray(0.125, BF16)
    values = dot(points_ref[...], w_value_ref[...]).astype(BF16)
    store_quarters(place_ref, keep_ref, send_ref, keys, values, slice(0, keys.shape[0]))


def rows_kernel(
    place_ref, count_ref, latents_hbm, d_out_hbm, w_query_hbm, w_out_hbm,
    keep_ref, send_ref, latents_ref, d_out_ref, w_query_ref, w_out_ref, sems
):
    own, pieces = latents_ref.shape[0], sems.shape[1] - 1
    loads = []
    for i, (small, small_to, big, big_to) in enumerate(
        (
            (latents_hbm, latents_ref, w_query_hbm, w_query_ref),
            (d_out_hbm, d_out_ref, w_out_hbm, w_out_ref),
        )
    ):
        step = big.shape[0] // pieces
        group = [pltpu.make_async_copy(small, small_to, sems.at[i, pieces])]
        for k in range(pieces):
            at = slice(k * step, (k + 1) * step)
            group.append(pltpu.make_async_copy(big.at[at], big_to.at[at], sems.at[i, k]))
        for copy in group:
            copy.start()
        loads.append(group)
    for copy in loads[0]:
        copy.wait()
    query = dot(latents_ref[...], w_query_ref[...]).astype(BF16)
    for copy in loads[1]:
        copy.wait()
    grad = dot_nt(d_out_ref[...], w_out_ref[...]).astype(BF16)
    store_quarters(place_ref, keep_ref, send_ref, query, grad, slice(0, own))
    extra = keep_ref.shape[1] - own, keep_ref.shape[2]
    first = lax.broadcasted_iota(jnp.int32, extra, 1) < extra[1] // 2
    count = jnp.where(first, count_ref[0] // 16, count_ref[0] % 16).astype(F32).astype(BF16)
    for ref in (keep_ref, send_ref):
        for across in range(2):
            ref[across, own:, :] = count


def turn_kernel(picks, *refs):
    for i, (ref, which) in enumerate(picks):
        refs[-1][i] = refs[ref][which].T


def dead_slots(slot, count_ref, block):
    count = jnp.concatenate([count_ref[block : block + 1, :]] * (slot.shape[1] // LANES), axis=1)
    return slot >= count


def forward_kernel(
    count_ref, qg_ref, keep_ref, core_ref, far_ref, near_t_ref, far_t_ref,
    numer_ref, max_ref, stat_ref, score_ref, weight_ref
):
    rows = qg_ref.shape[0]
    slots = keep_ref.shape[1]
    dim = keep_ref.shape[2] // (2 * MINE)
    depth = score_ref.shape[0]
    kv_refs = [keep_ref.at[0], core_ref.at[0], far_ref.at[0], far_ref.at[1]]
    kv_t_refs = [near_t_ref.at[0], near_t_ref.at[1], far_t_ref.at[0], far_t_ref.at[1]]
    slot = lax.broadcasted_iota(jnp.int32, (slots, rows), 0).astype(F32)
    units = [(head, block) for head in range(MINE) for block in range(TEAM)]
    tops, totals, numers = {}, {}, {}

    def score(step):
        head, block = units[step]
        keys = keep_part(kv_refs[block][:, lanes_of(head)], head)
        score_ref[step % depth] = dot_nt(keys, qg_ref[:, lanes_of(head)])

    def weigh(step):
        dead = dead_slots(slot, count_ref, units[step][1])
        scores = jnp.where(dead, -jnp.inf, score_ref[step % depth])
        tops[step] = jnp.max(scores, axis=0, keepdims=True)
        weights = jnp.exp(scores - tops[step])
        totals[step] = jnp.sum(weights, axis=0, keepdims=True)
        weight_ref[step % depth] = weights.astype(BF16)

    def attend(step):
        head, block = units[step]
        part = MINE + head
        at = slice(part * dim, (part + 1) * dim)
        numers[step] = dot(kv_t_refs[block][at, :], weight_ref[step % depth])
        if block < TEAM - 1:
            return
        steps = range(step - TEAM + 1, step + 1)
        top = functools.reduce(jnp.maximum, [tops[s] for s in steps])
        scale = {s: jnp.exp(tops[s] - top) for s in steps}
        total = sum(scale[s] * totals[s] for s in steps)
        numer = sum(scale[s] * numers[s] for s in steps)
        numer_ref[head * dim : (head + 1) * dim, :] = numer
        half = part % 2 * dim
        grad_t = qg_ref[:, lanes_of(part)].astype(F32).T[half : half + dim, :]
        inner = jnp.sum(grad_t * numer, axis=0, keepdims=True)
        max_ref[head : head + 1, :] = top
        stat_ref[head : head + 1, :] = top + jnp.log(total)
        stat_ref[MINE + head : MINE + head + 1, :] = inner / total

    for step in range(len(units) + 2):
        if step < len(units):
            score(step)
        if 0 <= step - 1 < len(units):
            weigh(step - 1)
        if 0 <= step - 2:
            attend(step - 2)


def backward_kernel(chunks, start, side, first, last, count_ref, *refs):
    qg_refs, stat_refs, refs = refs[:chunks], refs[chunks : 2 * chunks], refs[2 * chunks :]
    even_ref, odd_ref, kv_t_ref, *refs = refs
    kv_refs = even_ref.at[0], odd_ref.at[side]
    if not first:
        sum_in_ref, *refs = refs
    gq_in_ref = None
    if side == 0:
        gq_in_ref, *refs = refs
    gq_ref, sum_ref, total_ref, score_ref, gw_ref, prob_ref, ds_ref = refs
    rows = qg_refs[0].shape[0]
    slots, dim = even_ref.shape[1], even_ref.shape[2] // (2 * MINE)
    depth = score_ref.shape[0]
    slot = lax.broadcasted_iota(jnp.int32, (slots, rows), 0).astype(F32)
    low = low_lanes((slots, LANES))
    units = [(c, head, block) for c in range(chunks) for block in range(2) for head in range(MINE)]
    gq, held = {}, {}

    def product(chunk, block, part):
        return dot_nt(keep_part(kv_refs[block][:, lanes_of(part)], part), qg_refs[chunk][:, lanes_of(part)])

    def score(step):
        chunk, head, block = units[step]
        score_ref[step % depth] = product(chunk, block, head)
        gw_ref[step % depth] = product(chunk, block, MINE + head)

    def weigh(step):
        chunk, head, block = units[step]
        dead = dead_slots(slot, count_ref, 2 * side + block)
        scores = jnp.where(dead, -jnp.inf, score_ref[step % depth])
        prob = jnp.exp(scores - stat_refs[chunk][head : head + 1, :])
        delta = stat_refs[chunk][MINE + head : MINE + head + 1, :]
        prob_ref[step % depth] = prob.astype(BF16)
        ds_ref[step % depth] = (prob * (gw_ref[step % depth] - delta)).astype(BF16)

    def store(chunk, block, part, value):
        held[part] = value
        pair = part // 2 * 2, part // 2 * 2 + 1
        if not all(p in held for p in pair):
            return
        at = block, slice(0, slots), lanes_of(part)
        total = jnp.where(low, held.pop(pair[0]), held.pop(pair[1]))
        if chunk > 0:
            total += total_ref[at]
        elif not first:
            total += sum_in_ref[at]
        if chunk < chunks - 1:
            total_ref[at] = total
            return
        if last:
            scales = [0.125 if p < MINE else 1.0 for p in pair]
            total *= scales[0] if scales[0] == scales[1] else jnp.where(low, *scales)
        sum_ref[at] = total.astype(sum_ref.dtype)

    def collect(step):
        chunk, head, block = units[step]
        qg_ref = qg_refs[chunk]
        store(chunk, block, head, dot(ds_ref[step % depth], qg_ref[:, lanes_of(head)]))
        store(chunk, block, MINE + head, dot(prob_ref[step % depth], qg_ref[:, lanes_of(MINE + head)]))
        at = slice(head * dim, (head + 1) * dim)
        term = dot(kv_t_ref[block, at, :], ds_ref[step % depth])
        if block == 0:
            gq[head] = term if gq_in_ref is None else term + gq_in_ref[start + chunk, at, :]
        else:
            gq_ref[chunk, at, :] = (gq[head] + term).astype(gq_ref.dtype)

    for step in range(len(units) + 2):
        if 0 <= step - 2:
            collect(step - 2)
        if 0 <= step - 1 < len(units):
            weigh(step - 1)
        if step < len(units):
            score(step)


def queries_kernel(
    place_ref, near_ref, far_ref, core_ref, latents_ref, d_out_ref, w_out_ref, w_query_ref,
    result_ref, d_latents_ref, joined_ref
):
    own = latents_ref.shape[0]
    mine = near_ref.shape[1]
    for kind in range(2):
        for relative in range(TEAM):
            core, across = relative % 2, relative // 2
            quarter = (place_ref[0] % TEAM) ^ relative
            piece = core_ref[across, kind] if core else (near_ref, far_ref)[across][kind, :, :own]
            joined_ref[pl.ds(pl.multiple_of(quarter * mine, mine), mine), :] = piece.astype(F32)
        joined = joined_ref[...].T.astype(BF16)
        if kind == 0:
            result_ref[...] = (latents_ref[...].astype(F32) + dot(joined, w_out_ref[...])).astype(BF16)
        else:
            d_latents_ref[...] = (
                d_out_ref[...].astype(F32) + dot_nt(joined, w_query_ref[...])
            ).astype(BF16)


def points_kernel(
    place_ref, near_ref, far_ref, core_ref, w_key_ref, w_value_ref, out_ref, key_ref, value_ref
):
    mine = key_ref.shape[1] // TEAM
    for relative in range(TEAM):
        core, across = relative % 2, relative // 2
        piece = core_ref[across] if core else (near_ref, far_ref)[across][0]
        for quarter in range(TEAM):

            @pl.when((place_ref[0] % TEAM) ^ relative == quarter)
            def _():
                key_ref[:, quarter * mine : (quarter + 1) * mine] = piece[:, :mine]
                value_ref[:, quarter * mine : (quarter + 1) * mine] = piece[:, mine:]

    total = dot_nt(key_ref[...], w_key_ref[...]) + dot_nt(value_ref[...], w_value_ref[...])
    out_ref[...] = total.astype(BF16)


def call(kernel, ins, out_shapes, scratch=(), flops=0, exps=0, space=pltpu.VMEM):
    vmem = pl.BlockSpec(memory_space=pltpu.VMEM)
    other = pl.BlockSpec(memory_space=space)
    smem = pl.BlockSpec(memory_space=pltpu.SMEM)
    moved = sum(a.size * a.dtype.itemsize for a in list(ins) + list(out_shapes))
    return pl.pallas_call(
        kernel,
        in_specs=[smem if a.dtype == jnp.int32 else other for a in ins],
        out_specs=[vmem] * len(out_shapes),
        out_shape=out_shapes,
        scratch_shapes=scratch,
        compiler_params=pltpu.CompilerParams(vmem_limit_bytes=40 << 20),
        cost_estimate=pl.CostEstimate(flops=flops // 8, transcendentals=exps // 8, bytes_accessed=moved // 8),
    )(*ins)


def body(size, latents, points, counts, w_query, w_key, w_value, w_out, d_out):
    own, width = latents.shape
    slots = points.shape[0]
    mine = width // TEAM
    shape = jax.ShapeDtypeStruct
    near_bit, far_bit = size // 4, size // 2
    middle = []
    bit = size // 8
    while bit >= TEAM:
        middle.append(bit)
        bit //= 2
    place = lax.axis_index("pts").astype(jnp.int32).reshape(1)

    def swap(array, mask):
        return lax.ppermute(array, "pts", [(i, i ^ mask) for i in range(size)])

    each = own + 16
    keep_qg, send_qg = call(
        rows_kernel,
        [place, counts, latents, d_out, w_query, w_out],
        [shape((2, each, 2 * mine), BF16)] * 2,
        [pltpu.VMEM((own, width), BF16)] * 2
        + [pltpu.VMEM((width, width), BF16)] * 2
        + [pltpu.SemaphoreType.DMA((2, 5))],
        flops=4 * own * width * width,
        space=pltpu.HBM,
    )
    keep, send = call(
        slots_kernel,
        [place, points, w_key, w_value],
        [shape((2, slots, 2 * mine), BF16)] * 2,
        flops=4 * slots * width * width,
    )
    core_qg = swap(send_qg, 1)
    far_qg = swap(jnp.stack([keep_qg[1], core_qg[1]]), 2)
    core = swap(send, 1)
    far = swap(jnp.stack([keep[1], core[1]]), 2)
    blocks = [keep_qg[0], core_qg[0], far_qg[0], far_qg[1]]
    qg = jnp.concatenate([a[:own] for a in blocks], axis=0)
    tail = jnp.concatenate([a[own : own + 1] for a in blocks], axis=0).astype(F32)
    count = 16 * tail[:, :LANES] + tail[:, mine : mine + LANES]
    for mask in middle:
        qg = jnp.concatenate([qg, swap(qg, mask)], axis=0)
    qg = [qg, swap(qg, near_bit), swap(qg, far_bit)]
    turned = [shape((2, 2 * mine, slots), BF16)]
    (near_t,) = call(functools.partial(turn_kernel, ((0, 0), (1, 0))), [keep, core], turned)
    (far_t,) = call(functools.partial(turn_kernel, ((0, 0), (0, 1))), [far], turned)
    rows = qg[0].shape[0]
    team_slots = TEAM * slots
    work = 2 * rows * team_slots * mine

    numer, tops, stats = [None] * 4, [None] * 4, [None] * 4
    for p in range(4):
        if p == 2:
            qg[2], stats[0] = lax.optimization_barrier((qg[2], stats[0]))
            qg.append(swap(qg[2], near_bit))
        numer[p], tops[p], stats[p] = call(
            forward_kernel,
            [count, qg[p], keep, core, far, near_t, far_t],
            [shape((mine, rows), F32), shape((MINE, rows), F32), shape((2 * MINE, rows), F32)],
            [pltpu.VMEM((3, slots, rows), F32), pltpu.VMEM((3, slots, rows), BF16)],
            flops=8 * work,
            exps=rows * team_slots * MINE,
        )

    def merge(*parts):
        lse = [p[..., :MINE, :] for p in parts]
        top = functools.reduce(jnp.maximum, lse)
        scale = [jnp.exp(x - top) for x in lse]
        total = sum(scale)
        delta = sum(s * p[..., MINE:, :] for s, p in zip(scale, parts)) / total
        return jnp.concatenate([top + jnp.log(total), delta], axis=-2)

    stat = jnp.stack(stats)
    for mask, turn in ((near_bit, 1), (far_bit, 2)):
        came = swap(stat, mask)
        stat = merge(stat, jnp.stack([came[q ^ turn] for q in range(4)]))
    final = [stat[q] for q in range(4)]
    if middle:
        final = stat
        for mask in reversed(middle):
            half = final.shape[-1] // 2
            final = merge(final[..., :half], swap(final[..., half:], mask))
        for mask in middle:
            final = jnp.concatenate([final, swap(final, mask)], axis=-1)
        final = [final[q] for q in range(4)]

    def add(array, came):
        return array.astype(F32) + came.astype(F32)

    def scaled(p):
        scale = jnp.exp(tops[p] - final[p][:MINE])
        return (numer[p].reshape(MINE, -1, rows) * scale[:, None, :]).reshape(mine, rows)

    order = (3, 2, 1, 0)

    def backward(chunks, side, kind, sums=(), partial=(), last=False):
        kept = (2, slots, 2 * mine)
        return call(
            functools.partial(
                backward_kernel, len(chunks), order.index(chunks[0]), side, not sums, last
            ),
            [count]
            + [qg[p] for p in chunks]
            + [final[p] for p in chunks]
            + ([far, far, far_t] if side else [keep, core, near_t])
            + list(sums)
            + list(partial),
            [shape((len(chunks), mine, rows), kind), shape(kept, BF16 if last else F32)],
            [pltpu.VMEM(kept if len(chunks) > 1 else (1, 8, LANES), F32)]
            + [pltpu.VMEM((2, slots, rows), F32)] * 2
            + [pltpu.VMEM((2, slots, rows), BF16)] * 2,
            flops=7 * work * len(chunks),
            exps=rows * team_slots // 2 * MINE * len(chunks),
        )

    came_a = swap(jnp.stack([scaled(3), scaled(2)]).astype(BF16), far_bit)
    partial, gkv_far = backward(order, 1, F32, last=True)
    came_a, partial = lax.optimization_barrier((came_a, partial))
    came_far = swap(gkv_far, 2)
    near_a = swap(add(scaled(1), came_a[0]).astype(BF16), near_bit)
    gq, total = backward((3,), 0, BF16, partial=[partial])
    came = swap(gq[0], near_bit)
    gq, total = backward((2,), 0, F32, [total], [partial])
    sent, total = lax.optimization_barrier((add(gq[0], came).astype(BF16), total))
    far_q = swap(sent, far_bit)
    gq, total = backward((1,), 0, BF16, [total], [partial])
    near_q = swap(gq[0], near_bit)
    came_far, total = lax.optimization_barrier((came_far, total))
    gq, gkv_near = backward((0,), 0, F32, [total], [partial], True)
    attended = add(add(scaled(0), near_a), came_a[1])
    grad_query = add(add(gq[0], near_q), far_q)

    both = jnp.stack([attended, grad_query])
    for mask in reversed(middle):
        half = both.shape[-1] // 2
        both = add(both[..., :half], swap(both[..., half:].astype(BF16), mask))
    both, came_far = lax.optimization_barrier((both.astype(BF16), came_far))
    far_both = swap(both[..., 2 * own :], 2)
    near_both = both[..., : 2 * own]

    core_gkv = swap(jnp.stack([gkv_near[1], came_far[1]]), 1)
    (d_points,) = call(
        points_kernel,
        [place, gkv_near, came_far, core_gkv, w_key, w_value],
        [shape((slots, width), BF16)],
        [pltpu.VMEM((slots, width), BF16)] * 2,
        flops=4 * slots * width * width,
    )
    far_both, d_points = lax.optimization_barrier((far_both, d_points))
    core_both = swap(jnp.stack([near_both[..., own:], far_both[..., own:]]), 1)
    result, d_latents = call(
        queries_kernel,
        [place, near_both, far_both, core_both, latents, d_out, w_out, w_query],
        [shape((own, width), BF16)] * 2,
        [pltpu.VMEM((width, own), F32)],
        flops=4 * own * width * width,
    )
    return (result, d_latents, d_points)


def solution(mesh):
    part = P(("groups", "pts"), None)
    in_specs = (part, part, P(("groups", "pts")), P(), P(), P(), P(), part)
    return jax.shard_map(
        functools.partial(body, mesh.shape["pts"]),
        mesh=mesh,
        in_specs=in_specs,
        out_specs=(part, part, part),
        check_vma=False,
    )
```

```python
import functools

import jax
import jax.numpy as jnp
from jax import lax
from jax.experimental import pallas as pl
from jax.experimental.pallas import tpu as pltpu
from jax.sharding import PartitionSpec as P

HEADS = 12
TEAM = 4
MINE = HEADS // TEAM
BF16 = jnp.bfloat16
F32 = jnp.float32
LANES = 128
NT = (((1,), (1,)), ((), ()))


def dot(a, b):
    return jnp.dot(a, b, preferred_element_type=F32)


def dot_nt(a, b):
    return lax.dot_general(a, b, NT, preferred_element_type=F32)


def low_lanes(shape):
    return lax.broadcasted_iota(jnp.int32, shape, 1) < shape[1] // 2


def lanes_of(part):
    start = part // 2 * LANES
    return slice(start, start + LANES)


def keep_part(array, part):
    low = low_lanes(array.shape)
    return jnp.where(low if part % 2 == 0 else ~low, array, jnp.zeros_like(array))


def team_place(place_ref, quarter):
    relative = (place_ref[0] % TEAM) ^ quarter
    return relative % 2, relative // 2


def store_quarters(place_ref, keep_ref, send_ref, one, two, at):
    mine = one.shape[1] // TEAM
    for quarter in range(TEAM):
        cols = slice(quarter * mine, (quarter + 1) * mine)
        piece = jnp.concatenate([one[:, cols], two[:, cols]], axis=1)
        core, across = team_place(place_ref, quarter)
        for ref, which in ((keep_ref, 0), (send_ref, 1)):

            @pl.when(core == which)
            def _():
                ref[across, at, :] = piece


def load(source, target, sems, pieces):
    step = source.shape[0] // pieces
    copies = []
    for k in range(pieces):
        at = slice(k * step, (k + 1) * step)
        copies.append(pltpu.make_async_copy(source.at[at], target.at[at], sems.at[k]))
        copies[-1].start()
    return copies


def project_kernel(
    place_ref, count_ref, latents_hbm, d_out_hbm, points_hbm, w_query_hbm, w_out_hbm, w_key_hbm, w_value_hbm,
    keep_qg_ref, send_qg_ref, keep_ref, send_ref,
    latents_ref, d_out_ref, points_ref, w_query_ref, w_out_ref, w_key_ref, w_value_ref, sems
):
    pieces = sems.shape[1]
    own = latents_ref.shape[0]
    loads = [
        load(latents_hbm, latents_ref, sems.at[0], 1),
        load(w_query_hbm, w_query_ref, sems.at[1], pieces),
        load(d_out_hbm, d_out_ref, sems.at[2], 1),
        load(w_out_hbm, w_out_ref, sems.at[3], pieces),
        load(points_hbm, points_ref, sems.at[4], pieces),
        load(w_key_hbm, w_key_ref, sems.at[5], pieces),
        load(w_value_hbm, w_value_ref, sems.at[6], pieces),
    ]

    def arrived(*which):
        for i in which:
            for copy in loads[i]:
                copy.wait()

    extra = keep_qg_ref.shape[1] - own, keep_qg_ref.shape[2]
    first = lax.broadcasted_iota(jnp.int32, extra, 1) < extra[1] // 2
    count = jnp.where(first, count_ref[0] // 16, count_ref[0] % 16).astype(F32).astype(BF16)
    for ref in (keep_qg_ref, send_qg_ref):
        for across in range(2):
            ref[across, own:, :] = count
    arrived(0, 1)
    query = dot(latents_ref[...], w_query_ref[...]).astype(BF16)
    arrived(2, 3)
    grad = dot_nt(d_out_ref[...], w_out_ref[...]).astype(BF16)
    store_quarters(place_ref, keep_qg_ref, send_qg_ref, query, grad, slice(0, own))
    arrived(4, 5)
    keys = dot(points_ref[...], w_key_ref[...]).astype(BF16) * jnp.asarray(0.125, BF16)
    arrived(6)
    values = dot(points_ref[...], w_value_ref[...]).astype(BF16)
    store_quarters(place_ref, keep_ref, send_ref, keys, values, slice(0, keys.shape[0]))


def weights_kernel(w_key_ref, w_value_ref, out_ref):
    mine = out_ref.shape[1] // 2
    for i, ref in enumerate((w_key_ref, w_value_ref)):
        turned = ref[...].T
        for quarter in range(TEAM):
            out_ref[quarter, i * mine : (i + 1) * mine, :] = turned[quarter * mine : (quarter + 1) * mine]


def turn_kernel(picks, *refs):
    for i, (ref, which) in enumerate(picks):
        refs[-1][i] = refs[ref][which].T


def dead_slots(slot, count_ref, block):
    count = jnp.concatenate([count_ref[block : block + 1, :]] * (slot.shape[1] // LANES), axis=1)
    return slot >= count


def forward_kernel(
    count_ref, qg_ref, keep_ref, core_ref, far_ref, near_t_ref, far_t_ref,
    numer_ref, max_ref, stat_ref, score_ref, weight_ref
):
    rows = qg_ref.shape[0]
    slots = keep_ref.shape[1]
    dim = keep_ref.shape[2] // (2 * MINE)
    depth = score_ref.shape[0]
    kv_refs = [keep_ref.at[0], core_ref.at[0], far_ref.at[0], far_ref.at[1]]
    kv_t_refs = [near_t_ref.at[0], near_t_ref.at[1], far_t_ref.at[0], far_t_ref.at[1]]
    slot = lax.broadcasted_iota(jnp.int32, (slots, rows), 0).astype(F32)
    units = [(head, block) for head in range(MINE) for block in range(TEAM)]
    tops, totals, numers = {}, {}, {}

    def score(step):
        head, block = units[step]
        keys = keep_part(kv_refs[block][:, lanes_of(head)], head)
        score_ref[step % depth] = dot_nt(keys, qg_ref[:, lanes_of(head)])

    def weigh(step):
        dead = dead_slots(slot, count_ref, units[step][1])
        scores = jnp.where(dead, -jnp.inf, score_ref[step % depth])
        tops[step] = jnp.max(scores, axis=0, keepdims=True)
        weights = jnp.exp(scores - tops[step])
        totals[step] = jnp.sum(weights, axis=0, keepdims=True)
        weight_ref[step % depth] = weights.astype(BF16)

    def attend(step):
        head, block = units[step]
        part = MINE + head
        at = slice(part * dim, (part + 1) * dim)
        numers[step] = dot(kv_t_refs[block][at, :], weight_ref[step % depth])
        if block < TEAM - 1:
            return
        steps = range(step - TEAM + 1, step + 1)
        top = functools.reduce(jnp.maximum, [tops[s] for s in steps])
        scale = {s: jnp.exp(tops[s] - top) for s in steps}
        total = sum(scale[s] * totals[s] for s in steps)
        numer = sum(scale[s] * numers[s] for s in steps)
        numer_ref[head * dim : (head + 1) * dim, :] = numer
        half = part % 2 * dim
        grad_t = qg_ref[:, lanes_of(part)].astype(F32).T[half : half + dim, :]
        inner = jnp.sum(grad_t * numer, axis=0, keepdims=True)
        max_ref[head : head + 1, :] = top
        stat_ref[head : head + 1, :] = top + jnp.log(total)
        stat_ref[MINE + head : MINE + head + 1, :] = inner / total

    for step in range(len(units) + 2):
        if step < len(units):
            score(step)
        if 0 <= step - 1 < len(units):
            weigh(step - 1)
        if 0 <= step - 2:
            attend(step - 2)


def backward_kernel(chunks, start, side, first, last, count_ref, *refs):
    qg_refs, stat_refs, refs = refs[:chunks], refs[chunks : 2 * chunks], refs[2 * chunks :]
    even_ref, odd_ref, kv_t_ref, *refs = refs
    kv_refs = even_ref.at[0], odd_ref.at[side]
    if not first:
        sum_in_ref, *refs = refs
    gq_in_ref = None
    if side == 0:
        gq_in_ref, *refs = refs
    gq_ref, sum_ref, total_ref, score_ref, gw_ref, prob_ref, ds_ref = refs
    rows = qg_refs[0].shape[0]
    slots, dim = even_ref.shape[1], even_ref.shape[2] // (2 * MINE)
    depth = score_ref.shape[0]
    slot = lax.broadcasted_iota(jnp.int32, (slots, rows), 0).astype(F32)
    low = low_lanes((slots, LANES))
    units = [(c, head, block) for c in range(chunks) for block in range(2) for head in range(MINE)]
    gq, held = {}, {}

    def product(chunk, block, part):
        return dot_nt(keep_part(kv_refs[block][:, lanes_of(part)], part), qg_refs[chunk][:, lanes_of(part)])

    def score(step):
        chunk, head, block = units[step]
        score_ref[step % depth] = product(chunk, block, head)
        gw_ref[step % depth] = product(chunk, block, MINE + head)

    def weigh(step):
        chunk, head, block = units[step]
        dead = dead_slots(slot, count_ref, 2 * side + block)
        scores = jnp.where(dead, -jnp.inf, score_ref[step % depth])
        prob = jnp.exp(scores - stat_refs[chunk][head : head + 1, :])
        delta = stat_refs[chunk][MINE + head : MINE + head + 1, :]
        prob_ref[step % depth] = prob.astype(BF16)
        ds_ref[step % depth] = (prob * (gw_ref[step % depth] - delta)).astype(BF16)

    def store(chunk, block, part, value):
        held[part] = value
        pair = part // 2 * 2, part // 2 * 2 + 1
        if not all(p in held for p in pair):
            return
        at = block, slice(0, slots), lanes_of(part)
        total = jnp.where(low, held.pop(pair[0]), held.pop(pair[1]))
        if chunk > 0:
            total += total_ref[at]
        elif not first:
            total += sum_in_ref[at]
        if chunk < chunks - 1:
            total_ref[at] = total
            return
        if last:
            scales = [0.125 if p < MINE else 1.0 for p in pair]
            total *= scales[0] if scales[0] == scales[1] else jnp.where(low, *scales)
        sum_ref[at] = total.astype(sum_ref.dtype)

    def collect(step):
        chunk, head, block = units[step]
        qg_ref = qg_refs[chunk]
        store(chunk, block, head, dot(ds_ref[step % depth], qg_ref[:, lanes_of(head)]))
        store(chunk, block, MINE + head, dot(prob_ref[step % depth], qg_ref[:, lanes_of(MINE + head)]))
        at = slice(head * dim, (head + 1) * dim)
        term = dot(kv_t_ref[block, at, :], ds_ref[step % depth])
        if block == 0:
            gq[head] = term if gq_in_ref is None else term + gq_in_ref[start + chunk, at, :]
        else:
            gq_ref[chunk, at, :] = (gq[head] + term).astype(gq_ref.dtype)

    for step in range(len(units) + 2):
        if 0 <= step - 2:
            collect(step - 2)
        if 0 <= step - 1 < len(units):
            weigh(step - 1)
        if step < len(units):
            score(step)


def queries_kernel(
    place_ref, near_ref, far_ref, core_ref, latents_ref, d_out_ref, w_out_ref, w_query_ref,
    result_ref, d_latents_ref, joined_ref
):
    own = latents_ref.shape[0]
    mine = near_ref.shape[1]
    for kind in range(2):
        for relative in range(TEAM):
            core, across = relative % 2, relative // 2
            quarter = (place_ref[0] % TEAM) ^ relative
            piece = core_ref[across, kind] if core else (near_ref, far_ref)[across][kind, :, :own]
            joined_ref[pl.ds(pl.multiple_of(quarter * mine, mine), mine), :] = piece.astype(F32)
        joined = joined_ref[...].T.astype(BF16)
        if kind == 0:
            result_ref[...] = (latents_ref[...].astype(F32) + dot(joined, w_out_ref[...])).astype(BF16)
        else:
            d_latents_ref[...] = (
                d_out_ref[...].astype(F32) + dot_nt(joined, w_query_ref[...])
            ).astype(BF16)


def points_kernel(place_ref, near_ref, far_ref, core_ref, weight_ref, out_ref):
    total = None
    for relative in range(TEAM):
        core, across = relative % 2, relative // 2
        piece = core_ref[across] if core else (near_ref, far_ref)[across][0]
        term = dot(piece, weight_ref[(place_ref[0] % TEAM) ^ relative])
        total = term if total is None else total + term
    out_ref[...] = total.astype(BF16)


def call(kernel, ins, out_shapes, scratch=(), flops=0, exps=0, space=pltpu.VMEM, grant=40):
    vmem = pl.BlockSpec(memory_space=pltpu.VMEM)
    other = pl.BlockSpec(memory_space=space)
    smem = pl.BlockSpec(memory_space=pltpu.SMEM)
    moved = sum(a.size * a.dtype.itemsize for a in list(ins) + list(out_shapes))
    return pl.pallas_call(
        kernel,
        in_specs=[smem if a.dtype == jnp.int32 else other for a in ins],
        out_specs=[vmem] * len(out_shapes),
        out_shape=out_shapes,
        scratch_shapes=scratch,
        compiler_params=pltpu.CompilerParams(vmem_limit_bytes=grant << 20),
        cost_estimate=pl.CostEstimate(flops=flops // 8, transcendentals=exps // 8, bytes_accessed=moved // 8),
    )(*ins)


def body(size, latents, points, counts, w_query, w_key, w_value, w_out, d_out):
    own, width = latents.shape
    slots = points.shape[0]
    mine = width // TEAM
    shape = jax.ShapeDtypeStruct
    near_bit, far_bit = size // 4, size // 2
    middle = []
    bit = size // 8
    while bit >= TEAM:
        middle.append(bit)
        bit //= 2
    place = lax.axis_index("pts").astype(jnp.int32).reshape(1)

    def swap(array, mask):
        return lax.ppermute(array, "pts", [(i, i ^ mask) for i in range(size)])

    each = own + 16
    inputs = [latents, d_out, points, w_query, w_out, w_key, w_value]
    keep_qg, send_qg, keep, send = call(
        project_kernel,
        [place, counts] + inputs,
        [shape((2, each, 2 * mine), BF16)] * 2 + [shape((2, slots, 2 * mine), BF16)] * 2,
        [pltpu.VMEM(a.shape, BF16) for a in inputs] + [pltpu.SemaphoreType.DMA((len(inputs), 4))],
        flops=4 * (own + slots) * width * width,
        space=pltpu.HBM,
        grant=60,
    )
    core_qg = swap(send_qg, 1)
    far_qg = swap(jnp.stack([keep_qg[1], core_qg[1]]), 2)
    core = swap(send, 1)
    far = swap(jnp.stack([keep[1], core[1]]), 2)
    blocks = [keep_qg[0], core_qg[0], far_qg[0], far_qg[1]]
    qg = jnp.concatenate([a[:own] for a in blocks], axis=0)
    tail = jnp.concatenate([a[own : own + 1] for a in blocks], axis=0).astype(F32)
    count = 16 * tail[:, :LANES] + tail[:, mine : mine + LANES]
    for mask in middle:
        qg = jnp.concatenate([qg, swap(qg, mask)], axis=0)
    qg, w_key, w_value = lax.optimization_barrier((qg, w_key, w_value))
    far_qg = swap(qg, far_bit)
    qg = [qg, swap(qg, near_bit), far_qg]
    (weights,) = call(weights_kernel, [w_key, w_value], [shape((TEAM, 2 * mine, width), BF16)])
    turned = [shape((2, 2 * mine, slots), BF16)]
    (near_t,) = call(functools.partial(turn_kernel, ((0, 0), (1, 0))), [keep, core], turned)
    near_t, weights = lax.optimization_barrier((near_t, weights))
    (far_t,) = call(functools.partial(turn_kernel, ((0, 0), (0, 1))), [far], turned)
    rows = qg[0].shape[0]
    team_slots = TEAM * slots
    work = 2 * rows * team_slots * mine

    numer, tops, stats = [None] * 4, [None] * 4, [None] * 4
    for p in range(4):
        if p == 2:
            qg[2], stats[0] = lax.optimization_barrier((qg[2], stats[0]))
            qg.append(swap(qg[2], near_bit))
        numer[p], tops[p], stats[p] = call(
            forward_kernel,
            [count, qg[p], keep, core, far, near_t, far_t],
            [shape((mine, rows), F32), shape((MINE, rows), F32), shape((2 * MINE, rows), F32)],
            [pltpu.VMEM((3, slots, rows), F32), pltpu.VMEM((3, slots, rows), BF16)],
            flops=8 * work,
            exps=rows * team_slots * MINE,
        )

    def merge(*parts):
        lse = [p[..., :MINE, :] for p in parts]
        top = functools.reduce(jnp.maximum, lse)
        scale = [jnp.exp(x - top) for x in lse]
        total = sum(scale)
        delta = sum(s * p[..., MINE:, :] for s, p in zip(scale, parts)) / total
        return jnp.concatenate([top + jnp.log(total), delta], axis=-2)

    stat = jnp.stack(stats)
    for mask, turn in ((near_bit, 1), (far_bit, 2)):
        came = swap(stat, mask)
        stat = merge(stat, jnp.stack([came[q ^ turn] for q in range(4)]))
    final = [stat[q] for q in range(4)]
    if middle:
        final = stat
        for mask in reversed(middle):
            half = final.shape[-1] // 2
            final = merge(final[..., :half], swap(final[..., half:], mask))
        for mask in middle:
            final = jnp.concatenate([final, swap(final, mask)], axis=-1)
        final = [final[q] for q in range(4)]

    def add(array, came):
        return array.astype(F32) + came.astype(F32)

    def scaled(p):
        scale = jnp.exp(tops[p] - final[p][:MINE])
        return (numer[p].reshape(MINE, -1, rows) * scale[:, None, :]).reshape(mine, rows)

    order = (3, 2, 1, 0)

    def backward(chunks, side, kind, sums=(), partial=(), last=False):
        kept = (2, slots, 2 * mine)
        return call(
            functools.partial(
                backward_kernel, len(chunks), order.index(chunks[0]), side, not sums, last
            ),
            [count]
            + [qg[p] for p in chunks]
            + [final[p] for p in chunks]
            + ([far, far, far_t] if side else [keep, core, near_t])
            + list(sums)
            + list(partial),
            [shape((len(chunks), mine, rows), kind), shape(kept, BF16 if last else F32)],
            [pltpu.VMEM(kept if len(chunks) > 1 else (1, 8, LANES), F32)]
            + [pltpu.VMEM((2, slots, rows), F32)] * 2
            + [pltpu.VMEM((2, slots, rows), BF16)] * 2,
            flops=7 * work * len(chunks),
            exps=rows * team_slots // 2 * MINE * len(chunks),
        )

    came_a = swap(jnp.stack([scaled(3), scaled(2)]).astype(BF16), far_bit)
    partial, gkv_far = backward(order, 1, F32, last=True)
    came_a, partial = lax.optimization_barrier((came_a, partial))
    came_far = swap(gkv_far, 2)
    near_a = swap(add(scaled(1), came_a[0]).astype(BF16), near_bit)
    gq, total = backward((3,), 0, BF16, partial=[partial])
    came = swap(gq[0], near_bit)
    gq, total = backward((2,), 0, F32, [total], [partial])
    sent, total = lax.optimization_barrier((add(gq[0], came).astype(BF16), total))
    far_q = swap(sent, far_bit)
    gq, total = backward((1,), 0, BF16, [total], [partial])
    near_q = swap(gq[0], near_bit)
    came_far, total = lax.optimization_barrier((came_far, total))
    gq, gkv_near = backward((0,), 0, F32, [total], [partial], True)
    attended = add(add(scaled(0), near_a), came_a[1])
    grad_query = add(add(gq[0], near_q), far_q)

    both = jnp.stack([attended, grad_query])
    for mask in reversed(middle):
        half = both.shape[-1] // 2
        both = add(both[..., :half], swap(both[..., half:].astype(BF16), mask))
    both, came_far = lax.optimization_barrier((both.astype(BF16), came_far))
    far_both = swap(both[..., 2 * own :], 2)
    near_both = both[..., : 2 * own]

    core_gkv = swap(jnp.stack([gkv_near[1], came_far[1]]), 1)
    (d_points,) = call(
        points_kernel,
        [place, gkv_near, came_far, core_gkv, weights],
        [shape((slots, width), BF16)],
        flops=4 * slots * width * width,
    )
    far_both, d_points = lax.optimization_barrier((far_both, d_points))
    core_both = swap(jnp.stack([near_both[..., own:], far_both[..., own:]]), 1)
    result, d_latents = call(
        queries_kernel,
        [place, near_both, far_both, core_both, latents, d_out, w_out, w_query],
        [shape((own, width), BF16)] * 2,
        [pltpu.VMEM((width, own), F32)],
        flops=4 * own * width * width,
    )
    return (result, d_latents, d_points)


def solution(mesh):
    part = P(("groups", "pts"), None)
    in_specs = (part, part, P(("groups", "pts")), P(), P(), P(), P(), part)
    return jax.shard_map(
        functools.partial(body, mesh.shape["pts"]),
        mesh=mesh,
        in_specs=in_specs,
        out_specs=(part, part, part),
        check_vma=False,
    )
```

```python
import functools

import jax
import jax.numpy as jnp
from jax import lax
from jax.experimental import pallas as pl
from jax.experimental.pallas import tpu as pltpu
from jax.sharding import PartitionSpec as P

HEADS = 12
TEAM = 4
MINE = HEADS // TEAM
BF16 = jnp.bfloat16
F32 = jnp.float32
LANES = 128
NT = (((1,), (1,)), ((), ()))


def dot(a, b):
    return jnp.dot(a, b, preferred_element_type=F32)


def dot_nt(a, b):
    return lax.dot_general(a, b, NT, preferred_element_type=F32)


def low_lanes(shape):
    return lax.broadcasted_iota(jnp.int32, shape, 1) < shape[1] // 2


def lanes_of(part):
    start = part // 2 * LANES
    return slice(start, start + LANES)


def keep_part(array, part):
    low = low_lanes(array.shape)
    return jnp.where(low if part % 2 == 0 else ~low, array, jnp.zeros_like(array))


def team_place(place_ref, quarter):
    relative = (place_ref[0] % TEAM) ^ quarter
    return relative % 2, relative // 2


def store_quarters(place_ref, keep_ref, send_ref, one, two, at):
    mine = one.shape[1] // TEAM
    for quarter in range(TEAM):
        cols = slice(quarter * mine, (quarter + 1) * mine)
        piece = jnp.concatenate([one[:, cols], two[:, cols]], axis=1)
        core, across = team_place(place_ref, quarter)
        for ref, which in ((keep_ref, 0), (send_ref, 1)):

            @pl.when(core == which)
            def _():
                ref[across, at, :] = piece


def load(source, target, sems, pieces):
    step = source.shape[0] // pieces
    copies = []
    for k in range(pieces):
        at = slice(k * step, (k + 1) * step)
        copies.append(pltpu.make_async_copy(source.at[at], target.at[at], sems.at[k]))
        copies[-1].start()
    return copies


def project_kernel(
    place_ref, count_ref, latents_hbm, d_out_hbm, points_hbm, w_query_hbm, w_out_hbm, w_key_hbm, w_value_hbm,
    keep_qg_ref, send_qg_ref, keep_ref, send_ref,
    latents_ref, d_out_ref, points_ref, w_query_ref, w_out_ref, w_key_ref, w_value_ref, sems
):
    pieces = sems.shape[1]
    own = latents_ref.shape[0]
    loads = [
        load(latents_hbm, latents_ref, sems.at[0], 1),
        load(w_query_hbm, w_query_ref, sems.at[1], pieces),
        load(d_out_hbm, d_out_ref, sems.at[2], 1),
        load(w_out_hbm, w_out_ref, sems.at[3], pieces),
        load(points_hbm, points_ref, sems.at[4], pieces),
        load(w_key_hbm, w_key_ref, sems.at[5], pieces),
        load(w_value_hbm, w_value_ref, sems.at[6], pieces),
    ]

    def arrived(*which):
        for i in which:
            for copy in loads[i]:
                copy.wait()

    extra = keep_qg_ref.shape[1] - own, keep_qg_ref.shape[2]
    first = lax.broadcasted_iota(jnp.int32, extra, 1) < extra[1] // 2
    count = jnp.where(first, count_ref[0] // 16, count_ref[0] % 16).astype(F32).astype(BF16)
    for ref in (keep_qg_ref, send_qg_ref):
        for across in range(2):
            ref[across, own:, :] = count
    arrived(0, 1)
    query = dot(latents_ref[...], w_query_ref[...]).astype(BF16)
    arrived(2, 3)
    grad = dot_nt(d_out_ref[...], w_out_ref[...]).astype(BF16)
    store_quarters(place_ref, keep_qg_ref, send_qg_ref, query, grad, slice(0, own))
    arrived(4, 5)
    keys = dot(points_ref[...], w_key_ref[...]).astype(BF16) * jnp.asarray(0.125, BF16)
    arrived(6)
    values = dot(points_ref[...], w_value_ref[...]).astype(BF16)
    store_quarters(place_ref, keep_ref, send_ref, keys, values, slice(0, keys.shape[0]))


def weights_kernel(w_key_ref, w_value_ref, out_ref):
    mine = out_ref.shape[1] // 2
    for i, ref in enumerate((w_key_ref, w_value_ref)):
        turned = ref[...].T
        for quarter in range(TEAM):
            out_ref[quarter, i * mine : (i + 1) * mine, :] = turned[quarter * mine : (quarter + 1) * mine]


def pair_kernel(keep_ref, core_ref, out_ref):
    out_ref[0] = keep_ref[1]
    out_ref[1] = core_ref[1]


def chunk_kernel(keep_ref, core_ref, far_ref, out_ref, count_ref):
    own, mine = out_ref.shape[0] // TEAM, out_ref.shape[1] // 2
    blocks = keep_ref.at[0], core_ref.at[0], far_ref.at[0], far_ref.at[1]
    for i, ref in enumerate(blocks):
        out_ref[i * own : (i + 1) * own, :] = ref[:own, :]
        row = ref[own:, :].astype(F32)[:1, :]
        count_ref[i : i + 1, :] = 16 * row[:, :LANES] + row[:, mine : mine + LANES]


def turn_kernel(picks, *refs):
    for i, (ref, which) in enumerate(picks):
        refs[-1][i] = refs[ref][which].T


def dead_slots(slot, count_ref, block):
    count = jnp.concatenate([count_ref[block : block + 1, :]] * (slot.shape[1] // LANES), axis=1)
    return slot >= count


def forward_kernel(blocks, count_ref, qg_ref, *refs):
    kv_refs, kv_t_refs = {}, {}
    if 0 in blocks:
        keep_ref, core_ref, near_t_ref, *refs = refs
        kv_refs.update({0: keep_ref.at[0], 1: core_ref.at[0]})
        kv_t_refs.update({0: near_t_ref.at[0], 1: near_t_ref.at[1]})
    if 2 in blocks:
        far_ref, far_t_ref, *refs = refs
        kv_refs.update({2: far_ref.at[0], 3: far_ref.at[1]})
        kv_t_refs.update({2: far_t_ref.at[0], 3: far_t_ref.at[1]})
    before = refs[:2] if blocks[0] else ()
    numer_ref, stat_ref, score_ref, weight_ref = refs[len(before) :]
    rows = qg_ref.shape[0]
    slots = kv_refs[blocks[0]].shape[0]
    dim = qg_ref.shape[1] // (2 * MINE)
    depth = score_ref.shape[0]
    slot = lax.broadcasted_iota(jnp.int32, (slots, rows), 0).astype(F32)
    units = [(head, block) for head in range(MINE) for block in blocks]
    tops, totals, numers = {}, {}, {}

    def score(step):
        head, block = units[step]
        keys = keep_part(kv_refs[block][:, lanes_of(head)], head)
        score_ref[step % depth] = dot_nt(keys, qg_ref[:, lanes_of(head)])

    def weigh(step):
        dead = dead_slots(slot, count_ref, units[step][1])
        scores = jnp.where(dead, -jnp.inf, score_ref[step % depth])
        tops[step] = jnp.max(scores, axis=0, keepdims=True)
        weights = jnp.exp(scores - tops[step])
        totals[step] = jnp.sum(weights, axis=0, keepdims=True)
        weight_ref[step % depth] = weights.astype(BF16)

    def attend(step):
        head, block = units[step]
        part = MINE + head
        at = slice(part * dim, (part + 1) * dim)
        numers[step] = dot(kv_t_refs[block][at, :], weight_ref[step % depth])
        if block != blocks[-1]:
            return
        steps = list(range(step - len(blocks) + 1, step + 1))
        own_rows = slice(head * dim, (head + 1) * dim)
        if before:
            steps.append(-1)
            numers[-1] = before[0][own_rows, :]
            tops[-1] = before[1][head : head + 1, :]
            totals[-1] = before[1][MINE + head : MINE + head + 1, :]
        top = functools.reduce(jnp.maximum, [tops[s] for s in steps])
        scale = {s: jnp.exp(tops[s] - top) for s in steps}
        total = sum(scale[s] * totals[s] for s in steps)
        numer = sum(scale[s] * numers[s] for s in steps)
        numer_ref[own_rows, :] = numer
        half = part % 2 * dim
        grad_t = qg_ref[:, lanes_of(part)].astype(F32).T[half : half + dim, :]
        inner = jnp.sum(grad_t * numer, axis=0, keepdims=True)
        for i, row in enumerate((top, total, top + jnp.log(total), inner / total)):
            stat_ref[i * MINE + head : i * MINE + head + 1, :] = row

    for step in range(len(units) + 2):
        if step < len(units):
            score(step)
        if 0 <= step - 1 < len(units):
            weigh(step - 1)
        if 0 <= step - 2:
            attend(step - 2)


def backward_kernel(chunks, start, side, first, last, count_ref, *refs):
    qg_refs, stat_refs, refs = refs[:chunks], refs[chunks : 2 * chunks], refs[2 * chunks :]
    even_ref, odd_ref, kv_t_ref, *refs = refs
    kv_refs = even_ref.at[0], odd_ref.at[side]
    if not first:
        sum_in_ref, *refs = refs
    gq_in_ref = None
    if side == 0:
        gq_in_ref, *refs = refs
    gq_ref, sum_ref, total_ref, score_ref, gw_ref, prob_ref, ds_ref = refs
    rows = qg_refs[0].shape[0]
    slots, dim = even_ref.shape[1], even_ref.shape[2] // (2 * MINE)
    depth = score_ref.shape[0]
    slot = lax.broadcasted_iota(jnp.int32, (slots, rows), 0).astype(F32)
    low = low_lanes((slots, LANES))
    units = [(c, head, block) for c in range(chunks) for block in range(2) for head in range(MINE)]
    gq, held = {}, {}

    def product(chunk, block, part):
        return dot_nt(keep_part(kv_refs[block][:, lanes_of(part)], part), qg_refs[chunk][:, lanes_of(part)])

    def score(step):
        chunk, head, block = units[step]
        score_ref[step % depth] = product(chunk, block, head)
        gw_ref[step % depth] = product(chunk, block, MINE + head)

    def weigh(step):
        chunk, head, block = units[step]
        dead = dead_slots(slot, count_ref, 2 * side + block)
        scores = jnp.where(dead, -jnp.inf, score_ref[step % depth])
        prob = jnp.exp(scores - stat_refs[chunk][head : head + 1, :])
        delta = stat_refs[chunk][MINE + head : MINE + head + 1, :]
        prob_ref[step % depth] = prob.astype(BF16)
        ds_ref[step % depth] = (prob * (gw_ref[step % depth] - delta)).astype(BF16)

    def store(chunk, block, part, value):
        held[part] = value
        pair = part // 2 * 2, part // 2 * 2 + 1
        if not all(p in held for p in pair):
            return
        at = block, slice(0, slots), lanes_of(part)
        total = jnp.where(low, held.pop(pair[0]), held.pop(pair[1]))
        if chunk > 0:
            total += total_ref[at]
        elif not first:
            total += sum_in_ref[at]
        if chunk < chunks - 1:
            total_ref[at] = total
            return
        if last:
            scales = [0.125 if p < MINE else 1.0 for p in pair]
            total *= scales[0] if scales[0] == scales[1] else jnp.where(low, *scales)
        sum_ref[at] = total.astype(sum_ref.dtype)

    def collect(step):
        chunk, head, block = units[step]
        qg_ref = qg_refs[chunk]
        store(chunk, block, head, dot(ds_ref[step % depth], qg_ref[:, lanes_of(head)]))
        store(chunk, block, MINE + head, dot(prob_ref[step % depth], qg_ref[:, lanes_of(MINE + head)]))
        at = slice(head * dim, (head + 1) * dim)
        term = dot(kv_t_ref[block, at, :], ds_ref[step % depth])
        if block == 0:
            gq[head] = term if gq_in_ref is None else term + gq_in_ref[start + chunk, at, :]
        else:
            gq_ref[chunk, at, :] = (gq[head] + term).astype(gq_ref.dtype)

    for step in range(len(units) + 2):
        if 0 <= step - 2:
            collect(step - 2)
        if 0 <= step - 1 < len(units):
            weigh(step - 1)
        if step < len(units):
            score(step)


def queries_kernel(
    place_ref, near_ref, far_ref, core_ref, latents_ref, d_out_ref, w_out_ref, w_query_ref,
    result_ref, d_latents_ref, joined_ref
):
    own = latents_ref.shape[0]
    mine = near_ref.shape[1]
    for kind in range(2):
        for relative in range(TEAM):
            core, across = relative % 2, relative // 2
            quarter = (place_ref[0] % TEAM) ^ relative
            piece = core_ref[across, kind] if core else (near_ref, far_ref)[across][kind, :, :own]
            joined_ref[pl.ds(pl.multiple_of(quarter * mine, mine), mine), :] = piece.astype(F32)
        joined = joined_ref[...].T.astype(BF16)
        if kind == 0:
            result_ref[...] = (latents_ref[...].astype(F32) + dot(joined, w_out_ref[...])).astype(BF16)
        else:
            d_latents_ref[...] = (
                d_out_ref[...].astype(F32) + dot_nt(joined, w_query_ref[...])
            ).astype(BF16)


def points_kernel(place_ref, near_ref, far_ref, core_ref, weight_ref, out_ref):
    total = None
    for relative in range(TEAM):
        core, across = relative % 2, relative // 2
        piece = core_ref[across] if core else (near_ref, far_ref)[across][0]
        term = dot(piece, weight_ref[(place_ref[0] % TEAM) ^ relative])
        total = term if total is None else total + term
    out_ref[...] = total.astype(BF16)


def call(kernel, ins, out_shapes, scratch=(), flops=0, exps=0, space=pltpu.VMEM, grant=40):
    vmem = pl.BlockSpec(memory_space=pltpu.VMEM)
    other = pl.BlockSpec(memory_space=space)
    smem = pl.BlockSpec(memory_space=pltpu.SMEM)
    moved = sum(a.size * a.dtype.itemsize for a in list(ins) + list(out_shapes))
    return pl.pallas_call(
        kernel,
        in_specs=[smem if a.dtype == jnp.int32 else other for a in ins],
        out_specs=[vmem] * len(out_shapes),
        out_shape=out_shapes,
        scratch_shapes=scratch,
        compiler_params=pltpu.CompilerParams(vmem_limit_bytes=grant << 20),
        cost_estimate=pl.CostEstimate(flops=flops // 8, transcendentals=exps // 8, bytes_accessed=moved // 8),
    )(*ins)


def body(size, latents, points, counts, w_query, w_key, w_value, w_out, d_out):
    own, width = latents.shape
    slots = points.shape[0]
    mine = width // TEAM
    shape = jax.ShapeDtypeStruct
    near_bit, far_bit = size // 4, size // 2
    middle = []
    bit = size // 8
    while bit >= TEAM:
        middle.append(bit)
        bit //= 2
    place = lax.axis_index("pts").astype(jnp.int32).reshape(1)

    def swap(array, mask):
        return lax.ppermute(array, "pts", [(i, i ^ mask) for i in range(size)])

    each = own + 16
    inputs = [latents, d_out, points, w_query, w_out, w_key, w_value]
    keep_qg, send_qg, keep, send = call(
        project_kernel,
        [place, counts] + inputs,
        [shape((2, each, 2 * mine), BF16)] * 2 + [shape((2, slots, 2 * mine), BF16)] * 2,
        [pltpu.VMEM(a.shape, BF16) for a in inputs] + [pltpu.SemaphoreType.DMA((len(inputs), 4))],
        flops=4 * (own + slots) * width * width,
        space=pltpu.HBM,
        grant=60,
    )
    core_qg = swap(send_qg, 1)
    core = swap(send, 1)
    (far_qg,) = call(pair_kernel, [keep_qg, core_qg], [shape(keep_qg.shape, BF16)])
    far_qg, core = lax.optimization_barrier((far_qg, core))
    far_qg = swap(far_qg, 2)
    far = swap(call(pair_kernel, [keep, core], [shape(keep.shape, BF16)])[0], 2)
    qg, count = call(
        chunk_kernel,
        [keep_qg, core_qg, far_qg],
        [shape((TEAM * own, 2 * mine), BF16), shape((TEAM, LANES), F32)],
    )
    for mask in middle:
        qg = jnp.concatenate([qg, swap(qg, mask)], axis=0)
    qg, w_key, w_value = lax.optimization_barrier((qg, w_key, w_value))
    far_qg = swap(qg, far_bit)
    qg = [qg, swap(qg, near_bit), far_qg]
    (weights,) = call(weights_kernel, [w_key, w_value], [shape((TEAM, 2 * mine, width), BF16)])
    turned = [shape((2, 2 * mine, slots), BF16)]
    (near_t,) = call(functools.partial(turn_kernel, ((0, 0), (1, 0))), [keep, core], turned)
    near_t, weights = lax.optimization_barrier((near_t, weights))
    rows = qg[0].shape[0]
    team_slots = TEAM * slots
    work = 2 * rows * team_slots * mine

    def forward(p, blocks, before=()):
        return call(
            functools.partial(forward_kernel, blocks),
            [count, qg[p]]
            + ([keep, core, near_t] if 0 in blocks else [])
            + ([far, far_t] if 2 in blocks else [])
            + list(before),
            [shape((mine, rows), F32), shape((4 * MINE, rows), F32)],
            [pltpu.VMEM((3, slots, rows), F32), pltpu.VMEM((3, slots, rows), BF16)],
            flops=2 * work * len(blocks),
            exps=rows * slots * len(blocks) * MINE,
        )

    early = [forward(p, (0, 1)) for p in range(2)]
    (early, far) = lax.optimization_barrier((early, far))
    (far_t,) = call(functools.partial(turn_kernel, ((0, 0), (0, 1))), [far], turned)
    done = [forward(p, (2, 3), early[p]) for p in range(2)]
    qg[2], done[0] = lax.optimization_barrier((qg[2], done[0]))
    qg.append(swap(qg[2], near_bit))
    done += [forward(p, (0, 1, 2, 3)) for p in (2, 3)]
    numer = [d[0] for d in done]
    tops = [d[1][:MINE] for d in done]
    stats = [d[1][2 * MINE :] for d in done]

    def merge(*parts):
        lse = [p[..., :MINE, :] for p in parts]
        top = functools.reduce(jnp.maximum, lse)
        scale = [jnp.exp(x - top) for x in lse]
        total = sum(scale)
        delta = sum(s * p[..., MINE:, :] for s, p in zip(scale, parts)) / total
        return jnp.concatenate([top + jnp.log(total), delta], axis=-2)

    stat = jnp.stack(stats)
    for mask, turn in ((near_bit, 1), (far_bit, 2)):
        came = swap(stat, mask)
        stat = merge(stat, jnp.stack([came[q ^ turn] for q in range(4)]))
    final = [stat[q] for q in range(4)]
    if middle:
        final = stat
        for mask in reversed(middle):
            half = final.shape[-1] // 2
            final = merge(final[..., :half], swap(final[..., half:], mask))
        for mask in middle:
            final = jnp.concatenate([final, swap(final, mask)], axis=-1)
        final = [final[q] for q in range(4)]

    def add(array, came):
        return array.astype(F32) + came.astype(F32)

    def scaled(p):
        scale = jnp.exp(tops[p] - final[p][:MINE])
        return (numer[p].reshape(MINE, -1, rows) * scale[:, None, :]).reshape(mine, rows)

    order = (3, 2, 1, 0)

    def backward(chunks, side, kind, sums=(), partial=(), last=False):
        kept = (2, slots, 2 * mine)
        return call(
            functools.partial(
                backward_kernel, len(chunks), order.index(chunks[0]), side, not sums, last
            ),
            [count]
            + [qg[p] for p in chunks]
            + [final[p] for p in chunks]
            + ([far, far, far_t] if side else [keep, core, near_t])
            + list(sums)
            + list(partial),
            [shape((len(chunks), mine, rows), kind), shape(kept, BF16 if last else F32)],
            [pltpu.VMEM(kept if len(chunks) > 1 else (1, 8, LANES), F32)]
            + [pltpu.VMEM((2, slots, rows), F32)] * 2
            + [pltpu.VMEM((2, slots, rows), BF16)] * 2,
            flops=7 * work * len(chunks),
            exps=rows * team_slots // 2 * MINE * len(chunks),
        )

    came_a = swap(jnp.stack([scaled(3), scaled(2)]).astype(BF16), far_bit)
    partial, gkv_far = backward(order, 1, F32, last=True)
    came_a, partial = lax.optimization_barrier((came_a, partial))
    came_far = swap(gkv_far, 2)
    near_a = swap(add(scaled(1), came_a[0]).astype(BF16), near_bit)
    gq, total = backward((3,), 0, BF16, partial=[partial])
    came = swap(gq[0], near_bit)
    gq, total = backward((2,), 0, F32, [total], [partial])
    sent, total = lax.optimization_barrier((add(gq[0], came).astype(BF16), total))
    far_q = swap(sent, far_bit)
    gq, total = backward((1,), 0, BF16, [total], [partial])
    near_q = swap(gq[0], near_bit)
    came_far, far_q, total = lax.optimization_barrier((came_far, far_q, total))
    gq, gkv_near = backward((0,), 0, F32, [total], [partial], True)
    attended = add(add(scaled(0), near_a), came_a[1])
    grad_query = add(add(gq[0], near_q), far_q)

    both = jnp.stack([attended, grad_query])
    for mask in reversed(middle):
        half = both.shape[-1] // 2
        both = add(both[..., :half], swap(both[..., half:].astype(BF16), mask))
    both, came_far = lax.optimization_barrier((both.astype(BF16), came_far))
    far_both = swap(both[..., 2 * own :], 2)
    near_both = both[..., : 2 * own]

    core_gkv = swap(jnp.stack([gkv_near[1], came_far[1]]), 1)
    (d_points,) = call(
        points_kernel,
        [place, gkv_near, came_far, core_gkv, weights],
        [shape((slots, width), BF16)],
        flops=4 * slots * width * width,
    )
    far_both, d_points = lax.optimization_barrier((far_both, d_points))
    core_both = swap(jnp.stack([near_both[..., own:], far_both[..., own:]]), 1)
    result, d_latents = call(
        queries_kernel,
        [place, near_both, far_both, core_both, latents, d_out, w_out, w_query],
        [shape((own, width), BF16)] * 2,
        [pltpu.VMEM((width, own), F32)],
        flops=4 * own * width * width,
    )
    return (result, d_latents, d_points)


def solution(mesh):
    part = P(("groups", "pts"), None)
    in_specs = (part, part, P(("groups", "pts")), P(), P(), P(), P(), part)
    return jax.shard_map(
        functools.partial(body, mesh.shape["pts"]),
        mesh=mesh,
        in_specs=in_specs,
        out_specs=(part, part, part),
        check_vma=False,
    )
```

```python
import functools

import jax
import jax.numpy as jnp
from jax import lax
from jax.experimental import pallas as pl
from jax.experimental.pallas import tpu as pltpu
from jax.sharding import PartitionSpec as P

HEADS = 12
TEAM = 4
MINE = HEADS // TEAM
BF16 = jnp.bfloat16
F32 = jnp.float32
LANES = 128
NT = (((1,), (1,)), ((), ()))


def dot(a, b):
    return jnp.dot(a, b, preferred_element_type=F32)


def dot_nt(a, b):
    return lax.dot_general(a, b, NT, preferred_element_type=F32)


def low_lanes(shape):
    return lax.broadcasted_iota(jnp.int32, shape, 1) < shape[1] // 2


def lanes_of(part):
    start = part // 2 * LANES
    return slice(start, start + LANES)


def keep_part(array, part):
    low = low_lanes(array.shape)
    return jnp.where(low if part % 2 == 0 else ~low, array, jnp.zeros_like(array))


def store_quarters(place_ref, near_refs, far_ref, one, two, at):
    mine = one.shape[1] // TEAM
    for quarter in range(TEAM):
        cols = slice(quarter * mine, (quarter + 1) * mine)
        piece = jnp.concatenate([one[:, cols], two[:, cols]], axis=1)
        relative = (place_ref[0] % TEAM) ^ quarter
        for which, ref in enumerate(near_refs):

            @pl.when(relative == which)
            def _():
                ref[at, :] = piece

        @pl.when(relative >= 2)
        def _():
            far_ref[relative % 2, at, :] = piece


def load(source, target, sems, pieces):
    step = source.shape[0] // pieces
    copies = []
    for k in range(pieces):
        at = slice(k * step, (k + 1) * step)
        copies.append(pltpu.make_async_copy(source.at[at], target.at[at], sems.at[k]))
        copies[-1].start()
    return copies


def wait(*groups):
    for group in groups:
        for copy in group:
            copy.wait()


def rows_kernel(
    place_ref, count_ref, latents_hbm, d_out_hbm, w_query_hbm, w_out_hbm,
    keep_ref, core_ref, far_ref, latents_ref, d_out_ref, w_query_ref, w_out_ref, sems
):
    pieces = sems.shape[1]
    own = latents_ref.shape[0]
    loads = [
        load(latents_hbm, latents_ref, sems.at[0], 1),
        load(w_query_hbm, w_query_ref, sems.at[1], pieces),
        load(d_out_hbm, d_out_ref, sems.at[2], 1),
        load(w_out_hbm, w_out_ref, sems.at[3], pieces),
    ]
    extra = keep_ref.shape[0] - own, keep_ref.shape[1]
    first = lax.broadcasted_iota(jnp.int32, extra, 1) < extra[1] // 2
    count = jnp.where(first, count_ref[0] // 16, count_ref[0] % 16).astype(F32).astype(BF16)
    for ref in (keep_ref, core_ref, far_ref.at[0], far_ref.at[1]):
        ref[own:, :] = count
    wait(*loads[:2])
    query = dot(latents_ref[...], w_query_ref[...]).astype(BF16)
    wait(*loads[2:])
    grad = dot_nt(d_out_ref[...], w_out_ref[...]).astype(BF16)
    store_quarters(place_ref, (keep_ref, core_ref), far_ref, query, grad, slice(0, own))


def slots_kernel(
    place_ref, points_hbm, w_key_hbm, w_value_hbm,
    keep_ref, core_ref, far_ref, points_ref, w_key_ref, w_value_ref, sems
):
    pieces = sems.shape[1]
    loads = [
        load(points_hbm, points_ref, sems.at[0], pieces),
        load(w_key_hbm, w_key_ref, sems.at[1], pieces),
        load(w_value_hbm, w_value_ref, sems.at[2], pieces),
    ]
    wait(*loads[:2])
    keys = dot(points_ref[...], w_key_ref[...]).astype(BF16) * jnp.asarray(0.125, BF16)
    wait(*loads[2:])
    values = dot(points_ref[...], w_value_ref[...]).astype(BF16)
    store_quarters(place_ref, (keep_ref, core_ref), far_ref, keys, values, slice(0, keys.shape[0]))


def weights_kernel(w_key_ref, w_value_ref, out_ref):
    mine = out_ref.shape[1] // 2
    for i, ref in enumerate((w_key_ref, w_value_ref)):
        turned = ref[...].T
        for quarter in range(TEAM):
            out_ref[quarter, i * mine : (i + 1) * mine, :] = turned[quarter * mine : (quarter + 1) * mine]


def chunk_kernel(keep_ref, core_ref, far_ref, diagonal_ref, out_ref, count_ref):
    own, mine = out_ref.shape[0] // TEAM, out_ref.shape[1] // 2
    for i, ref in enumerate((keep_ref, core_ref, far_ref.at[0], diagonal_ref.at[1])):
        out_ref[i * own : (i + 1) * own, :] = ref[:own, :]
        row = ref[own:, :].astype(F32)[:1, :]
        count_ref[i : i + 1, :] = 16 * row[:, :LANES] + row[:, mine : mine + LANES]


def turn_kernel(picks, *refs):
    for i, (ref, which) in enumerate(picks):
        refs[-1][i] = (refs[ref][...] if which is None else refs[ref][which]).T


def dead_slots(slot, count_ref, block):
    count = jnp.concatenate([count_ref[block : block + 1, :]] * (slot.shape[1] // LANES), axis=1)
    return slot >= count


def forward_kernel(blocks, count_ref, qg_ref, *refs):
    kv_refs, kv_t_refs = {}, {}
    if 0 in blocks:
        keep_ref, core_ref, near_t_ref, *refs = refs
        kv_refs.update({0: keep_ref, 1: core_ref})
        kv_t_refs.update({0: near_t_ref.at[0], 1: near_t_ref.at[1]})
    if 2 in blocks:
        far_ref, diagonal_ref, far_t_ref, *refs = refs
        kv_refs.update({2: far_ref.at[0], 3: diagonal_ref.at[1]})
        kv_t_refs.update({2: far_t_ref.at[0], 3: far_t_ref.at[1]})
    before = refs[:2] if blocks[0] else ()
    numer_ref, stat_ref, score_ref, weight_ref = refs[len(before) :]
    rows = qg_ref.shape[0]
    slots = kv_refs[blocks[0]].shape[0]
    dim = qg_ref.shape[1] // (2 * MINE)
    depth = score_ref.shape[0]
    slot = lax.broadcasted_iota(jnp.int32, (slots, rows), 0).astype(F32)
    units = [(head, block) for head in range(MINE) for block in blocks]
    tops, totals, numers = {}, {}, {}

    def score(step):
        head, block = units[step]
        keys = keep_part(kv_refs[block][:, lanes_of(head)], head)
        score_ref[step % depth] = dot_nt(keys, qg_ref[:, lanes_of(head)])

    def weigh(step):
        dead = dead_slots(slot, count_ref, units[step][1])
        scores = jnp.where(dead, -jnp.inf, score_ref[step % depth])
        tops[step] = jnp.max(scores, axis=0, keepdims=True)
        weights = jnp.exp(scores - tops[step])
        totals[step] = jnp.sum(weights, axis=0, keepdims=True)
        weight_ref[step % depth] = weights.astype(BF16)

    def attend(step):
        head, block = units[step]
        part = MINE + head
        at = slice(part * dim, (part + 1) * dim)
        numers[step] = dot(kv_t_refs[block][at, :], weight_ref[step % depth])
        if block != blocks[-1]:
            return
        steps = list(range(step - len(blocks) + 1, step + 1))
        own_rows = slice(head * dim, (head + 1) * dim)
        if before:
            steps.append(-1)
            numers[-1] = before[0][own_rows, :]
            tops[-1] = before[1][head : head + 1, :]
            totals[-1] = before[1][MINE + head : MINE + head + 1, :]
        top = functools.reduce(jnp.maximum, [tops[s] for s in steps])
        scale = {s: jnp.exp(tops[s] - top) for s in steps}
        total = sum(scale[s] * totals[s] for s in steps)
        numer = sum(scale[s] * numers[s] for s in steps)
        numer_ref[own_rows, :] = numer
        half = part % 2 * dim
        grad_t = qg_ref[:, lanes_of(part)].astype(F32).T[half : half + dim, :]
        inner = jnp.sum(grad_t * numer, axis=0, keepdims=True)
        for i, row in enumerate((top, total, top + jnp.log(total), inner / total)):
            stat_ref[i * MINE + head : i * MINE + head + 1, :] = row

    for step in range(len(units) + 2):
        if step < len(units):
            score(step)
        if 0 <= step - 1 < len(units):
            weigh(step - 1)
        if 0 <= step - 2:
            attend(step - 2)


def backward_kernel(chunks, start, side, first, last, count_ref, *refs):
    qg_refs, stat_refs, refs = refs[:chunks], refs[chunks : 2 * chunks], refs[2 * chunks :]
    even_ref, odd_ref, kv_t_ref, *refs = refs
    kv_refs = (even_ref.at[0], odd_ref.at[1]) if side else (even_ref, odd_ref)
    if not first:
        sum_in_ref, *refs = refs
    gq_in_ref = None
    if side == 0:
        gq_in_ref, *refs = refs
    gq_ref, sum_ref, total_ref, score_ref, gw_ref, prob_ref, ds_ref = refs
    rows = qg_refs[0].shape[0]
    slots, dim = even_ref.shape[-2], even_ref.shape[-1] // (2 * MINE)
    depth = score_ref.shape[0]
    slot = lax.broadcasted_iota(jnp.int32, (slots, rows), 0).astype(F32)
    low = low_lanes((slots, LANES))
    units = [(c, head, block) for c in range(chunks) for block in range(2) for head in range(MINE)]
    gq, held = {}, {}

    def product(chunk, block, part):
        return dot_nt(keep_part(kv_refs[block][:, lanes_of(part)], part), qg_refs[chunk][:, lanes_of(part)])

    def score(step):
        chunk, head, block = units[step]
        score_ref[step % depth] = product(chunk, block, head)
        gw_ref[step % depth] = product(chunk, block, MINE + head)

    def weigh(step):
        chunk, head, block = units[step]
        dead = dead_slots(slot, count_ref, 2 * side + block)
        scores = jnp.where(dead, -jnp.inf, score_ref[step % depth])
        prob = jnp.exp(scores - stat_refs[chunk][head : head + 1, :])
        delta = stat_refs[chunk][MINE + head : MINE + head + 1, :]
        prob_ref[step % depth] = prob.astype(BF16)
        ds_ref[step % depth] = (prob * (gw_ref[step % depth] - delta)).astype(BF16)

    def store(chunk, block, part, value):
        held[part] = value
        pair = part // 2 * 2, part // 2 * 2 + 1
        if not all(p in held for p in pair):
            return
        at = block, slice(0, slots), lanes_of(part)
        total = jnp.where(low, held.pop(pair[0]), held.pop(pair[1]))
        if chunk > 0:
            total += total_ref[at]
        elif not first:
            total += sum_in_ref[at]
        if chunk < chunks - 1:
            total_ref[at] = total
            return
        if last:
            scales = [0.125 if p < MINE else 1.0 for p in pair]
            total *= scales[0] if scales[0] == scales[1] else jnp.where(low, *scales)
        sum_ref[at] = total.astype(sum_ref.dtype)

    def collect(step):
        chunk, head, block = units[step]
        qg_ref = qg_refs[chunk]
        store(chunk, block, head, dot(ds_ref[step % depth], qg_ref[:, lanes_of(head)]))
        store(chunk, block, MINE + head, dot(prob_ref[step % depth], qg_ref[:, lanes_of(MINE + head)]))
        at = slice(head * dim, (head + 1) * dim)
        term = dot(kv_t_ref[block, at, :], ds_ref[step % depth])
        if block == 0:
            gq[head] = term if gq_in_ref is None else term + gq_in_ref[start + chunk, at, :]
        else:
            gq_ref[chunk, at, :] = (gq[head] + term).astype(gq_ref.dtype)

    for step in range(len(units) + 2):
        if 0 <= step - 2:
            collect(step - 2)
        if 0 <= step - 1 < len(units):
            weigh(step - 1)
        if step < len(units):
            score(step)


def queries_kernel(
    place_ref, near_ref, far_ref, core_ref, latents_ref, d_out_ref, w_out_ref, w_query_ref,
    result_ref, d_latents_ref, joined_ref
):
    own = latents_ref.shape[0]
    mine = near_ref.shape[1]
    for kind in range(2):
        for relative in range(TEAM):
            core, across = relative % 2, relative // 2
            quarter = (place_ref[0] % TEAM) ^ relative
            piece = core_ref[across, kind] if core else (near_ref, far_ref)[across][kind, :, :own]
            joined_ref[pl.ds(pl.multiple_of(quarter * mine, mine), mine), :] = piece.astype(F32)
        joined = joined_ref[...].T.astype(BF16)
        if kind == 0:
            result_ref[...] = (latents_ref[...].astype(F32) + dot(joined, w_out_ref[...])).astype(BF16)
        else:
            d_latents_ref[...] = (
                d_out_ref[...].astype(F32) + dot_nt(joined, w_query_ref[...])
            ).astype(BF16)


def points_kernel(place_ref, near_ref, far_ref, core_ref, weight_ref, out_ref):
    total = None
    for relative in range(TEAM):
        core, across = relative % 2, relative // 2
        piece = core_ref[across] if core else (near_ref, far_ref)[across][0]
        term = dot(piece, weight_ref[(place_ref[0] % TEAM) ^ relative])
        total = term if total is None else total + term
    out_ref[...] = total.astype(BF16)


def call(kernel, ins, out_shapes, scratch=(), flops=0, exps=0, space=pltpu.VMEM, grant=40):
    vmem = pl.BlockSpec(memory_space=pltpu.VMEM)
    other = pl.BlockSpec(memory_space=space)
    smem = pl.BlockSpec(memory_space=pltpu.SMEM)
    moved = sum(a.size * a.dtype.itemsize for a in list(ins) + list(out_shapes))
    return pl.pallas_call(
        kernel,
        in_specs=[smem if a.dtype == jnp.int32 else other for a in ins],
        out_specs=[vmem] * len(out_shapes),
        out_shape=out_shapes,
        scratch_shapes=scratch,
        compiler_params=pltpu.CompilerParams(vmem_limit_bytes=grant << 20),
        cost_estimate=pl.CostEstimate(flops=flops // 8, transcendentals=exps // 8, bytes_accessed=moved // 8),
    )(*ins)


def body(size, latents, points, counts, w_query, w_key, w_value, w_out, d_out):
    own, width = latents.shape
    slots = points.shape[0]
    mine = width // TEAM
    shape = jax.ShapeDtypeStruct
    near_bit, far_bit = size // 4, size // 2
    middle = []
    bit = size // 8
    while bit >= TEAM:
        middle.append(bit)
        bit //= 2
    place = lax.axis_index("pts").astype(jnp.int32).reshape(1)

    def swap(array, mask):
        return lax.ppermute(array, "pts", [(i, i ^ mask) for i in range(size)])

    def project(kernel, scalars, inputs, rows):
        return call(
            kernel,
            scalars + inputs,
            [shape((rows, 2 * mine), BF16)] * 2 + [shape((2, rows, 2 * mine), BF16)],
            [pltpu.VMEM(a.shape, BF16) for a in inputs] + [pltpu.SemaphoreType.DMA((len(inputs), 4))],
            flops=4 * rows * width * width,
            space=pltpu.HBM,
            grant=60,
        )

    keep_qg, core_qg, far_qg = project(
        rows_kernel, [place, counts], [latents, d_out, w_query, w_out], own + 16
    )
    keep_qg, points = lax.optimization_barrier((keep_qg, points))
    far_qg = swap(far_qg, 2)
    core_qg = swap(core_qg, 1)
    keep, core, far = project(slots_kernel, [place], [points, w_key, w_value], slots)
    far_qg, far = lax.optimization_barrier((far_qg, far))
    far = swap(far, 2)
    core = swap(core, 1)
    qg, count = call(
        chunk_kernel,
        [keep_qg, core_qg, far_qg, swap(far_qg, 1)],
        [shape((TEAM * own, 2 * mine), BF16), shape((TEAM, LANES), F32)],
    )
    for mask in middle:
        qg = jnp.concatenate([qg, swap(qg, mask)], axis=0)
    qg, w_key, w_value = lax.optimization_barrier((qg, w_key, w_value))
    far_qg = swap(qg, far_bit)
    qg = [qg, swap(qg, near_bit), far_qg]
    (weights,) = call(weights_kernel, [w_key, w_value], [shape((TEAM, 2 * mine, width), BF16)])
    turned = [shape((2, 2 * mine, slots), BF16)]
    (near_t,) = call(functools.partial(turn_kernel, ((0, None), (1, None))), [keep, core], turned)
    near_t, weights = lax.optimization_barrier((near_t, weights))
    rows = qg[0].shape[0]
    team_slots = TEAM * slots
    work = 2 * rows * team_slots * mine

    def forward(p, blocks, before=()):
        return call(
            functools.partial(forward_kernel, blocks),
            [count, qg[p]]
            + ([keep, core, near_t] if 0 in blocks else [])
            + ([far, diagonal, far_t] if 2 in blocks else [])
            + list(before),
            [shape((mine, rows), F32), shape((4 * MINE, rows), F32)],
            [pltpu.VMEM((3, slots, rows), F32), pltpu.VMEM((3, slots, rows), BF16)],
            flops=2 * work * len(blocks),
            exps=rows * slots * len(blocks) * MINE,
        )

    early = [forward(p, (0, 1)) for p in range(2)]
    early, far, qg[2] = lax.optimization_barrier((early, far, qg[2]))
    qg.append(swap(qg[2], near_bit))
    diagonal = swap(far, 1)
    (far_t,) = call(functools.partial(turn_kernel, ((0, 0), (1, 1))), [far, diagonal], turned)
    done = [forward(p, (2, 3), early[p]) for p in range(2)]
    done += [forward(p, (0, 1, 2, 3)) for p in (2, 3)]
    numer = [d[0] for d in done]
    tops = [d[1][:MINE] for d in done]
    stats = [d[1][2 * MINE :] for d in done]

    def merge(*parts):
        lse = [p[..., :MINE, :] for p in parts]
        top = functools.reduce(jnp.maximum, lse)
        scale = [jnp.exp(x - top) for x in lse]
        total = sum(scale)
        delta = sum(s * p[..., MINE:, :] for s, p in zip(scale, parts)) / total
        return jnp.concatenate([top + jnp.log(total), delta], axis=-2)

    stat = jnp.stack(stats)
    for mask, turn in ((near_bit, 1), (far_bit, 2)):
        came = swap(stat, mask)
        stat = merge(stat, jnp.stack([came[q ^ turn] for q in range(4)]))
    final = [stat[q] for q in range(4)]
    if middle:
        final = stat
        for mask in reversed(middle):
            half = final.shape[-1] // 2
            final = merge(final[..., :half], swap(final[..., half:], mask))
        for mask in middle:
            final = jnp.concatenate([final, swap(final, mask)], axis=-1)
        final = [final[q] for q in range(4)]

    def add(array, came):
        return array.astype(F32) + came.astype(F32)

    def scaled(p):
        scale = jnp.exp(tops[p] - final[p][:MINE])
        return (numer[p].reshape(MINE, -1, rows) * scale[:, None, :]).reshape(mine, rows)

    order = (3, 2, 1, 0)

    def backward(chunks, side, kind, sums=(), partial=(), last=False):
        kept = (2, slots, 2 * mine)
        return call(
            functools.partial(
                backward_kernel, len(chunks), order.index(chunks[0]), side, not sums, last
            ),
            [count]
            + [qg[p] for p in chunks]
            + [final[p] for p in chunks]
            + ([far, diagonal, far_t] if side else [keep, core, near_t])
            + list(sums)
            + list(partial),
            [shape((len(chunks), mine, rows), kind), shape(kept, BF16 if last else F32)],
            [pltpu.VMEM(kept if len(chunks) > 1 else (1, 8, LANES), F32)]
            + [pltpu.VMEM((2, slots, rows), F32)] * 2
            + [pltpu.VMEM((2, slots, rows), BF16)] * 2,
            flops=7 * work * len(chunks),
            exps=rows * team_slots // 2 * MINE * len(chunks),
        )

    came_a = swap(jnp.stack([scaled(3), scaled(2)]).astype(BF16), far_bit)
    partial, gkv_far = backward(order, 1, F32, last=True)
    came_a, partial = lax.optimization_barrier((came_a, partial))
    came_far = swap(gkv_far, 2)
    near_a = swap(add(scaled(1), came_a[0]).astype(BF16), near_bit)
    gq, total = backward((3,), 0, BF16, partial=[partial])
    came = swap(gq[0], near_bit)
    gq, total = backward((2,), 0, F32, [total], [partial])
    sent, total = lax.optimization_barrier((add(gq[0], came).astype(BF16), total))
    far_q = swap(sent, far_bit)
    gq, total = backward((1,), 0, BF16, [total], [partial])
    near_q = swap(gq[0], near_bit)
    came_far, far_q, total = lax.optimization_barrier((came_far, far_q, total))
    gq, gkv_near = backward((0,), 0, F32, [total], [partial], True)
    attended = add(add(scaled(0), near_a), came_a[1])
    grad_query = add(add(gq[0], near_q), far_q)

    both = jnp.stack([attended, grad_query])
    for mask in reversed(middle):
        half = both.shape[-1] // 2
        both = add(both[..., :half], swap(both[..., half:].astype(BF16), mask))
    both, came_far = lax.optimization_barrier((both.astype(BF16), came_far))
    far_both = swap(both[..., 2 * own :], 2)
    near_both = both[..., : 2 * own]

    core_gkv = swap(jnp.stack([gkv_near[1], came_far[1]]), 1)
    (d_points,) = call(
        points_kernel,
        [place, gkv_near, came_far, core_gkv, weights],
        [shape((slots, width), BF16)],
        flops=4 * slots * width * width,
    )
    far_both, d_points = lax.optimization_barrier((far_both, d_points))
    core_both = swap(jnp.stack([near_both[..., own:], far_both[..., own:]]), 1)
    result, d_latents = call(
        queries_kernel,
        [place, near_both, far_both, core_both, latents, d_out, w_out, w_query],
        [shape((own, width), BF16)] * 2,
        [pltpu.VMEM((width, own), F32)],
        flops=4 * own * width * width,
    )
    return (result, d_latents, d_points)


def solution(mesh):
    part = P(("groups", "pts"), None)
    in_specs = (part, part, P(("groups", "pts")), P(), P(), P(), P(), part)
    return jax.shard_map(
        functools.partial(body, mesh.shape["pts"]),
        mesh=mesh,
        in_specs=in_specs,
        out_specs=(part, part, part),
        check_vma=False,
    )
```

```python
import functools

import jax
import jax.numpy as jnp
from jax import lax
from jax.experimental import pallas as pl
from jax.experimental.pallas import tpu as pltpu
from jax.sharding import PartitionSpec as P

HEADS = 12
TEAM = 4
MINE = HEADS // TEAM
BF16 = jnp.bfloat16
F32 = jnp.float32
LANES = 128
NT = (((1,), (1,)), ((), ()))


def dot(a, b):
    return jnp.dot(a, b, preferred_element_type=F32)


def dot_nt(a, b):
    return lax.dot_general(a, b, NT, preferred_element_type=F32)


def low_lanes(shape):
    return lax.broadcasted_iota(jnp.int32, shape, 1) < shape[1] // 2


def lanes_of(part):
    start = part // 2 * LANES
    return slice(start, start + LANES)


def keep_part(array, part):
    low = low_lanes(array.shape)
    return jnp.where(low if part % 2 == 0 else ~low, array, jnp.zeros_like(array))


def store_quarters(place_ref, near_refs, far_ref, one, two, at):
    mine = one.shape[1] // TEAM
    for quarter in range(TEAM):
        cols = slice(quarter * mine, (quarter + 1) * mine)
        piece = jnp.concatenate([one[:, cols], two[:, cols]], axis=1)
        relative = (place_ref[0] % TEAM) ^ quarter
        for which, ref in enumerate(near_refs):

            @pl.when(relative == which)
            def _():
                ref[at, :] = piece

        @pl.when(relative >= 2)
        def _():
            far_ref[relative % 2, at, :] = piece


def load(source, target, sems, pieces):
    step = source.shape[0] // pieces
    copies = []
    for k in range(pieces):
        at = slice(k * step, (k + 1) * step)
        copies.append(pltpu.make_async_copy(source.at[at], target.at[at], sems.at[k]))
        copies[-1].start()
    return copies


def wait(*groups):
    for group in groups:
        for copy in group:
            copy.wait()


def rows_kernel(
    place_ref, count_ref, latents_hbm, d_out_hbm, w_query_hbm, w_out_hbm,
    keep_ref, core_ref, far_ref, latents_ref, d_out_ref, w_query_ref, w_out_ref, sems
):
    pieces = sems.shape[1]
    own = latents_ref.shape[0]
    loads = [
        load(latents_hbm, latents_ref, sems.at[0], 1),
        load(w_query_hbm, w_query_ref, sems.at[1], pieces),
        load(d_out_hbm, d_out_ref, sems.at[2], 1),
        load(w_out_hbm, w_out_ref, sems.at[3], pieces),
    ]
    extra = keep_ref.shape[0] - own, keep_ref.shape[1]
    first = lax.broadcasted_iota(jnp.int32, extra, 1) < extra[1] // 2
    count = jnp.where(first, count_ref[0] // 16, count_ref[0] % 16).astype(F32).astype(BF16)
    for ref in (keep_ref, core_ref, far_ref.at[0], far_ref.at[1]):
        ref[own:, :] = count
    wait(*loads[:2])
    query = dot(latents_ref[...], w_query_ref[...]).astype(BF16)
    wait(*loads[2:])
    grad = dot_nt(d_out_ref[...], w_out_ref[...]).astype(BF16)
    store_quarters(place_ref, (keep_ref, core_ref), far_ref, query, grad, slice(0, own))


def slots_kernel(place_ref, points_ref, w_key_ref, w_value_ref, keep_ref, core_ref, far_ref):
    keys = dot(points_ref[...], w_key_ref[...]).astype(BF16) * jnp.asarray(0.125, BF16)
    values = dot(points_ref[...], w_value_ref[...]).astype(BF16)
    store_quarters(place_ref, (keep_ref, core_ref), far_ref, keys, values, slice(0, keys.shape[0]))


def weights_kernel(w_key_ref, w_value_ref, out_ref):
    mine = out_ref.shape[1] // 2
    for i, ref in enumerate((w_key_ref, w_value_ref)):
        turned = ref[...].T
        for quarter in range(TEAM):
            out_ref[quarter, i * mine : (i + 1) * mine, :] = turned[quarter * mine : (quarter + 1) * mine]


def chunk_kernel(keep_ref, core_ref, far_ref, diagonal_ref, out_ref, count_ref):
    own, mine = out_ref.shape[0] // TEAM, out_ref.shape[1] // 2
    for i, ref in enumerate((keep_ref, core_ref, far_ref.at[0], diagonal_ref.at[1])):
        out_ref[i * own : (i + 1) * own, :] = ref[:own, :]
        row = ref[own:, :].astype(F32)[:1, :]
        count_ref[i : i + 1, :] = 16 * row[:, :LANES] + row[:, mine : mine + LANES]


def turn_kernel(picks, *refs):
    for i, (ref, which) in enumerate(picks):
        refs[-1][i] = (refs[ref][...] if which is None else refs[ref][which]).T


def dead_slots(slot, count_ref, block):
    count = jnp.concatenate([count_ref[block : block + 1, :]] * (slot.shape[1] // LANES), axis=1)
    return slot >= count


def forward_kernel(blocks, count_ref, qg_ref, *refs):
    kv_refs, kv_t_refs = {}, {}
    if 0 in blocks:
        keep_ref, core_ref, near_t_ref, *refs = refs
        kv_refs.update({0: keep_ref, 1: core_ref})
        kv_t_refs.update({0: near_t_ref.at[0], 1: near_t_ref.at[1]})
    if 2 in blocks:
        far_ref, diagonal_ref, far_t_ref, *refs = refs
        kv_refs.update({2: far_ref.at[0], 3: diagonal_ref.at[1]})
        kv_t_refs.update({2: far_t_ref.at[0], 3: far_t_ref.at[1]})
    before = refs[:2] if blocks[0] else ()
    numer_ref, stat_ref, score_ref, weight_ref = refs[len(before) :]
    rows = qg_ref.shape[0]
    slots = kv_refs[blocks[0]].shape[0]
    dim = qg_ref.shape[1] // (2 * MINE)
    depth = score_ref.shape[0]
    slot = lax.broadcasted_iota(jnp.int32, (slots, rows), 0).astype(F32)
    units = [(head, block) for head in range(MINE) for block in blocks]
    tops, totals, numers = {}, {}, {}

    def score(step):
        head, block = units[step]
        keys = keep_part(kv_refs[block][:, lanes_of(head)], head)
        score_ref[step % depth] = dot_nt(keys, qg_ref[:, lanes_of(head)])

    def weigh(step):
        dead = dead_slots(slot, count_ref, units[step][1])
        scores = jnp.where(dead, -jnp.inf, score_ref[step % depth])
        tops[step] = jnp.max(scores, axis=0, keepdims=True)
        weights = jnp.exp(scores - tops[step])
        totals[step] = jnp.sum(weights, axis=0, keepdims=True)
        weight_ref[step % depth] = weights.astype(BF16)

    def attend(step):
        head, block = units[step]
        part = MINE + head
        at = slice(part * dim, (part + 1) * dim)
        numers[step] = dot(kv_t_refs[block][at, :], weight_ref[step % depth])
        if block != blocks[-1]:
            return
        steps = list(range(step - len(blocks) + 1, step + 1))
        own_rows = slice(head * dim, (head + 1) * dim)
        if before:
            steps.append(-1)
            numers[-1] = before[0][own_rows, :]
            tops[-1] = before[1][head : head + 1, :]
            totals[-1] = before[1][MINE + head : MINE + head + 1, :]
        top = functools.reduce(jnp.maximum, [tops[s] for s in steps])
        scale = {s: jnp.exp(tops[s] - top) for s in steps}
        total = sum(scale[s] * totals[s] for s in steps)
        numer = sum(scale[s] * numers[s] for s in steps)
        numer_ref[own_rows, :] = numer
        half = part % 2 * dim
        grad_t = qg_ref[:, lanes_of(part)].astype(F32).T[half : half + dim, :]
        inner = jnp.sum(grad_t * numer, axis=0, keepdims=True)
        for i, row in enumerate((top, total, top + jnp.log(total), inner / total)):
            stat_ref[i * MINE + head : i * MINE + head + 1, :] = row

    for step in range(len(units) + 2):
        if step < len(units):
            score(step)
        if 0 <= step - 1 < len(units):
            weigh(step - 1)
        if 0 <= step - 2:
            attend(step - 2)


def backward_kernel(chunks, start, side, first, last, count_ref, *refs):
    qg_refs, stat_refs, refs = refs[:chunks], refs[chunks : 2 * chunks], refs[2 * chunks :]
    even_ref, odd_ref, kv_t_ref, *refs = refs
    kv_refs = (even_ref.at[0], odd_ref.at[1]) if side else (even_ref, odd_ref)
    if not first:
        sum_in_ref, *refs = refs
    gq_in_ref = None
    if side == 0:
        gq_in_ref, *refs = refs
    gq_ref, sum_ref, total_ref, score_ref, gw_ref, prob_ref, ds_ref = refs
    rows = qg_refs[0].shape[0]
    slots, dim = even_ref.shape[-2], even_ref.shape[-1] // (2 * MINE)
    depth = score_ref.shape[0]
    slot = lax.broadcasted_iota(jnp.int32, (slots, rows), 0).astype(F32)
    low = low_lanes((slots, LANES))
    units = [(c, head, block) for c in range(chunks) for block in range(2) for head in range(MINE)]
    gq, held = {}, {}

    def product(chunk, block, part):
        return dot_nt(keep_part(kv_refs[block][:, lanes_of(part)], part), qg_refs[chunk][:, lanes_of(part)])

    def score(step):
        chunk, head, block = units[step]
        score_ref[step % depth] = product(chunk, block, head)
        gw_ref[step % depth] = product(chunk, block, MINE + head)

    def weigh(step):
        chunk, head, block = units[step]
        dead = dead_slots(slot, count_ref, 2 * side + block)
        scores = jnp.where(dead, -jnp.inf, score_ref[step % depth])
        prob = jnp.exp(scores - stat_refs[chunk][head : head + 1, :])
        delta = stat_refs[chunk][MINE + head : MINE + head + 1, :]
        prob_ref[step % depth] = prob.astype(BF16)
        ds_ref[step % depth] = (prob * (gw_ref[step % depth] - delta)).astype(BF16)

    def store(chunk, block, part, value):
        held[part] = value
        pair = part // 2 * 2, part // 2 * 2 + 1
        if not all(p in held for p in pair):
            return
        at = block, slice(0, slots), lanes_of(part)
        total = jnp.where(low, held.pop(pair[0]), held.pop(pair[1]))
        if chunk > 0:
            total += total_ref[at]
        elif not first:
            total += sum_in_ref[at]
        if chunk < chunks - 1:
            total_ref[at] = total
            return
        if last:
            scales = [0.125 if p < MINE else 1.0 for p in pair]
            total *= scales[0] if scales[0] == scales[1] else jnp.where(low, *scales)
        sum_ref[at] = total.astype(sum_ref.dtype)

    def collect(step):
        chunk, head, block = units[step]
        qg_ref = qg_refs[chunk]
        store(chunk, block, head, dot(ds_ref[step % depth], qg_ref[:, lanes_of(head)]))
        store(chunk, block, MINE + head, dot(prob_ref[step % depth], qg_ref[:, lanes_of(MINE + head)]))
        at = slice(head * dim, (head + 1) * dim)
        term = dot(kv_t_ref[block, at, :], ds_ref[step % depth])
        if block == 0:
            gq[head] = term if gq_in_ref is None else term + gq_in_ref[start + chunk, at, :]
        else:
            gq_ref[chunk, at, :] = (gq[head] + term).astype(gq_ref.dtype)

    for step in range(len(units) + 2):
        if 0 <= step - 2:
            collect(step - 2)
        if 0 <= step - 1 < len(units):
            weigh(step - 1)
        if step < len(units):
            score(step)


def queries_kernel(
    place_ref, near_ref, far_ref, core_ref, latents_ref, d_out_ref, w_out_ref, w_query_ref,
    result_ref, d_latents_ref, joined_ref
):
    own = latents_ref.shape[0]
    mine = near_ref.shape[1]
    for kind in range(2):
        for relative in range(TEAM):
            core, across = relative % 2, relative // 2
            quarter = (place_ref[0] % TEAM) ^ relative
            piece = core_ref[across, kind] if core else (near_ref, far_ref)[across][kind, :, :own]
            joined_ref[pl.ds(pl.multiple_of(quarter * mine, mine), mine), :] = piece.astype(F32)
        joined = joined_ref[...].T.astype(BF16)
        if kind == 0:
            result_ref[...] = (latents_ref[...].astype(F32) + dot(joined, w_out_ref[...])).astype(BF16)
        else:
            d_latents_ref[...] = (
                d_out_ref[...].astype(F32) + dot_nt(joined, w_query_ref[...])
            ).astype(BF16)


def points_kernel(place_ref, near_ref, far_ref, core_ref, weight_ref, out_ref):
    total = None
    for relative in range(TEAM):
        core, across = relative % 2, relative // 2
        piece = core_ref[across] if core else (near_ref, far_ref)[across][0]
        term = dot(piece, weight_ref[(place_ref[0] % TEAM) ^ relative])
        total = term if total is None else total + term
    out_ref[...] = total.astype(BF16)


def call(kernel, ins, out_shapes, scratch=(), flops=0, exps=0, space=pltpu.VMEM, grant=40):
    vmem = pl.BlockSpec(memory_space=pltpu.VMEM)
    other = pl.BlockSpec(memory_space=space)
    smem = pl.BlockSpec(memory_space=pltpu.SMEM)
    moved = sum(a.size * a.dtype.itemsize for a in list(ins) + list(out_shapes))
    return pl.pallas_call(
        kernel,
        in_specs=[smem if a.dtype == jnp.int32 else other for a in ins],
        out_specs=[vmem] * len(out_shapes),
        out_shape=out_shapes,
        scratch_shapes=scratch,
        compiler_params=pltpu.CompilerParams(vmem_limit_bytes=grant << 20),
        cost_estimate=pl.CostEstimate(flops=flops // 8, transcendentals=exps // 8, bytes_accessed=moved // 8),
    )(*ins)


def body(size, latents, points, counts, w_query, w_key, w_value, w_out, d_out):
    own, width = latents.shape
    slots = points.shape[0]
    mine = width // TEAM
    shape = jax.ShapeDtypeStruct
    near_bit, far_bit = size // 4, size // 2
    middle = []
    bit = size // 8
    while bit >= TEAM:
        middle.append(bit)
        bit //= 2
    place = lax.axis_index("pts").astype(jnp.int32).reshape(1)

    def swap(array, mask):
        return lax.ppermute(array, "pts", [(i, i ^ mask) for i in range(size)])

    def pieces(rows):
        return [shape((rows, 2 * mine), BF16)] * 2 + [shape((2, rows, 2 * mine), BF16)]

    inputs = [latents, d_out, w_query, w_out]
    keep_qg, core_qg, far_qg = call(
        rows_kernel,
        [place, counts] + inputs,
        pieces(own + 16),
        [pltpu.VMEM(a.shape, BF16) for a in inputs] + [pltpu.SemaphoreType.DMA((len(inputs), 4))],
        flops=4 * own * width * width,
        space=pltpu.HBM,
        grant=60,
    )
    keep_qg, then_place = lax.optimization_barrier((keep_qg, place))
    far_qg = swap(far_qg, 2)
    core_qg = swap(core_qg, 1)
    keep, core, far = call(
        slots_kernel, [then_place, points, w_key, w_value], pieces(slots), flops=4 * slots * width * width
    )
    far_qg, far = lax.optimization_barrier((far_qg, far))
    far = swap(far, 2)
    core = swap(core, 1)
    qg, count = call(
        chunk_kernel,
        [keep_qg, core_qg, far_qg, swap(far_qg, 1)],
        [shape((TEAM * own, 2 * mine), BF16), shape((TEAM, LANES), F32)],
    )
    for mask in middle:
        qg = jnp.concatenate([qg, swap(qg, mask)], axis=0)
    qg, w_key, w_value = lax.optimization_barrier((qg, w_key, w_value))
    far_qg = swap(qg, far_bit)
    qg = [qg, swap(qg, near_bit), far_qg]
    (weights,) = call(weights_kernel, [w_key, w_value], [shape((TEAM, 2 * mine, width), BF16)])
    turned = [shape((2, 2 * mine, slots), BF16)]
    (near_t,) = call(functools.partial(turn_kernel, ((0, None), (1, None))), [keep, core], turned)
    near_t, weights = lax.optimization_barrier((near_t, weights))
    rows = qg[0].shape[0]
    team_slots = TEAM * slots
    work = 2 * rows * team_slots * mine

    def forward(p, blocks, before=()):
        return call(
            functools.partial(forward_kernel, blocks),
            [count, qg[p]]
            + ([keep, core, near_t] if 0 in blocks else [])
            + ([far, diagonal, far_t] if 2 in blocks else [])
            + list(before),
            [shape((mine, rows), F32), shape((4 * MINE, rows), F32)],
            [pltpu.VMEM((3, slots, rows), F32), pltpu.VMEM((3, slots, rows), BF16)],
            flops=2 * work * len(blocks),
            exps=rows * slots * len(blocks) * MINE,
        )

    early = [forward(p, (0, 1)) for p in range(2)]
    early, far, qg[2] = lax.optimization_barrier((early, far, qg[2]))
    qg.append(swap(qg[2], near_bit))
    diagonal = swap(far, 1)
    (far_t,) = call(functools.partial(turn_kernel, ((0, 0), (1, 1))), [far, diagonal], turned)
    done = [forward(p, (2, 3), early[p]) for p in range(2)]
    done += [forward(p, (0, 1, 2, 3)) for p in (2, 3)]
    numer = [d[0] for d in done]
    tops = [d[1][:MINE] for d in done]
    stats = [d[1][2 * MINE :] for d in done]

    def merge(*parts):
        lse = [p[..., :MINE, :] for p in parts]
        top = functools.reduce(jnp.maximum, lse)
        scale = [jnp.exp(x - top) for x in lse]
        total = sum(scale)
        delta = sum(s * p[..., MINE:, :] for s, p in zip(scale, parts)) / total
        return jnp.concatenate([top + jnp.log(total), delta], axis=-2)

    stat = jnp.stack(stats)
    for mask, turn in ((near_bit, 1), (far_bit, 2)):
        came = swap(stat, mask)
        stat = merge(stat, jnp.stack([came[q ^ turn] for q in range(4)]))
    final = [stat[q] for q in range(4)]
    if middle:
        final = stat
        for mask in reversed(middle):
            half = final.shape[-1] // 2
            final = merge(final[..., :half], swap(final[..., half:], mask))
        for mask in middle:
            final = jnp.concatenate([final, swap(final, mask)], axis=-1)
        final = [final[q] for q in range(4)]

    def add(array, came):
        return array.astype(F32) + came.astype(F32)

    def scaled(p):
        scale = jnp.exp(tops[p] - final[p][:MINE])
        return (numer[p].reshape(MINE, -1, rows) * scale[:, None, :]).reshape(mine, rows)

    order = (3, 2, 1, 0)

    def backward(chunks, side, kind, sums=(), partial=(), last=False):
        kept = (2, slots, 2 * mine)
        return call(
            functools.partial(
                backward_kernel, len(chunks), order.index(chunks[0]), side, not sums, last
            ),
            [count]
            + [qg[p] for p in chunks]
            + [final[p] for p in chunks]
            + ([far, diagonal, far_t] if side else [keep, core, near_t])
            + list(sums)
            + list(partial),
            [shape((len(chunks), mine, rows), kind), shape(kept, BF16 if last else F32)],
            [pltpu.VMEM(kept if len(chunks) > 1 else (1, 8, LANES), F32)]
            + [pltpu.VMEM((2, slots, rows), F32)] * 2
            + [pltpu.VMEM((2, slots, rows), BF16)] * 2,
            flops=7 * work * len(chunks),
            exps=rows * team_slots // 2 * MINE * len(chunks),
        )

    came_a = swap(jnp.stack([scaled(3), scaled(2)]).astype(BF16), far_bit)
    partial, gkv_far = backward(order, 1, F32, last=True)
    came_a, partial = lax.optimization_barrier((came_a, partial))
    came_far = swap(gkv_far, 2)
    near_a = swap(add(scaled(1), came_a[0]).astype(BF16), near_bit)
    gq, total = backward((3,), 0, BF16, partial=[partial])
    came = swap(gq[0], near_bit)
    gq, total = backward((2,), 0, F32, [total], [partial])
    sent, total = lax.optimization_barrier((add(gq[0], came).astype(BF16), total))
    far_q = swap(sent, far_bit)
    gq, total = backward((1,), 0, BF16, [total], [partial])
    near_q = swap(gq[0], near_bit)
    came_far, far_q, total = lax.optimization_barrier((came_far, far_q, total))
    gq, gkv_near = backward((0,), 0, F32, [total], [partial], True)
    attended = add(add(scaled(0), near_a), came_a[1])
    grad_query = add(add(gq[0], near_q), far_q)

    both = jnp.stack([attended, grad_query])
    for mask in reversed(middle):
        half = both.shape[-1] // 2
        both = add(both[..., :half], swap(both[..., half:].astype(BF16), mask))
    both, came_far = lax.optimization_barrier((both.astype(BF16), came_far))
    far_both = swap(both[..., 2 * own :], 2)
    near_both = both[..., : 2 * own]

    core_gkv = swap(jnp.stack([gkv_near[1], came_far[1]]), 1)
    (d_points,) = call(
        points_kernel,
        [place, gkv_near, came_far, core_gkv, weights],
        [shape((slots, width), BF16)],
        flops=4 * slots * width * width,
    )
    far_both, d_points = lax.optimization_barrier((far_both, d_points))
    core_both = swap(jnp.stack([near_both[..., own:], far_both[..., own:]]), 1)
    result, d_latents = call(
        queries_kernel,
        [place, near_both, far_both, core_both, latents, d_out, w_out, w_query],
        [shape((own, width), BF16)] * 2,
        [pltpu.VMEM((width, own), F32)],
        flops=4 * own * width * width,
    )
    return (result, d_latents, d_points)


def solution(mesh):
    part = P(("groups", "pts"), None)
    in_specs = (part, part, P(("groups", "pts")), P(), P(), P(), P(), part)
    return jax.shard_map(
        functools.partial(body, mesh.shape["pts"]),
        mesh=mesh,
        in_specs=in_specs,
        out_specs=(part, part, part),
        check_vma=False,
    )
```

```python
import functools

import jax
import jax.numpy as jnp
from jax import lax
from jax.experimental import pallas as pl
from jax.experimental.pallas import tpu as pltpu
from jax.sharding import PartitionSpec as P

HEADS = 12
TEAM = 4
MINE = HEADS // TEAM
BF16 = jnp.bfloat16
F32 = jnp.float32
LANES = 128
NT = (((1,), (1,)), ((), ()))


def dot(a, b):
    return jnp.dot(a, b, preferred_element_type=F32)


def dot_nt(a, b):
    return lax.dot_general(a, b, NT, preferred_element_type=F32)


def low_lanes(shape):
    return lax.broadcasted_iota(jnp.int32, shape, 1) < shape[1] // 2


def lanes_of(part):
    start = part // 2 * LANES
    return slice(start, start + LANES)


def keep_part(array, part):
    low = low_lanes(array.shape)
    return jnp.where(low if part % 2 == 0 else ~low, array, jnp.zeros_like(array))


def store_quarters(place_ref, near_refs, far_ref, one, two, at):
    mine = one.shape[1] // TEAM
    for quarter in range(TEAM):
        cols = slice(quarter * mine, (quarter + 1) * mine)
        piece = jnp.concatenate([one[:, cols], two[:, cols]], axis=1)
        relative = (place_ref[0] % TEAM) ^ quarter
        for which, ref in enumerate(near_refs):

            @pl.when(relative == which)
            def _():
                ref[at, :] = piece

        @pl.when(relative >= 2)
        def _():
            far_ref[relative % 2, at, :] = piece


def load(source, target, sems, pieces):
    step = source.shape[0] // pieces
    copies = []
    for k in range(pieces):
        at = slice(k * step, (k + 1) * step)
        copies.append(pltpu.make_async_copy(source.at[at], target.at[at], sems.at[k]))
        copies[-1].start()
    return copies


def wait(*groups):
    for group in groups:
        for copy in group:
            copy.wait()


def rows_kernel(
    place_ref, count_ref, latents_hbm, d_out_hbm, w_query_hbm, w_out_hbm,
    keep_ref, core_ref, far_ref, latents_ref, d_out_ref, w_query_ref, w_out_ref, sems
):
    pieces = sems.shape[1]
    own = latents_ref.shape[0]
    loads = [
        load(latents_hbm, latents_ref, sems.at[0], 1),
        load(w_query_hbm, w_query_ref, sems.at[1], pieces),
        load(d_out_hbm, d_out_ref, sems.at[2], 1),
        load(w_out_hbm, w_out_ref, sems.at[3], pieces),
    ]
    extra = keep_ref.shape[0] - own, keep_ref.shape[1]
    first = lax.broadcasted_iota(jnp.int32, extra, 1) < extra[1] // 2
    count = jnp.where(first, count_ref[0] // 16, count_ref[0] % 16).astype(F32).astype(BF16)
    for ref in (keep_ref, core_ref, far_ref.at[0], far_ref.at[1]):
        ref[own:, :] = count
    wait(*loads[:2])
    query = dot(latents_ref[...], w_query_ref[...]).astype(BF16)
    wait(*loads[2:])
    grad = dot_nt(d_out_ref[...], w_out_ref[...]).astype(BF16)
    store_quarters(place_ref, (keep_ref, core_ref), far_ref, query, grad, slice(0, own))


def slots_kernel(place_ref, points_ref, w_key_ref, w_value_ref, keep_ref, core_ref, far_ref):
    keys = dot(points_ref[...], w_key_ref[...]).astype(BF16) * jnp.asarray(0.125, BF16)
    values = dot(points_ref[...], w_value_ref[...]).astype(BF16)
    store_quarters(place_ref, (keep_ref, core_ref), far_ref, keys, values, slice(0, keys.shape[0]))


def weights_kernel(w_key_ref, w_value_ref, out_ref):
    mine = out_ref.shape[1] // 2
    for i, ref in enumerate((w_key_ref, w_value_ref)):
        turned = ref[...].T
        for quarter in range(TEAM):
            out_ref[quarter, i * mine : (i + 1) * mine, :] = turned[quarter * mine : (quarter + 1) * mine]


def chunk_kernel(keep_ref, core_ref, far_ref, diagonal_ref, out_ref, count_ref):
    own, mine = out_ref.shape[0] // TEAM, out_ref.shape[1] // 2
    for i, ref in enumerate((keep_ref, core_ref, far_ref.at[0], diagonal_ref.at[1])):
        out_ref[i * own : (i + 1) * own, :] = ref[:own, :]
        row = ref[own:, :].astype(F32)[:1, :]
        count_ref[i : i + 1, :] = 16 * row[:, :LANES] + row[:, mine : mine + LANES]


def turn_kernel(picks, *refs):
    for i, (ref, which) in enumerate(picks):
        refs[-1][i] = (refs[ref][...] if which is None else refs[ref][which]).T


def dead_slots(slot, count_ref, block):
    count = jnp.concatenate([count_ref[block : block + 1, :]] * (slot.shape[1] // LANES), axis=1)
    return slot >= count


def forward_kernel(blocks, count_ref, qg_ref, *refs):
    kv_refs, kv_t_refs = {}, {}
    if 0 in blocks:
        keep_ref, core_ref, near_t_ref, *refs = refs
        kv_refs.update({0: keep_ref, 1: core_ref})
        kv_t_refs.update({0: near_t_ref.at[0], 1: near_t_ref.at[1]})
    if 2 in blocks:
        far_ref, diagonal_ref, far_t_ref, *refs = refs
        kv_refs.update({2: far_ref.at[0], 3: diagonal_ref.at[1]})
        kv_t_refs.update({2: far_t_ref.at[0], 3: far_t_ref.at[1]})
    before = refs[:2] if blocks[0] else ()
    numer_ref, stat_ref, score_ref, weight_ref = refs[len(before) :]
    rows = qg_ref.shape[0]
    slots = kv_refs[blocks[0]].shape[0]
    dim = qg_ref.shape[1] // (2 * MINE)
    depth = score_ref.shape[0]
    slot = lax.broadcasted_iota(jnp.int32, (slots, rows), 0).astype(F32)
    units = [(head, block) for head in range(MINE) for block in blocks]
    tops, totals, numers = {}, {}, {}

    def score(step):
        head, block = units[step]
        keys = keep_part(kv_refs[block][:, lanes_of(head)], head)
        score_ref[step % depth] = dot_nt(keys, qg_ref[:, lanes_of(head)])

    def weigh(step):
        dead = dead_slots(slot, count_ref, units[step][1])
        scores = jnp.where(dead, -jnp.inf, score_ref[step % depth])
        tops[step] = jnp.max(scores, axis=0, keepdims=True)
        weights = jnp.exp(scores - tops[step])
        totals[step] = jnp.sum(weights, axis=0, keepdims=True)
        weight_ref[step % depth] = weights.astype(BF16)

    def attend(step):
        head, block = units[step]
        part = MINE + head
        at = slice(part * dim, (part + 1) * dim)
        numers[step] = dot(kv_t_refs[block][at, :], weight_ref[step % depth])
        if block != blocks[-1]:
            return
        steps = list(range(step - len(blocks) + 1, step + 1))
        own_rows = slice(head * dim, (head + 1) * dim)
        if before:
            steps.append(-1)
            numers[-1] = before[0][own_rows, :]
            tops[-1] = before[1][head : head + 1, :]
            totals[-1] = before[1][MINE + head : MINE + head + 1, :]
        top = functools.reduce(jnp.maximum, [tops[s] for s in steps])
        scale = {s: jnp.exp(tops[s] - top) for s in steps}
        total = sum(scale[s] * totals[s] for s in steps)
        numer = sum(scale[s] * numers[s] for s in steps)
        numer_ref[own_rows, :] = numer
        half = part % 2 * dim
        grad_t = qg_ref[:, lanes_of(part)].astype(F32).T[half : half + dim, :]
        inner = jnp.sum(grad_t * numer, axis=0, keepdims=True)
        for i, row in enumerate((top, total, top + jnp.log(total), inner / total)):
            stat_ref[i * MINE + head : i * MINE + head + 1, :] = row

    for step in range(len(units) + 2):
        if step < len(units):
            score(step)
        if 0 <= step - 1 < len(units):
            weigh(step - 1)
        if 0 <= step - 2:
            attend(step - 2)


def backward_kernel(chunks, start, side, first, last, count_ref, *refs):
    qg_refs, stat_refs, refs = refs[:chunks], refs[chunks : 2 * chunks], refs[2 * chunks :]
    even_ref, odd_ref, kv_t_ref, *refs = refs
    kv_refs = (even_ref.at[0], odd_ref.at[1]) if side else (even_ref, odd_ref)
    if not first:
        sum_in_ref, *refs = refs
    gq_in_ref = None
    if side == 0:
        gq_in_ref, *refs = refs
    gq_ref, sum_ref, total_ref, score_ref, gw_ref, prob_ref, ds_ref = refs
    rows = qg_refs[0].shape[0]
    slots, dim = even_ref.shape[-2], even_ref.shape[-1] // (2 * MINE)
    depth = score_ref.shape[0]
    slot = lax.broadcasted_iota(jnp.int32, (slots, rows), 0).astype(F32)
    low = low_lanes((slots, LANES))
    units = [(c, head, block) for c in range(chunks) for block in range(2) for head in range(MINE)]
    gq, held = {}, {}

    def product(chunk, block, part):
        return dot_nt(keep_part(kv_refs[block][:, lanes_of(part)], part), qg_refs[chunk][:, lanes_of(part)])

    def score(step):
        chunk, head, block = units[step]
        score_ref[step % depth] = product(chunk, block, head)
        gw_ref[step % depth] = product(chunk, block, MINE + head)

    def weigh(step):
        chunk, head, block = units[step]
        dead = dead_slots(slot, count_ref, 2 * side + block)
        scores = jnp.where(dead, -jnp.inf, score_ref[step % depth])
        prob = jnp.exp(scores - stat_refs[chunk][head : head + 1, :])
        delta = stat_refs[chunk][MINE + head : MINE + head + 1, :]
        prob_ref[step % depth] = prob.astype(BF16)
        ds_ref[step % depth] = (prob * (gw_ref[step % depth] - delta)).astype(BF16)

    def store(chunk, block, part, value):
        held[part] = value
        pair = part // 2 * 2, part // 2 * 2 + 1
        if not all(p in held for p in pair):
            return
        at = block, slice(0, slots), lanes_of(part)
        total = jnp.where(low, held.pop(pair[0]), held.pop(pair[1]))
        if chunk > 0:
            total += total_ref[at]
        elif not first:
            total += sum_in_ref[at]
        if chunk < chunks - 1:
            total_ref[at] = total
            return
        if last:
            scales = [0.125 if p < MINE else 1.0 for p in pair]
            total *= scales[0] if scales[0] == scales[1] else jnp.where(low, *scales)
        sum_ref[at] = total.astype(sum_ref.dtype)

    def collect(step):
        chunk, head, block = units[step]
        qg_ref = qg_refs[chunk]
        store(chunk, block, head, dot(ds_ref[step % depth], qg_ref[:, lanes_of(head)]))
        store(chunk, block, MINE + head, dot(prob_ref[step % depth], qg_ref[:, lanes_of(MINE + head)]))
        at = slice(head * dim, (head + 1) * dim)
        term = dot(kv_t_ref[block, at, :], ds_ref[step % depth])
        if block == 0:
            gq[head] = term if gq_in_ref is None else term + gq_in_ref[start + chunk, at, :]
        else:
            gq_ref[chunk, at, :] = (gq[head] + term).astype(gq_ref.dtype)

    for step in range(len(units) + 2):
        if 0 <= step - 2:
            collect(step - 2)
        if 0 <= step - 1 < len(units):
            weigh(step - 1)
        if step < len(units):
            score(step)


def queries_kernel(place_ref, *refs):
    pieces, refs = refs[:TEAM], refs[TEAM:]
    latents_ref, d_out_ref, w_out_ref, w_query_ref, result_ref, d_latents_ref, joined_ref = refs
    mine = pieces[0].shape[1]
    for kind in range(2):
        for relative in range(TEAM):
            quarter = (place_ref[0] % TEAM) ^ relative
            piece = pieces[relative][kind]
            joined_ref[pl.ds(pl.multiple_of(quarter * mine, mine), mine), :] = piece.astype(F32)
        joined = joined_ref[...].T.astype(BF16)
        if kind == 0:
            result_ref[...] = (latents_ref[...].astype(F32) + dot(joined, w_out_ref[...])).astype(BF16)
        else:
            d_latents_ref[...] = (
                d_out_ref[...].astype(F32) + dot_nt(joined, w_query_ref[...])
            ).astype(BF16)


def points_kernel(place_ref, near_ref, far_ref, core_ref, weight_ref, out_ref):
    total = None
    for relative in range(TEAM):
        core, across = relative % 2, relative // 2
        piece = core_ref[across] if core else (near_ref, far_ref)[across][0]
        term = dot(piece, weight_ref[(place_ref[0] % TEAM) ^ relative])
        total = term if total is None else total + term
    out_ref[...] = total.astype(BF16)


def call(kernel, ins, out_shapes, scratch=(), flops=0, exps=0, space=pltpu.VMEM, grant=40):
    vmem = pl.BlockSpec(memory_space=pltpu.VMEM)
    other = pl.BlockSpec(memory_space=space)
    smem = pl.BlockSpec(memory_space=pltpu.SMEM)
    moved = sum(a.size * a.dtype.itemsize for a in list(ins) + list(out_shapes))
    return pl.pallas_call(
        kernel,
        in_specs=[smem if a.dtype == jnp.int32 else other for a in ins],
        out_specs=[vmem] * len(out_shapes),
        out_shape=out_shapes,
        scratch_shapes=scratch,
        compiler_params=pltpu.CompilerParams(vmem_limit_bytes=grant << 20),
        cost_estimate=pl.CostEstimate(flops=flops // 8, transcendentals=exps // 8, bytes_accessed=moved // 8),
    )(*ins)


def body(size, latents, points, counts, w_query, w_key, w_value, w_out, d_out):
    own, width = latents.shape
    slots = points.shape[0]
    mine = width // TEAM
    shape = jax.ShapeDtypeStruct
    near_bit, far_bit = size // 4, size // 2
    middle = []
    bit = size // 8
    while bit >= TEAM:
        middle.append(bit)
        bit //= 2
    place = lax.axis_index("pts").astype(jnp.int32).reshape(1)

    def swap(array, mask):
        return lax.ppermute(array, "pts", [(i, i ^ mask) for i in range(size)])

    def pieces(rows):
        return [shape((rows, 2 * mine), BF16)] * 2 + [shape((2, rows, 2 * mine), BF16)]

    inputs = [latents, d_out, w_query, w_out]
    keep_qg, core_qg, far_qg = call(
        rows_kernel,
        [place, counts] + inputs,
        pieces(own + 16),
        [pltpu.VMEM(a.shape, BF16) for a in inputs] + [pltpu.SemaphoreType.DMA((len(inputs), 4))],
        flops=4 * own * width * width,
        space=pltpu.HBM,
        grant=60,
    )
    keep_qg, then_place = lax.optimization_barrier((keep_qg, place))
    far_qg = swap(far_qg, 2)
    core_qg = swap(core_qg, 1)
    keep, core, far = call(
        slots_kernel, [then_place, points, w_key, w_value], pieces(slots), flops=4 * slots * width * width
    )
    far_qg, far = lax.optimization_barrier((far_qg, far))
    far = swap(far, 2)
    core = swap(core, 1)
    qg, count = call(
        chunk_kernel,
        [keep_qg, core_qg, far_qg, swap(far_qg, 1)],
        [shape((TEAM * own, 2 * mine), BF16), shape((TEAM, LANES), F32)],
    )
    for mask in middle:
        qg = jnp.concatenate([qg, swap(qg, mask)], axis=0)
    qg, w_key, w_value = lax.optimization_barrier((qg, w_key, w_value))
    far_qg = swap(qg, far_bit)
    qg = [qg, swap(qg, near_bit), far_qg]
    (weights,) = call(weights_kernel, [w_key, w_value], [shape((TEAM, 2 * mine, width), BF16)])
    turned = [shape((2, 2 * mine, slots), BF16)]
    (near_t,) = call(functools.partial(turn_kernel, ((0, None), (1, None))), [keep, core], turned)
    near_t, weights = lax.optimization_barrier((near_t, weights))
    rows = qg[0].shape[0]
    team_slots = TEAM * slots
    work = 2 * rows * team_slots * mine

    def forward(p, blocks, before=()):
        return call(
            functools.partial(forward_kernel, blocks),
            [count, qg[p]]
            + ([keep, core, near_t] if 0 in blocks else [])
            + ([far, diagonal, far_t] if 2 in blocks else [])
            + list(before),
            [shape((mine, rows), F32), shape((4 * MINE, rows), F32)],
            [pltpu.VMEM((3, slots, rows), F32), pltpu.VMEM((3, slots, rows), BF16)],
            flops=2 * work * len(blocks),
            exps=rows * slots * len(blocks) * MINE,
        )

    early = [forward(p, (0, 1)) for p in range(2)]
    early, far, qg[2] = lax.optimization_barrier((early, far, qg[2]))
    qg.append(swap(qg[2], near_bit))
    diagonal = swap(far, 1)
    (far_t,) = call(functools.partial(turn_kernel, ((0, 0), (1, 1))), [far, diagonal], turned)
    done = [forward(p, (2, 3), early[p]) for p in range(2)]
    done += [forward(p, (0, 1, 2, 3)) for p in (2, 3)]
    numer = [d[0] for d in done]
    tops = [d[1][:MINE] for d in done]
    stats = [d[1][2 * MINE :] for d in done]

    def merge(*parts):
        lse = [p[..., :MINE, :] for p in parts]
        top = functools.reduce(jnp.maximum, lse)
        scale = [jnp.exp(x - top) for x in lse]
        total = sum(scale)
        delta = sum(s * p[..., MINE:, :] for s, p in zip(scale, parts)) / total
        return jnp.concatenate([top + jnp.log(total), delta], axis=-2)

    stat = jnp.stack(stats)
    for mask, turn in ((near_bit, 1), (far_bit, 2)):
        came = swap(stat, mask)
        stat = merge(stat, jnp.stack([came[q ^ turn] for q in range(4)]))
    final = [stat[q] for q in range(4)]
    if middle:
        final = stat
        for mask in reversed(middle):
            half = final.shape[-1] // 2
            final = merge(final[..., :half], swap(final[..., half:], mask))
        for mask in middle:
            final = jnp.concatenate([final, swap(final, mask)], axis=-1)
        final = [final[q] for q in range(4)]

    def add(array, came):
        return array.astype(F32) + came.astype(F32)

    def scaled(p):
        scale = jnp.exp(tops[p] - final[p][:MINE])
        return (numer[p].reshape(MINE, -1, rows) * scale[:, None, :]).reshape(mine, rows)

    order = (3, 2, 1, 0)

    def backward(chunks, side, kind, sums=(), partial=(), last=False):
        kept = (2, slots, 2 * mine)
        return call(
            functools.partial(
                backward_kernel, len(chunks), order.index(chunks[0]), side, not sums, last
            ),
            [count]
            + [qg[p] for p in chunks]
            + [final[p] for p in chunks]
            + ([far, diagonal, far_t] if side else [keep, core, near_t])
            + list(sums)
            + list(partial),
            [shape((len(chunks), mine, rows), kind), shape(kept, BF16 if last else F32)],
            [pltpu.VMEM(kept if len(chunks) > 1 else (1, 8, LANES), F32)]
            + [pltpu.VMEM((2, slots, rows), F32)] * 2
            + [pltpu.VMEM((2, slots, rows), BF16)] * 2,
            flops=7 * work * len(chunks),
            exps=rows * team_slots // 2 * MINE * len(chunks),
        )

    came_a = swap(jnp.stack([scaled(3), scaled(2)]).astype(BF16), far_bit)
    partial, gkv_far = backward(order, 1, F32, last=True)
    came_a, partial = lax.optimization_barrier((came_a, partial))
    came_far = swap(gkv_far, 2)
    gq, total = backward((3,), 0, BF16, partial=[partial])
    came, near_a = swap(jnp.stack([gq[0], add(scaled(1), came_a[0]).astype(BF16)]), near_bit)
    gq, total = backward((2,), 0, F32, [total], [partial])
    sent, total = lax.optimization_barrier((add(gq[0], came).astype(BF16), total))
    far_q = swap(sent, far_bit)
    gq, total = backward((1,), 0, BF16, [total], [partial])
    near_q = swap(gq[0], near_bit)
    came_far, far_q, total = lax.optimization_barrier((came_far, far_q, total))
    gq, gkv_near = backward((0,), 0, F32, [total], [partial], True)
    attended = add(add(scaled(0), near_a), came_a[1])
    grad_query = add(add(gq[0], near_q), far_q)

    both = jnp.stack([attended, grad_query])
    for mask in reversed(middle):
        half = both.shape[-1] // 2
        both = add(both[..., :half], swap(both[..., half:].astype(BF16), mask))
    both, came_far = lax.optimization_barrier((both.astype(BF16), came_far))
    pieces_both = [both[..., i * own : (i + 1) * own] for i in range(TEAM)]
    pieces_both[1:] = [swap(pieces_both[i], i) for i in range(1, TEAM)]

    core_gkv = swap(jnp.stack([gkv_near[1], came_far[1]]), 1)
    (d_points,) = call(
        points_kernel,
        [place, gkv_near, came_far, core_gkv, weights],
        [shape((slots, width), BF16)],
        flops=4 * slots * width * width,
    )
    *pieces_both, d_points = lax.optimization_barrier((*pieces_both, d_points))
    result, d_latents = call(
        queries_kernel,
        [place] + pieces_both + [latents, d_out, w_out, w_query],
        [shape((own, width), BF16)] * 2,
        [pltpu.VMEM((width, own), F32)],
        flops=4 * own * width * width,
    )
    return (result, d_latents, d_points)


def solution(mesh):
    part = P(("groups", "pts"), None)
    in_specs = (part, part, P(("groups", "pts")), P(), P(), P(), P(), part)
    return jax.shard_map(
        functools.partial(body, mesh.shape["pts"]),
        mesh=mesh,
        in_specs=in_specs,
        out_specs=(part, part, part),
        check_vma=False,
    )
```

```python
import functools

import jax
import jax.numpy as jnp
from jax import lax
from jax.experimental import pallas as pl
from jax.experimental.pallas import tpu as pltpu
from jax.sharding import PartitionSpec as P

HEADS = 12
TEAM = 4
MINE = HEADS // TEAM
BF16 = jnp.bfloat16
F32 = jnp.float32
LANES = 128
NT = (((1,), (1,)), ((), ()))


def dot(a, b):
    return jnp.dot(a, b, preferred_element_type=F32)


def dot_nt(a, b):
    return lax.dot_general(a, b, NT, preferred_element_type=F32)


def low_lanes(shape):
    return lax.broadcasted_iota(jnp.int32, shape, 1) < shape[1] // 2


def lanes_of(part):
    start = part // 2 * LANES
    return slice(start, start + LANES)


def keep_part(array, part):
    low = low_lanes(array.shape)
    return jnp.where(low if part % 2 == 0 else ~low, array, jnp.zeros_like(array))


def store_quarters(place_ref, near_refs, far_ref, one, two, at):
    mine = one.shape[1] // TEAM
    for quarter in range(TEAM):
        cols = slice(quarter * mine, (quarter + 1) * mine)
        piece = jnp.concatenate([one[:, cols], two[:, cols]], axis=1)
        relative = (place_ref[0] % TEAM) ^ quarter
        for which, ref in enumerate(near_refs):

            @pl.when(relative == which)
            def _():
                ref[at, :] = piece

        if far_ref is None:
            continue

        @pl.when(relative >= 2)
        def _():
            far_ref[relative % 2, at, :] = piece


def load(source, target, sems, pieces):
    step = source.shape[0] // pieces
    copies = []
    for k in range(pieces):
        at = slice(k * step, (k + 1) * step)
        copies.append(pltpu.make_async_copy(source.at[at], target.at[at], sems.at[k]))
        copies[-1].start()
    return copies


def wait(*groups):
    for group in groups:
        for copy in group:
            copy.wait()


def rows_kernel(
    place_ref, count_ref, latents_hbm, d_out_hbm, w_query_hbm, w_out_hbm,
    keep_ref, core_ref, far_ref, latents_ref, d_out_ref, w_query_ref, w_out_ref, sems
):
    pieces = sems.shape[1]
    own = latents_ref.shape[0]
    loads = [
        load(latents_hbm, latents_ref, sems.at[0], 1),
        load(w_query_hbm, w_query_ref, sems.at[1], pieces),
        load(d_out_hbm, d_out_ref, sems.at[2], 1),
        load(w_out_hbm, w_out_ref, sems.at[3], pieces),
    ]
    extra = keep_ref.shape[0] - own, keep_ref.shape[1]
    first = lax.broadcasted_iota(jnp.int32, extra, 1) < extra[1] // 2
    count = jnp.where(first, count_ref[0] // 16, count_ref[0] % 16).astype(F32).astype(BF16)
    for ref in (keep_ref, core_ref, far_ref.at[0], far_ref.at[1]):
        ref[own:, :] = count
    wait(*loads[:2])
    query = dot(latents_ref[...], w_query_ref[...]).astype(BF16)
    wait(*loads[2:])
    grad = dot_nt(d_out_ref[...], w_out_ref[...]).astype(BF16)
    store_quarters(place_ref, (keep_ref, core_ref), far_ref, query, grad, slice(0, own))


def slots_kernel(place_ref, points_ref, w_key_ref, w_value_ref, *piece_refs):
    keys = dot(points_ref[...], w_key_ref[...]).astype(BF16) * jnp.asarray(0.125, BF16)
    values = dot(points_ref[...], w_value_ref[...]).astype(BF16)
    store_quarters(place_ref, piece_refs, None, keys, values, slice(0, keys.shape[0]))


def weights_kernel(w_key_ref, w_value_ref, out_ref):
    mine = out_ref.shape[1] // 2
    for i, ref in enumerate((w_key_ref, w_value_ref)):
        turned = ref[...].T
        for quarter in range(TEAM):
            out_ref[quarter, i * mine : (i + 1) * mine, :] = turned[quarter * mine : (quarter + 1) * mine]


def chunk_kernel(keep_ref, core_ref, far_ref, diagonal_ref, out_ref, count_ref):
    own, mine = out_ref.shape[0] // TEAM, out_ref.shape[1] // 2
    for i, ref in enumerate((keep_ref, core_ref, far_ref.at[0], diagonal_ref.at[1])):
        out_ref[i * own : (i + 1) * own, :] = ref[:own, :]
        row = ref[own:, :].astype(F32)[:1, :]
        count_ref[i : i + 1, :] = 16 * row[:, :LANES] + row[:, mine : mine + LANES]


def turn_kernel(picks, *refs):
    for i, (ref, which) in enumerate(picks):
        refs[-1][i] = (refs[ref][...] if which is None else refs[ref][which]).T


def dead_slots(slot, count_ref, block):
    count = jnp.concatenate([count_ref[block : block + 1, :]] * (slot.shape[1] // LANES), axis=1)
    return slot >= count


def forward_kernel(blocks, count_ref, qg_ref, *refs):
    kv_refs, kv_t_refs = {}, {}
    if 0 in blocks:
        keep_ref, core_ref, near_t_ref, *refs = refs
        kv_refs.update({0: keep_ref, 1: core_ref})
        kv_t_refs.update({0: near_t_ref.at[0], 1: near_t_ref.at[1]})
    if 2 in blocks:
        far_ref, diagonal_ref, far_t_ref, *refs = refs
        kv_refs.update({2: far_ref, 3: diagonal_ref})
        kv_t_refs.update({2: far_t_ref.at[0], 3: far_t_ref.at[1]})
    before = refs[:2] if blocks[0] else ()
    numer_ref, stat_ref, score_ref, weight_ref = refs[len(before) :]
    rows = qg_ref.shape[0]
    slots = kv_refs[blocks[0]].shape[0]
    dim = qg_ref.shape[1] // (2 * MINE)
    depth = score_ref.shape[0]
    slot = lax.broadcasted_iota(jnp.int32, (slots, rows), 0).astype(F32)
    units = [(head, block) for head in range(MINE) for block in blocks]
    tops, totals, numers = {}, {}, {}

    def score(step):
        head, block = units[step]
        keys = keep_part(kv_refs[block][:, lanes_of(head)], head)
        score_ref[step % depth] = dot_nt(keys, qg_ref[:, lanes_of(head)])

    def weigh(step):
        dead = dead_slots(slot, count_ref, units[step][1])
        scores = jnp.where(dead, -jnp.inf, score_ref[step % depth])
        tops[step] = jnp.max(scores, axis=0, keepdims=True)
        weights = jnp.exp(scores - tops[step])
        totals[step] = jnp.sum(weights, axis=0, keepdims=True)
        weight_ref[step % depth] = weights.astype(BF16)

    def attend(step):
        head, block = units[step]
        part = MINE + head
        at = slice(part * dim, (part + 1) * dim)
        numers[step] = dot(kv_t_refs[block][at, :], weight_ref[step % depth])
        if block != blocks[-1]:
            return
        steps = list(range(step - len(blocks) + 1, step + 1))
        own_rows = slice(head * dim, (head + 1) * dim)
        if before:
            steps.append(-1)
            numers[-1] = before[0][own_rows, :]
            tops[-1] = before[1][head : head + 1, :]
            totals[-1] = before[1][MINE + head : MINE + head + 1, :]
        top = functools.reduce(jnp.maximum, [tops[s] for s in steps])
        scale = {s: jnp.exp(tops[s] - top) for s in steps}
        total = sum(scale[s] * totals[s] for s in steps)
        numer = sum(scale[s] * numers[s] for s in steps)
        numer_ref[own_rows, :] = numer
        half = part % 2 * dim
        grad_t = qg_ref[:, lanes_of(part)].astype(F32).T[half : half + dim, :]
        inner = jnp.sum(grad_t * numer, axis=0, keepdims=True)
        for i, row in enumerate((top, total, top + jnp.log(total), inner / total)):
            stat_ref[i * MINE + head : i * MINE + head + 1, :] = row

    for step in range(len(units) + 2):
        if step < len(units):
            score(step)
        if 0 <= step - 1 < len(units):
            weigh(step - 1)
        if 0 <= step - 2:
            attend(step - 2)


def backward_kernel(chunks, start, side, first, last, count_ref, *refs):
    qg_refs, stat_refs, refs = refs[:chunks], refs[chunks : 2 * chunks], refs[2 * chunks :]
    even_ref, odd_ref, kv_t_ref, *refs = refs
    kv_refs = even_ref, odd_ref
    if not first:
        sum_in_ref, *refs = refs
    gq_in_ref = None
    if side == 0:
        gq_in_ref, *refs = refs
    gq_ref, sum_ref, total_ref, score_ref, gw_ref, prob_ref, ds_ref = refs
    rows = qg_refs[0].shape[0]
    slots, dim = even_ref.shape[-2], even_ref.shape[-1] // (2 * MINE)
    depth = score_ref.shape[0]
    slot = lax.broadcasted_iota(jnp.int32, (slots, rows), 0).astype(F32)
    low = low_lanes((slots, LANES))
    units = [(c, head, block) for c in range(chunks) for block in range(2) for head in range(MINE)]
    gq, held = {}, {}

    def product(chunk, block, part):
        return dot_nt(keep_part(kv_refs[block][:, lanes_of(part)], part), qg_refs[chunk][:, lanes_of(part)])

    def score(step):
        chunk, head, block = units[step]
        score_ref[step % depth] = product(chunk, block, head)
        gw_ref[step % depth] = product(chunk, block, MINE + head)

    def weigh(step):
        chunk, head, block = units[step]
        dead = dead_slots(slot, count_ref, 2 * side + block)
        scores = jnp.where(dead, -jnp.inf, score_ref[step % depth])
        prob = jnp.exp(scores - stat_refs[chunk][head : head + 1, :])
        delta = stat_refs[chunk][MINE + head : MINE + head + 1, :]
        prob_ref[step % depth] = prob.astype(BF16)
        ds_ref[step % depth] = (prob * (gw_ref[step % depth] - delta)).astype(BF16)

    def store(chunk, block, part, value):
        held[part] = value
        pair = part // 2 * 2, part // 2 * 2 + 1
        if not all(p in held for p in pair):
            return
        at = block, slice(0, slots), lanes_of(part)
        total = jnp.where(low, held.pop(pair[0]), held.pop(pair[1]))
        if chunk > 0:
            total += total_ref[at]
        elif not first:
            total += sum_in_ref[at]
        if chunk < chunks - 1:
            total_ref[at] = total
            return
        if last:
            scales = [0.125 if p < MINE else 1.0 for p in pair]
            total *= scales[0] if scales[0] == scales[1] else jnp.where(low, *scales)
        sum_ref[at] = total.astype(sum_ref.dtype)

    def collect(step):
        chunk, head, block = units[step]
        qg_ref = qg_refs[chunk]
        store(chunk, block, head, dot(ds_ref[step % depth], qg_ref[:, lanes_of(head)]))
        store(chunk, block, MINE + head, dot(prob_ref[step % depth], qg_ref[:, lanes_of(MINE + head)]))
        at = slice(head * dim, (head + 1) * dim)
        term = dot(kv_t_ref[block, at, :], ds_ref[step % depth])
        if block == 0:
            gq[head] = term if gq_in_ref is None else term + gq_in_ref[start + chunk, at, :]
        else:
            gq_ref[chunk, at, :] = (gq[head] + term).astype(gq_ref.dtype)

    for step in range(len(units) + 2):
        if 0 <= step - 2:
            collect(step - 2)
        if 0 <= step - 1 < len(units):
            weigh(step - 1)
        if step < len(units):
            score(step)


def queries_kernel(
    place_ref, near_ref, far_ref, core_ref, latents_ref, d_out_ref, w_out_ref, w_query_ref,
    result_ref, d_latents_ref, joined_ref
):
    own = latents_ref.shape[0]
    mine = near_ref.shape[1]
    for kind in range(2):
        for relative in range(TEAM):
            core, across = relative % 2, relative // 2
            quarter = (place_ref[0] % TEAM) ^ relative
            piece = core_ref[across, kind] if core else (near_ref, far_ref)[across][kind, :, :own]
            joined_ref[pl.ds(pl.multiple_of(quarter * mine, mine), mine), :] = piece.astype(F32)
        joined = joined_ref[...].T.astype(BF16)
        if kind == 0:
            result_ref[...] = (latents_ref[...].astype(F32) + dot(joined, w_out_ref[...])).astype(BF16)
        else:
            d_latents_ref[...] = (
                d_out_ref[...].astype(F32) + dot_nt(joined, w_query_ref[...])
            ).astype(BF16)


def points_kernel(place_ref, near_ref, far_ref, core_ref, weight_ref, out_ref):
    total = None
    for relative in range(TEAM):
        core, across = relative % 2, relative // 2
        piece = core_ref[across] if core else (near_ref, far_ref)[across][0]
        term = dot(piece, weight_ref[(place_ref[0] % TEAM) ^ relative])
        total = term if total is None else total + term
    out_ref[...] = total.astype(BF16)


def call(kernel, ins, out_shapes, scratch=(), flops=0, exps=0, space=pltpu.VMEM, grant=40):
    vmem = pl.BlockSpec(memory_space=pltpu.VMEM)
    other = pl.BlockSpec(memory_space=space)
    smem = pl.BlockSpec(memory_space=pltpu.SMEM)
    moved = sum(a.size * a.dtype.itemsize for a in list(ins) + list(out_shapes))
    return pl.pallas_call(
        kernel,
        in_specs=[smem if a.dtype == jnp.int32 else other for a in ins],
        out_specs=[vmem] * len(out_shapes),
        out_shape=out_shapes,
        scratch_shapes=scratch,
        compiler_params=pltpu.CompilerParams(vmem_limit_bytes=grant << 20),
        cost_estimate=pl.CostEstimate(flops=flops // 8, transcendentals=exps // 8, bytes_accessed=moved // 8),
    )(*ins)


def body(size, latents, points, counts, w_query, w_key, w_value, w_out, d_out):
    own, width = latents.shape
    slots = points.shape[0]
    mine = width // TEAM
    shape = jax.ShapeDtypeStruct
    near_bit, far_bit = size // 4, size // 2
    middle = []
    bit = size // 8
    while bit >= TEAM:
        middle.append(bit)
        bit //= 2
    place = lax.axis_index("pts").astype(jnp.int32).reshape(1)

    def swap(array, mask):
        return lax.ppermute(array, "pts", [(i, i ^ mask) for i in range(size)])

    def pieces(rows):
        return [shape((rows, 2 * mine), BF16)] * 2 + [shape((2, rows, 2 * mine), BF16)]

    inputs = [latents, d_out, w_query, w_out]
    keep_qg, core_qg, far_qg = call(
        rows_kernel,
        [place, counts] + inputs,
        pieces(own + 16),
        [pltpu.VMEM(a.shape, BF16) for a in inputs] + [pltpu.SemaphoreType.DMA((len(inputs), 4))],
        flops=4 * own * width * width,
        space=pltpu.HBM,
        grant=60,
    )
    keep_qg, then_place = lax.optimization_barrier((keep_qg, place))
    far_qg = swap(far_qg, 2)
    core_qg = swap(core_qg, 1)
    keep, core, far, diagonal = call(
        slots_kernel, [then_place, points, w_key, w_value], [shape((slots, 2 * mine), BF16)] * 4, flops=4 * slots * width * width
    )
    far_qg, diagonal = lax.optimization_barrier((far_qg, diagonal))
    diagonal = swap(diagonal, 2)
    far = swap(far, 2)
    core = swap(core, 1)
    qg, count = call(
        chunk_kernel,
        [keep_qg, core_qg, far_qg, swap(far_qg, 1)],
        [shape((TEAM * own, 2 * mine), BF16), shape((TEAM, LANES), F32)],
    )
    for mask in middle:
        qg = jnp.concatenate([qg, swap(qg, mask)], axis=0)
    qg, w_key, w_value = lax.optimization_barrier((qg, w_key, w_value))
    far_qg = swap(qg, far_bit)
    qg = [qg, swap(qg, near_bit), far_qg]
    (weights,) = call(weights_kernel, [w_key, w_value], [shape((TEAM, 2 * mine, width), BF16)])
    turned = [shape((2, 2 * mine, slots), BF16)]
    (near_t,) = call(functools.partial(turn_kernel, ((0, None), (1, None))), [keep, core], turned)
    near_t, weights, diagonal = lax.optimization_barrier((near_t, weights, diagonal))
    rows = qg[0].shape[0]
    team_slots = TEAM * slots
    work = 2 * rows * team_slots * mine

    def forward(p, blocks, before=()):
        return call(
            functools.partial(forward_kernel, blocks),
            [count, qg[p]]
            + ([keep, core, near_t] if 0 in blocks else [])
            + ([far, diagonal, far_t] if 2 in blocks else [])
            + list(before),
            [shape((mine, rows), F32), shape((4 * MINE, rows), F32)],
            [pltpu.VMEM((3, slots, rows), F32), pltpu.VMEM((3, slots, rows), BF16)],
            flops=2 * work * len(blocks),
            exps=rows * slots * len(blocks) * MINE,
        )

    early = [forward(p, (0, 1)) for p in range(2)]
    early, far, qg[2] = lax.optimization_barrier((early, far, qg[2]))
    qg.append(swap(qg[2], near_bit))
    diagonal = swap(diagonal, 1)
    (far_t,) = call(functools.partial(turn_kernel, ((0, None), (1, None))), [far, diagonal], turned)
    done = [forward(p, (2, 3), early[p]) for p in range(2)]
    done += [forward(p, (0, 1, 2, 3)) for p in (2, 3)]
    numer = [d[0] for d in done]
    tops = [d[1][:MINE] for d in done]
    stats = [d[1][2 * MINE :] for d in done]

    def merge(*parts):
        lse = [p[..., :MINE, :] for p in parts]
        top = functools.reduce(jnp.maximum, lse)
        scale = [jnp.exp(x - top) for x in lse]
        total = sum(scale)
        delta = sum(s * p[..., MINE:, :] for s, p in zip(scale, parts)) / total
        return jnp.concatenate([top + jnp.log(total), delta], axis=-2)

    stat = jnp.stack(stats)
    for mask, turn in ((near_bit, 1), (far_bit, 2)):
        came = swap(stat, mask)
        stat = merge(stat, jnp.stack([came[q ^ turn] for q in range(4)]))
    final = [stat[q] for q in range(4)]
    if middle:
        final = stat
        for mask in reversed(middle):
            half = final.shape[-1] // 2
            final = merge(final[..., :half], swap(final[..., half:], mask))
        for mask in middle:
            final = jnp.concatenate([final, swap(final, mask)], axis=-1)
        final = [final[q] for q in range(4)]

    def add(array, came):
        return array.astype(F32) + came.astype(F32)

    def scaled(p):
        scale = jnp.exp(tops[p] - final[p][:MINE])
        return (numer[p].reshape(MINE, -1, rows) * scale[:, None, :]).reshape(mine, rows)

    order = (3, 2, 1, 0)

    def backward(chunks, side, kind, sums=(), partial=(), last=False):
        kept = (2, slots, 2 * mine)
        return call(
            functools.partial(
                backward_kernel, len(chunks), order.index(chunks[0]), side, not sums, last
            ),
            [count]
            + [qg[p] for p in chunks]
            + [final[p] for p in chunks]
            + ([far, diagonal, far_t] if side else [keep, core, near_t])
            + list(sums)
            + list(partial),
            [shape((len(chunks), mine, rows), kind), shape(kept, BF16 if last else F32)],
            [pltpu.VMEM(kept if len(chunks) > 1 else (1, 8, LANES), F32)]
            + [pltpu.VMEM((2, slots, rows), F32)] * 2
            + [pltpu.VMEM((2, slots, rows), BF16)] * 2,
            flops=7 * work * len(chunks),
            exps=rows * team_slots // 2 * MINE * len(chunks),
        )

    came_a = swap(jnp.stack([scaled(3), scaled(2)]).astype(BF16), far_bit)
    partial, gkv_far = backward(order, 1, F32, last=True)
    came_a, partial = lax.optimization_barrier((came_a, partial))
    came_far = swap(gkv_far, 2)
    near_a = swap(add(scaled(1), came_a[0]).astype(BF16), near_bit)
    gq, total = backward((3,), 0, BF16, partial=[partial])
    came = swap(gq[0], near_bit)
    gq, total = backward((2,), 0, F32, [total], [partial])
    sent, total = lax.optimization_barrier((add(gq[0], came).astype(BF16), total))
    far_q = swap(sent, far_bit)
    gq, total = backward((1,), 0, BF16, [total], [partial])
    near_q = swap(gq[0], near_bit)
    came_far, far_q, total = lax.optimization_barrier((came_far, far_q, total))
    gq, gkv_near = backward((0,), 0, F32, [total], [partial], True)
    attended = add(add(scaled(0), near_a), came_a[1])
    grad_query = add(add(gq[0], near_q), far_q)

    both = jnp.stack([attended, grad_query])
    for mask in reversed(middle):
        half = both.shape[-1] // 2
        both = add(both[..., :half], swap(both[..., half:].astype(BF16), mask))
    both, came_far = lax.optimization_barrier((both.astype(BF16), came_far))
    far_both = swap(both[..., 2 * own :], 2)
    near_both = both[..., : 2 * own]

    core_gkv = swap(jnp.stack([gkv_near[1], came_far[1]]), 1)
    (d_points,) = call(
        points_kernel,
        [place, gkv_near, came_far, core_gkv, weights],
        [shape((slots, width), BF16)],
        flops=4 * slots * width * width,
    )
    far_both, d_points = lax.optimization_barrier((far_both, d_points))
    core_both = swap(jnp.stack([near_both[..., own:], far_both[..., own:]]), 1)
    result, d_latents = call(
        queries_kernel,
        [place, near_both, far_both, core_both, latents, d_out, w_out, w_query],
        [shape((own, width), BF16)] * 2,
        [pltpu.VMEM((width, own), F32)],
        flops=4 * own * width * width,
    )
    return (result, d_latents, d_points)


def solution(mesh):
    part = P(("groups", "pts"), None)
    in_specs = (part, part, P(("groups", "pts")), P(), P(), P(), P(), part)
    return jax.shard_map(
        functools.partial(body, mesh.shape["pts"]),
        mesh=mesh,
        in_specs=in_specs,
        out_specs=(part, part, part),
        check_vma=False,
    )
```
